32 devices in a mesh: dp: 8 (over y, x, core), seq: 4 (over z).
Axes of the slice: x: 2, y: 2, z: 4, core: 2. Of those that a mesh axis runs over, the one named last changes fastest.
Arguments:
- tokens: bfloat16 [16, 2048, 768], P('dp', 'seq'), may hold values from -6 to 6
- segment_ids: int32 [16, 2048], P('dp', 'seq'), may hold values from 0 to 3, never falling along the last dimension, each value on 1 to 1024 neighbouring positions
- boundary_mask: int32 [16, 4, 256], P('dp'), may hold values from 0 to 1, as said below
- w_qkv: bfloat16 [768, 2304], replicated, may hold values from -0.21875 to 0.21875
- b_qkv: float32 [2304], replicated, may hold values from -3 to 3
- w_out: bfloat16 [768, 768], replicated, may hold values from -1.75 to 1.75
- b_out: float32 [768], replicated, may hold values from -3 to 3
- ln1_gain: float32 [768], replicated, may hold values from 0.1 to 1.9
- ln1_bias: float32 [768], replicated, may hold values from -3 to 3
- w_in: bfloat16 [768, 3072], replicated, may hold values from -0.21875 to 0.21875
- b_in: float32 [3072], replicated, may hold values from -3 to 3
- w_down: bfloat16 [3072, 768], replicated, may hold values from -0.109375 to 0.109375
- b_down: float32 [768], replicated, may hold values from -3 to 3
- ln2_gain: float32 [768], replicated, may hold values from 0.1 to 1.9
- ln2_bias: float32 [768], replicated, may hold values from -3 to 3
- proj_e: bfloat16 [256, 2048], P(None, 'seq'), may hold values from -0.25 to 0.25
- cotangent: bfloat16 [16, 2048, 768], P('dp', 'seq'), may hold values from -6 to 6
Outputs:
- layer_out: bfloat16 [16, 2048, 768], P('dp', 'seq')
- grad_tokens: float32 [16, 2048, 768], P('dp', 'seq')
- grad_w_qkv: float32 [768, 2304], P(('dp', 'seq'))
- grad_b_qkv: float32 [2304], P(('dp', 'seq'))
- grad_w_out: float32 [768, 768], P(('dp', 'seq'))
- grad_b_out: float32 [768], P(('dp', 'seq'))
- grad_ln1_gain: float32 [768], P(('dp', 'seq'))
- grad_ln1_bias: float32 [768], P(('dp', 'seq'))
- grad_w_in: float32 [768, 3072], P(('dp', 'seq'))
- grad_b_in: float32 [3072], P(('dp', 'seq'))
- grad_w_down: float32 [3072, 768], P(('dp', 'seq'))
- grad_b_down: float32 [768], P(('dp', 'seq'))
- grad_ln2_gain: float32 [768], P(('dp', 'seq'))
- grad_ln2_bias: float32 [768], P(('dp', 'seq'))
- grad_proj_e: float32 [256, 2048], P(None, 'seq')
The draws below stay inside these ranges and needn't reach their ends.
Inputs may be any that keep to these rules, and one draw needn't show every extreme that they name: `segment_ids`: each sequence's ids never fall; every one of the 4 segments has 1 to 1024 positions, and one has exactly 1024. `boundary_mask`: for each sequence, each of the 256 slots is owned by exactly one of its 4 segments, and each segment owns at least one slot.
All inputs are finite; a program needn't handle non-finite values.
Results may differ from the reference program's by a relative error of at most 0.02.
Values may be sent and summed in bfloat16 or wider, within the bound.
No kernel may reach another device: no remote copies, remote signals or barrier semaphores. Data moves between devices by JAX's collectives and lax.ppermute only.
A program may use at most 192 MiB of HBM per device.

```python
import math
import jax
import jax.numpy as jnp
import numpy as np
from jax import lax

D = 768
HEADS = 12
HD = 64
FF = 3072
KP = 256
LEN = 2048
NSEG = 4
SEQS = 16
N_SEQ = 4


def draw_boundary_mask(key, part):
    owner_key = jax.random.fold_in(key, 11)
    order_key = jax.random.fold_in(key, 23)
    owners = jax.random.randint(owner_key, (SEQS, KP), 0, NSEG)
    ranks = jax.vmap(lambda k: jax.random.permutation(k, KP))(jax.random.split(order_key, SEQS)).astype(jnp.int32)
    owners = jnp.where(ranks < NSEG, ranks, owners)
    labels = jnp.arange(NSEG, dtype=jnp.int32)
    return (owners[:, None, :] == labels[None, :, None]).astype(jnp.int32)


def steps_of(own_key, dims, cuts, smallest, high):
    level = 1.0
    for axis_at, blocks in cuts:
        draws = jax.random.uniform(jax.random.fold_in(jax.random.fold_in(own_key, 6), axis_at), (blocks,), jnp.float32, smallest / len(cuts), high / len(cuts))
        level = level * jnp.repeat(jnp.exp(draws), dims[axis_at] // blocks).reshape((-1,) + (1,) * (len(dims) - 1 - axis_at))
    return level


def split_up(number_of, total, bound, skew):
    weights = [(1 << 20) // math.isqrt(rank ** skew) + 1 for rank in range(2, number_of + 1)]
    spare, counts = total - bound - (number_of - 1), [1] * (number_of - 1)
    while spare > 0:
        movable = [i for i in range(number_of - 1) if counts[i] < bound]
        whole, remaining = sum([weights[i] for i in movable]), spare
        for i in movable:
            more = min(bound - counts[i], max(1, remaining * weights[i] // whole), spare)
            counts[i] = counts[i] + more
            spare = spare - more
    return np.array([bound] + counts)


def uneven(own_key, number_of, total, reach, slope):
    if number_of == 2:
        one = jax.random.randint(own_key, (), max(1, total - reach), min(reach, total - 1) + 1)
        return jnp.stack([one, total - one])
    lengths = jnp.asarray(split_up(number_of, total, reach, slope), jnp.int32)
    couples = (number_of - 1) // 2
    giver, taker = lengths[1:1 + 2 * couples:2], lengths[2:2 + 2 * couples:2]
    margin = jnp.minimum(giver - 1, reach - taker)
    moved = jax.random.randint(jax.random.fold_in(own_key, 1), (couples,), 0, 1 << 20) % (margin + 1)
    lengths = lengths.at[1:1 + 2 * couples:2].set(giver - moved).at[2:2 + 2 * couples:2].set(taker + moved)
    return lengths[jax.random.permutation(jax.random.fold_in(own_key, 2), number_of)]


def scatter_about(rng, dims, deviation, limit, shards=(), kind=jnp.bfloat16):
    entries = jax.random.normal(rng, dims, jnp.float32) * deviation
    if len(shards) > 0:
        entries = steps_of(rng, dims, shards, -0.22, 0.18) * entries
    return jnp.clip(entries, min=-limit, max=limit).astype(kind)


def setup_inputs(seed: int = 0) -> dict:
    key_list = jax.random.split(jax.random.key(seed), 18)
    tokens = scatter_about(key_list[0], (SEQS, LEN, D), 1.0, 6.0, ((0, 8), (1, 4)))
    segment_ids = jax.vmap(lambda own: jnp.searchsorted(jnp.cumsum(uneven(own, NSEG, LEN, LEN // 2, 1)), jnp.arange(LEN), side="right"))(jax.random.split(key_list[1], SEQS)).reshape((SEQS, LEN)).astype(jnp.int32)
    boundary_mask = draw_boundary_mask(jax.random.fold_in(key_list[17], 71), 0)
    w_qkv = scatter_about(key_list[3], (D, 3 * D), D ** -0.5, 0.21875)
    b_qkv = scatter_about(key_list[4], (3 * D,), 0.5, 3.0, (), jnp.float32)
    w_out = scatter_about(key_list[5], (D, D), (D // 64) ** -0.5, 1.75)
    b_out = scatter_about(key_list[6], (D,), 0.5, 3.0, (), jnp.float32)
    ln1_gain = jnp.clip(1.0 + 0.18 * jax.random.normal(key_list[7], (D,), jnp.float32), 0.1, 1.9)
    ln1_bias = scatter_about(key_list[8], (D,), 0.5, 3.0, (), jnp.float32)
    w_in = scatter_about(key_list[9], (D, FF), D ** -0.5, 0.21875)
    b_in = scatter_about(key_list[10], (FF,), 0.5, 3.0, (), jnp.float32)
    w_down = scatter_about(key_list[11], (FF, D), FF ** -0.5, 0.109375)
    b_down = scatter_about(key_list[12], (D,), 0.5, 3.0, (), jnp.float32)
    ln2_gain = jnp.clip(1.0 + 0.18 * jax.random.normal(key_list[13], (D,), jnp.float32), 0.1, 1.9)
    ln2_bias = scatter_about(key_list[14], (D,), 0.5, 3.0, (), jnp.float32)
    proj_e = scatter_about(key_list[15], (KP, LEN), (LEN // NSEG) ** -0.5, 0.25, ((1, 4),))
    cotangent = scatter_about(key_list[16], (SEQS, LEN, D), 1.0, 6.0, ((0, 8), (1, 4)))
    return {"tokens": tokens, "segment_ids": segment_ids, "boundary_mask": boundary_mask, "w_qkv": w_qkv, "b_qkv": b_qkv, "w_out": w_out, "b_out": b_out, "ln1_gain": ln1_gain, "ln1_bias": ln1_bias, "w_in": w_in, "b_in": b_in, "w_down": w_down, "b_down": b_down, "ln2_gain": ln2_gain, "ln2_bias": ln2_bias, "proj_e": proj_e, "cotangent": cotangent}


@jax.custom_vjp
def low(v):
    return lax.optimization_barrier(v.astype(jnp.bfloat16)).astype(jnp.float32)

@jax.custom_vjp
def low_back(v):
    return v

def low_keep(v):
    return (low(v), None)

def low_pass(kept, grad):
    return (grad,)

def back_keep(v):
    return (v, None)

def back_low(kept, grad):
    return (low(grad),)
low.defvjp(low_keep, low_pass)
low_back.defvjp(back_keep, back_low)

def layer_norm(resid, gain, shift):
    center = resid - lax.optimization_barrier(jnp.mean(resid, -1, keepdims=True))
    inverse = lax.rsqrt(lax.optimization_barrier(jnp.mean(center * center, -1, keepdims=True)) + 1e-05)
    return center * inverse * gain + shift

def sequence_forward(rows, w_qkv, b_qkv, w_out, b_out, ln1_gain, ln1_bias, w_in, b_in, w_down, b_down, ln2_gain, ln2_bias, proj_e, allowed):
    highest = lax.Precision.HIGHEST
    projected = low_back(low(jnp.dot(rows, w_qkv, precision=highest) + b_qkv))
    query = projected[:, :D].reshape(LEN, HEADS, HD)
    keys_values = projected[:, D:]
    weighted = jnp.transpose(proj_e) * allowed
    block_len = LEN // N_SEQ
    partial_sums = jnp.einsum('nlk,nlc->nkc', weighted.reshape(N_SEQ, block_len, KP), keys_values.reshape(N_SEQ, block_len, 2 * D), precision=highest)
    summary = low_back(low(lax.optimization_barrier(jnp.sum(low(partial_sums), 0))))
    key_summary = summary[:, :D].reshape(KP, HEADS, HD)
    value_summary = summary[:, D:].reshape(KP, HEADS, HD)
    scores = low_back(jnp.einsum('lhd,khd->hlk', query, key_summary, precision=highest) * 0.125)
    masked = jnp.where(allowed[None] > 0.5, scores, -1e+30)
    probs = low(jax.nn.softmax(masked, -1))
    attended = low_back(low(jnp.einsum('hlk,khd->lhd', probs, value_summary, precision=highest).reshape(LEN, D)))
    branch = low_back(jnp.dot(attended, w_out, precision=highest) + b_out)
    mid = layer_norm(rows + branch, ln1_gain, ln1_bias)
    hidden = low_back(jnp.dot(low(mid), w_in, precision=highest) + b_in)
    activ = low(jax.nn.gelu(hidden, approximate=False))
    second = low_back(jnp.dot(activ, w_down, precision=highest) + b_down)
    return layer_norm(mid + second, ln2_gain, ln2_bias)

def reference(tokens, segment_ids, boundary_mask, w_qkv, b_qkv, w_out, b_out, ln1_gain, ln1_bias, w_in, b_in, w_down, b_down, ln2_gain, ln2_bias, proj_e, cotangent):
    weights = tuple((w.astype(jnp.float32) for w in (w_qkv, b_qkv, w_out, b_out, ln1_gain, ln1_bias, w_in, b_in, w_down, b_down, ln2_gain, ln2_bias, proj_e)))

    def one_sequence(totals, item):
        rows, segs, masks, upstream = item
        onehot = (segs[:, None] == jnp.arange(NSEG, dtype=jnp.int32)[None, :]).astype(jnp.float32)
        allowed = jnp.dot(onehot, masks.astype(jnp.float32), precision=lax.Precision.HIGHEST)

        def forward(inputs, *params):
            return sequence_forward(inputs, *params, allowed)
        result, pullback = jax.vjp(forward, rows.astype(jnp.float32), *weights)
        grads = pullback(upstream.astype(jnp.float32))
        totals = tuple((t + g for t, g in zip(totals, grads[1:])))
        return (totals, (result.astype(jnp.bfloat16), grads[0]))
    start = tuple((jnp.zeros_like(w) for w in weights))
    totals, (outputs, input_grads) = lax.scan(one_sequence, start, (tokens, segment_ids, boundary_mask, cotangent))
    return (outputs, input_grads, totals[0], totals[1], totals[2], totals[3], totals[4], totals[5], totals[6], totals[7], totals[8], totals[9], totals[10], totals[11], totals[12])
```

```python
import functools

import jax
import jax.numpy as jnp
from jax import lax
from jax.experimental import pallas as pl
from jax.experimental.pallas import tpu as pltpu
from jax.sharding import PartitionSpec as P

HEADS = 12
HD = 64
KP = 256
NSEG = 4
SEG_MAX = 1024
TE = 272
EPS = 1e-05
SCALE = 0.125
HALF_ROOT = 0.7071067811865476
INV_ROOT_TAU = 0.3989422804014327
F32 = jnp.float32
BF16 = jnp.bfloat16
VMEM_LIMIT = 60 * 1024 * 1024


def dot(left, right, cl=1, cr=0):
    return lax.dot_general(left, right, (((cl,), (cr,)), ((), ())), preferred_element_type=F32)


def call(kernel, out_shape, **kw):
    kw.setdefault("compiler_params", pltpu.CompilerParams(vmem_limit_bytes=VMEM_LIMIT))
    return pl.pallas_call(kernel, out_shape=out_shape, **kw)


def sds(shape, dtype=BF16):
    return jax.ShapeDtypeStruct(shape, dtype)


def cost(flops, nbytes, trans=0):
    return pl.CostEstimate(flops=int(flops), bytes_accessed=int(nbytes), transcendentals=int(trans))


def full(shape):
    return pl.BlockSpec(shape, lambda *_: (0,) * len(shape))


def prep_kernel(s, tok_ref, seg_ref, mask_ref, proj_ref, t_ref, al_ref, wt_ref):
    width = tok_ref.shape[-1]
    length = tok_ref.shape[1]
    m = mask_ref[0]
    owner = jnp.sum(m * lax.broadcasted_iota(jnp.int32, m.shape, 0), 0, keepdims=True).astype(F32)
    owner_col = jnp.transpose(jnp.broadcast_to(owner, (8, KP)))[:, 0:1]
    seg = seg_ref[s : s + 1, :].astype(F32)
    allowed = owner_col == seg
    weighted = jnp.where(allowed, proj_ref[...].astype(F32), 0.0).astype(BF16)
    al_ref[...] = jnp.where(allowed, 1.0, 0.0).astype(BF16)
    wt_ref[...] = weighted
    t_ref[0:KP, :] = dot(weighted, tok_ref[0]).astype(BF16)
    count = dot(jnp.ones((TE - KP, length), BF16), weighted, 1, 1).astype(BF16)
    t_ref[KP:TE, :] = jnp.concatenate([count, jnp.zeros((TE - KP, width - KP), BF16)], 1)


def prep(s, tokens, segment_ids, mask, proj_e):
    seqs, length, width = tokens.shape
    return call(
        functools.partial(prep_kernel, s),
        (sds((TE, width)), sds((KP, length)), sds((KP, length))),
        grid=(1,),
        in_specs=[
            pl.BlockSpec((1, length, width), lambda i: (s, 0, 0)),
            full((seqs, length)),
            pl.BlockSpec((1, NSEG, KP), lambda i: (s, 0, 0)),
            full((KP, length)),
        ],
        out_specs=(full((TE, width)), full((KP, length)), full((KP, length))),
        cost_estimate=cost(2 * KP * length * width, 2 * length * width),
        name="prep",
    )(tokens, segment_ids, mask, proj_e)


def query_kernel(me_ref, tok_ref, wq_ref, bq_ref, q_ref, tt_ref):
    units, rows = tt_ref.shape[1], tt_ref.shape[2]
    tok = tok_ref[0]
    q = (dot(tok, wq_ref[...]) + bq_ref[...]).astype(BF16).astype(F32) * SCALE
    q_ref[0] = jnp.transpose(q.astype(BF16))
    tt = jnp.transpose(tok)
    for u in range(units):
        tt_ref[0, u ^ me_ref[0]] = tt[u * rows : (u + 1) * rows]


def query(me, units, tokens, w_qkv, b_qkv):
    seqs, length, width = tokens.shape
    rows = width // units
    return call(
        query_kernel,
        (sds((seqs, width, length)), sds((seqs, units, rows, length))),
        grid_spec=pltpu.PrefetchScalarGridSpec(
            num_scalar_prefetch=1,
            grid=(seqs,),
            in_specs=[
                pl.BlockSpec((1, length, width), lambda s, me: (s, 0, 0)),
                pl.BlockSpec((width, width), lambda s, me: (0, 0)),
                pl.BlockSpec((1, width), lambda s, me: (0, 0)),
            ],
            out_specs=(
                pl.BlockSpec((1, width, length), lambda s, me: (s, 0, 0)),
                pl.BlockSpec((1, units, rows, length), lambda s, me: (s, 0, 0, 0)),
            ),
        ),
        cost_estimate=cost(2 * seqs * width * length * width, 6 * seqs * length * width),
        name="query",
    )(me, tokens, w_qkv, b_qkv)


def flip_kernel(w_ref, o_ref):
    o_ref[...] = jnp.transpose(w_ref[...])


def flip_kv(w_qkv):
    width = w_qkv.shape[0]
    return call(
        flip_kernel,
        sds((2 * width, width)),
        grid=(2,),
        in_specs=[pl.BlockSpec((width, width), lambda i: (0, 1 + i))],
        out_specs=pl.BlockSpec((width, width), lambda i: (i, 0)),
        cost_estimate=cost(0, 8 * width * width),
        name="flip_kv",
    )(w_qkv)


def norm_stats(resid):
    center = resid - jnp.mean(resid, -1, keepdims=True)
    inverse = lax.rsqrt(jnp.mean(center * center, -1, keepdims=True) + EPS)
    return center * inverse, inverse


def attend_kernel(nt, me_ref, *refs):
    t_refs = refs[:nt]
    wkv_ref, bkv_ref, q_ref, al_ref, tok_ref, wo_ref, bo_ref = refs[nt : nt + 7]
    tt_ref, c_ref, kv_ref, p_ref, att_ref, n_ref, inv_ref, att_scr = refs[nt + 7 :]
    width = wo_ref.shape[0]
    units, rows = tt_ref.shape[0], tt_ref.shape[1]
    total = t_refs[0][...].astype(F32)
    for r in t_refs[1:]:
        total = total + r[...].astype(F32)
    low = total.astype(BF16)
    t_low = low[0:KP]
    c_row = low[KP : KP + 8, 0:KP]
    c_ref[...] = c_row
    tt = jnp.transpose(t_low)
    me = me_ref[0]
    for u in range(units):
        tt_ref[u ^ me] = tt[u * rows : (u + 1) * rows]
    kv_ref[...] = (dot(wkv_ref[...], t_low, 1, 1) + bkv_ref[...] * c_row[0:1].astype(F32)).astype(BF16)
    allowed = al_ref[...] > 0.5

    def head(h, carry):
        rows_h = pl.ds(pl.multiple_of(h * HD, HD), HD)
        rows_v = pl.ds(pl.multiple_of(width + h * HD, HD), HD)
        scores = dot(kv_ref[rows_h, :], q_ref[0, rows_h, :], 0, 0)
        scores = jnp.where(allowed, scores, -1e30)
        expo = jnp.exp(scores - jnp.max(scores, 0, keepdims=True))
        probs = (expo * (1.0 / jnp.sum(expo, 0, keepdims=True))).astype(BF16)
        p_ref[h] = probs
        att_scr[rows_h, :] = dot(kv_ref[rows_v, :], probs).astype(BF16)
        return carry

    lax.fori_loop(0, width // HD, head, 0, unroll=2)
    att = att_scr[...]
    for u in range(units):
        att_ref[u ^ me] = att[u * rows : (u + 1) * rows]
    resid = tok_ref[0].astype(F32) + dot(att, wo_ref[...], 0, 0) + bo_ref[...]
    normed, inverse = norm_stats(resid)
    n_ref[...] = normed
    inv_ref[...] = inverse


def attend(me, s, units, tparts, wkv_t, bkv_col, q_t, allow, tokens, w_out, b_out):
    seqs, length, width = tokens.shape
    rows = width // units
    nt = len(tparts)
    m = lambda nd: (lambda i, me: (0,) * nd)
    return call(
        functools.partial(attend_kernel, nt),
        (
            sds((units, rows, KP)),
            sds((8, KP)),
            sds((2 * width, KP)),
            sds((width // HD, KP, length)),
            sds((units, rows, length)),
            sds((length, width), F32),
            sds((length, 1), F32),
        ),
        grid_spec=pltpu.PrefetchScalarGridSpec(
            num_scalar_prefetch=1,
            grid=(1,),
            in_specs=[pl.BlockSpec((TE, width), m(2))] * nt
            + [
                pl.BlockSpec((2 * width, width), m(2)),
                pl.BlockSpec((2 * width, 1), m(2)),
                pl.BlockSpec((1, width, length), lambda i, me: (s, 0, 0)),
                pl.BlockSpec((KP, length), m(2)),
                pl.BlockSpec((1, length, width), lambda i, me: (s, 0, 0)),
                pl.BlockSpec((width, width), m(2)),
                pl.BlockSpec((1, width), m(2)),
            ],
            out_specs=(
                pl.BlockSpec((units, rows, KP), m(3)),
                pl.BlockSpec((8, KP), m(2)),
                pl.BlockSpec((2 * width, KP), m(2)),
                pl.BlockSpec((width // HD, KP, length), m(3)),
                pl.BlockSpec((units, rows, length), m(3)),
                pl.BlockSpec((length, width), m(2)),
                pl.BlockSpec((length, 1), m(2)),
            ),
            scratch_shapes=[pltpu.VMEM((width, length), BF16)],
        ),
        cost_estimate=cost(2 * KP * width * 2 * width + 8 * KP * length * width + 2 * length * width * width, 16 * 2**20),
        name="attend",
    )(me, *tparts, wkv_t, bkv_col, q_t, allow, tokens, w_out, b_out)


def norm_back(upstream, normed, inverse, gain):
    scaled = upstream * gain
    return inverse * (
        scaled
        - jnp.mean(scaled, -1, keepdims=True)
        - normed * jnp.mean(scaled * normed, -1, keepdims=True)
    )


def feed_kernel(
    chunks, me_ref, n_ref, inv_ref, g1_ref, be1_ref, win_ref, bin_ref, wdn_ref, bdn_ref, g2_ref, be2_ref, cot_ref,
    mt_ref, at_ref, gb_ref, dh_ref, out_ref, gf_ref, gfl_ref, stat_ref, gbin_ref,
    low_scr, acc_scr, slope_scr, gb_scr,
):
    step = pl.program_id(0)
    me = me_ref[0]
    units, rows = mt_ref.shape[0], mt_ref.shape[1]
    per, arows = at_ref.shape[0], at_ref.shape[1]

    @pl.when(step == 0)
    def _():
        mid = n_ref[...] * g1_ref[...] + be1_ref[...]
        low = mid.astype(BF16)
        low_scr[...] = low
        acc_scr[...] = mid + bdn_ref[...]
        mt = jnp.transpose(low)
        for u in range(units):
            mt_ref[u ^ me] = mt[u * rows : (u + 1) * rows]

    @pl.when(step < chunks)
    def _():
        hidden = dot(low_scr[...], win_ref[...]) + bin_ref[...]
        phi = 0.5 * (1.0 + lax.erf(hidden * HALF_ROOT))
        activ = (hidden * phi).astype(BF16)
        slope_scr[step] = (phi + hidden * INV_ROOT_TAU * jnp.exp(-0.5 * hidden * hidden)).astype(BF16)
        acc_scr[...] += dot(activ, wdn_ref[...])
        at = jnp.transpose(activ)
        for i in range(per):
            at_ref[i ^ (me & (per - 1))] = at[i * arows : (i + 1) * arows]

    @pl.when(step == chunks - 1)
    def _():
        normed, inverse = norm_stats(acc_scr[...])
        out_ref[...] = (normed * g2_ref[...] + be2_ref[...]).astype(BF16)
        cot = cot_ref[0].astype(F32)
        stat_ref[0:1, :] = jnp.sum(cot * normed, 0, keepdims=True)
        stat_ref[1:2, :] = jnp.sum(cot, 0, keepdims=True)
        second = norm_back(cot, normed, inverse, g2_ref[...])
        low = second.astype(BF16)
        stat_ref[2:3, :] = jnp.sum(low.astype(F32), 0, keepdims=True)
        gb_ref[...] = low
        gb_scr[...] = low
        acc_scr[...] = second

    @pl.when(step >= chunks)
    def _():
        grad = dot(gb_scr[...], wdn_ref[...], 1, 1)
        dh = (grad * slope_scr[step - chunks].astype(F32)).astype(BF16)
        dh_ref[...] = dh
        gbin_ref[...] = jnp.sum(dh.astype(F32), 0, keepdims=True)
        acc_scr[...] += dot(dh, win_ref[...], 1, 1)

    @pl.when(step == 2 * chunks - 1)
    def _():
        up = acc_scr[...]
        normed = n_ref[...]
        stat_ref[3:4, :] = jnp.sum(up * normed, 0, keepdims=True)
        stat_ref[4:5, :] = jnp.sum(up, 0, keepdims=True)
        first = norm_back(up, normed, inv_ref[...], g1_ref[...])
        low = first.astype(BF16)
        gf_ref[...] = first
        gfl_ref[...] = low
        stat_ref[5:6, :] = jnp.sum(low.astype(F32), 0, keepdims=True)
        stat_ref[6:8, :] = jnp.zeros((2, stat_ref.shape[1]), F32)


def feed(me, s, units, normed, inverse, g1, be1, w_in, b_in, w_down, b_down, g2, be2, cot):
    length, width = normed.shape
    ff = w_in.shape[1]
    rows = width // units
    arows = ff // units
    chunk = 768
    chunks = ff // chunk
    per = chunk // arows
    fwd = lambda i: jnp.where(i < chunks, i, i - chunks)
    m = lambda nd: (lambda i, me: (0,) * nd)
    return call(
        functools.partial(feed_kernel, chunks),
        (
            sds((units, rows, length)),
            sds((units, arows, length)),
            sds((length, width)),
            sds((length, ff)),
            sds((length, width)),
            sds((length, width), F32),
            sds((length, width)),
            sds((8, width), F32),
            sds((1, ff), F32),
        ),
        grid_spec=pltpu.PrefetchScalarGridSpec(
            num_scalar_prefetch=1,
            grid=(2 * chunks,),
            in_specs=[
                pl.BlockSpec((length, width), m(2)),
                pl.BlockSpec((length, 1), m(2)),
                pl.BlockSpec((1, width), m(2)),
                pl.BlockSpec((1, width), m(2)),
                pl.BlockSpec((width, chunk), lambda i, me: (0, fwd(i))),
                pl.BlockSpec((1, chunk), lambda i, me: (0, fwd(i))),
                pl.BlockSpec((chunk, width), lambda i, me: (fwd(i), 0)),
                pl.BlockSpec((1, width), m(2)),
                pl.BlockSpec((1, width), m(2)),
                pl.BlockSpec((1, width), m(2)),
                pl.BlockSpec((1, length, width), lambda i, me: (s, 0, 0)),
            ],
            out_specs=(
                pl.BlockSpec((units, rows, length), m(3)),
                pl.BlockSpec((per, arows, length), lambda i, me: (jnp.minimum(i, chunks - 1) ^ (me[0] // per), 0, 0)),
                pl.BlockSpec((length, width), m(2)),
                pl.BlockSpec((length, chunk), lambda i, me: (0, jnp.maximum(i - chunks, 0))),
                pl.BlockSpec((length, width), m(2)),
                pl.BlockSpec((length, width), m(2)),
                pl.BlockSpec((length, width), m(2)),
                pl.BlockSpec((8, width), m(2)),
                pl.BlockSpec((1, chunk), lambda i, me: (0, jnp.maximum(i - chunks, 0))),
            ),
            scratch_shapes=[
                pltpu.VMEM((length, width), BF16),
                pltpu.VMEM((length, width), F32),
                pltpu.VMEM((chunks, length, chunk), BF16),
                pltpu.VMEM((length, width), BF16),
            ],
        ),
        cost_estimate=cost(8 * length * width * ff, 24 * 2**20, 2 * length * ff),
        name="feed",
    )(me, normed, inverse, g1, be1, w_in, b_in, w_down, b_down, g2, be2, cot)


def attend_back_kernel(gfl_ref, wo_ref, kv_ref, p_ref, q_ref, c_ref, wkv_ref, bkv_ref, dq_ref, gs_ref, gt_ref, st_ref, da_scr):
    width = wo_ref.shape[0]
    length = gfl_ref.shape[0]
    da_scr[...] = dot(wo_ref[...], gfl_ref[...], 1, 1).astype(BF16)

    def head(h, carry):
        rows_h = pl.ds(pl.multiple_of(h * HD, HD), HD)
        rows_v = pl.ds(pl.multiple_of(width + h * HD, HD), HD)
        probs = p_ref[h]
        wide = probs.astype(F32)
        da = da_scr[rows_h, :]
        grad = dot(kv_ref[rows_v, :], da, 0, 0)
        gs_ref[rows_v, :] = dot(da, probs, 1, 1).astype(BF16)
        ds = (wide * (grad - jnp.sum(wide * grad, 0, keepdims=True))).astype(BF16)
        dq_ref[rows_h, :] = (dot(kv_ref[rows_h, :], ds) * SCALE).astype(BF16)
        gs_ref[rows_h, :] = dot(q_ref[0, rows_h, :], ds, 1, 1).astype(BF16)
        return carry

    lax.fori_loop(0, width // HD, head, 0, unroll=2)
    gs = gs_ref[...]
    gt_ref[0:KP, :] = dot(gs, wkv_ref[...], 0, 0).astype(BF16)
    b_hi = bkv_ref[...].astype(BF16)
    b_lo = (bkv_ref[...] - b_hi.astype(F32)).astype(BF16)
    pad = TE - KP
    drow = dot(jnp.broadcast_to(b_hi, (pad, 2 * width)), gs) + dot(jnp.broadcast_to(b_lo, (pad, 2 * width)), gs)
    gt_ref[KP:TE, :] = jnp.concatenate([drow.astype(BF16), jnp.zeros((pad, width - KP), BF16)], 1)
    st_ref[:, 0:width] = dot(jnp.ones((8, length), BF16), dq_ref[...], 1, 1)
    st_ref[:, width:] = dot(c_ref[...], gs, 1, 1)


def attend_back(s, gfl, w_out, kv_t, probs, q_t, c_row, wkv_t, bkv_row):
    length, width = gfl.shape
    m = lambda nd: (lambda i: (0,) * nd)
    return call(
        attend_back_kernel,
        (sds((width, length)), sds((2 * width, KP)), sds((TE, width)), sds((8, 3 * width), F32)),
        grid=(1,),
        in_specs=[
            pl.BlockSpec((length, width), m(2)),
            pl.BlockSpec((width, width), m(2)),
            pl.BlockSpec((2 * width, KP), m(2)),
            pl.BlockSpec((width // HD, KP, length), m(3)),
            pl.BlockSpec((1, width, length), lambda i: (s, 0, 0)),
            pl.BlockSpec((8, KP), m(2)),
            pl.BlockSpec((2 * width, width), m(2)),
            pl.BlockSpec((1, 2 * width), m(2)),
        ],
        out_specs=(
            pl.BlockSpec((width, length), m(2)),
            pl.BlockSpec((2 * width, KP), m(2)),
            pl.BlockSpec((TE, width), m(2)),
            pl.BlockSpec((8, 3 * width), m(2)),
        ),
        scratch_shapes=[pltpu.VMEM((width, length), BF16)],
        cost_estimate=cost(2 * KP * width * 2 * width + 16 * KP * length * width + 2 * length * width * width, 12 * 2**20),
        name="attend_back",
    )(gfl, w_out, kv_t, probs, q_t, c_row, wkv_t, bkv_row)


def token_kernel(gf_ref, dq_ref, wq_ref, o_ref):
    o_ref[...] = gf_ref[...] + dot(dq_ref[...], wq_ref[...], 0, 1)


def token_grad(gf, dq_t, w_qkv):
    length, width = gf.shape
    return call(
        token_kernel,
        sds((length, width), F32),
        grid=(1,),
        in_specs=[full((length, width)), full((width, length)), pl.BlockSpec((width, width), lambda i: (0, 0))],
        out_specs=full((length, width)),
        cost_estimate=cost(2 * length * width * width, 8 * 2**20),
        name="token_grad",
    )(gf, dq_t, w_qkv)


def last_kernel(seqs, nt, *refs):
    t_refs = [refs[s * nt : (s + 1) * nt] for s in range(seqs)]
    base = seqs * nt
    part_refs = refs[base : base + seqs]
    wt_refs = refs[base + seqs : base + 2 * seqs]
    al_refs = refs[base + 2 * seqs : base + 3 * seqs]
    tok_ref = refs[base + 3 * seqs]
    o_ref, gp_ref = refs[base + 3 * seqs + 1 :]
    proj = None
    for s in range(seqs):
        total = t_refs[s][0][...].astype(F32)
        for r in t_refs[s][1:]:
            total = total + r[...].astype(F32)
        low = total[0:KP].astype(BF16)
        d_col = jnp.transpose(total[KP : KP + 8, 0:KP])[:, 0:1]
        o_ref[s] = part_refs[s][...] + dot(wt_refs[s][...], low, 0, 0)
        term = (dot(low, tok_ref[s], 1, 1) + d_col) * al_refs[s][...].astype(F32)
        proj = term if proj is None else proj + term
    gp_ref[...] = proj.astype(BF16)


def last(tparts, parts, weights, allows, tokens):
    seqs, length, width = tokens.shape
    nt = len(tparts[0])
    flat = [t for ts in tparts for t in ts]
    return call(
        functools.partial(last_kernel, seqs, nt),
        (sds((seqs, length, width), F32), sds((KP, length))),
        grid=(1,),
        in_specs=[full((TE, width))] * (seqs * nt)
        + [full((length, width))] * seqs
        + [full((KP, length))] * (2 * seqs)
        + [full((seqs, length, width))],
        out_specs=(full((seqs, length, width)), full((KP, length))),
        cost_estimate=cost(4 * seqs * length * width * KP, 12 * 2**20),
        name="last",
    )(*flat, *parts, *weights, *allows, tokens)


def down_kernel(seqs, half, order, with_recv, *refs):
    at_refs = refs[:seqs]
    gb_refs = refs[seqs : 2 * seqs]
    rest = refs[2 * seqs :]
    res = None
    for s in range(seqs):
        term = dot(at_refs[s][0, 0], gb_refs[s][...])
        res = term if res is None else res + term
    if with_recv:
        recv_ref, send_ref, keep_ref = rest
        low = (res + recv_ref[0].astype(F32)).astype(BF16)

        @pl.when(pl.program_id(0) < half)
        def _():
            send_ref[0] = low

        @pl.when(pl.program_id(0) >= half)
        def _():
            keep_ref[0] = low

    else:
        (out_ref,) = rest
        out_ref[0] = res.astype(BF16)


def down_grad(at, gb, core, recv=None, send_bit=None):
    seqs = len(at)
    units, arows, length = at[0].shape
    width = gb[0].shape[1]
    n = units // 2
    half = n // 2
    if send_bit is None:
        pick = lambda i: i
    elif send_bit == 0:
        pick = lambda i: jnp.where(i < half, 2 * i + 1, 2 * (i - half))
    else:
        pick = lambda i: (i + half) % n
    at4 = [a.reshape(n, 2, arows, length) for a in at]
    in_specs = [pl.BlockSpec((1, 1, arows, length), lambda i: (pick(i), core, 0, 0))] * seqs + [full((length, width))] * seqs
    args = [*at4, *gb]
    if recv is None:
        out_shape = sds((n, arows, width))
        out_specs = pl.BlockSpec((1, arows, width), lambda i: (i, 0, 0))
    else:
        in_specs.append(pl.BlockSpec((1, arows, width), lambda i: (pick(i), 0, 0)))
        args.append(recv)
        out_shape = (sds((half, arows, width)), sds((half, arows, width)))
        out_specs = (
            pl.BlockSpec((1, arows, width), lambda i: (jnp.minimum(i, half - 1), 0, 0)),
            pl.BlockSpec((1, arows, width), lambda i: (jnp.maximum(i - half, 0), 0, 0)),
        )
    return call(
        functools.partial(down_kernel, seqs, half, None, recv is not None),
        out_shape,
        grid=(n,),
        in_specs=in_specs,
        out_specs=out_specs,
        cost_estimate=cost(2 * seqs * n * arows * length * width, 10 * 2**20),
        name="down_grad",
    )(*args)


def split_store(low, send_ref, keep_ref, send_bit, where):
    n = low.shape[0]
    if send_bit == 0:
        for i in range(n):
            (send_ref if i & 1 else keep_ref)[i // 2, :, where] = low[i]
    else:
        half = n // 2
        keep_ref[:, :, where] = low[:half]
        send_ref[:, :, where] = low[half:]


def in_kernel(seqs, send_bit, *refs):
    mt_refs = refs[:seqs]
    dh_refs = refs[seqs : 2 * seqs]
    rest = refs[2 * seqs :]
    n, _, rows, length = mt_refs[0].shape
    res = None
    for s in range(seqs):
        term = dot(mt_refs[s][...].reshape(n * rows, length), dh_refs[s][...])
        res = term if res is None else res + term
    res = res.reshape(n, rows, res.shape[-1])
    if send_bit is None:
        rest[0][...] = res.astype(BF16)
    else:
        recv_ref, send_ref, keep_ref = rest
        low = (res + recv_ref[...].astype(F32)).astype(BF16)
        split_store(low, send_ref, keep_ref, send_bit, slice(None))


def in_grad(mt, dh, core, recv=None, send_bit=None):
    seqs = len(mt)
    units, rows, length = mt[0].shape
    ff = dh[0].shape[1]
    n = units // 2
    chunk = 768
    mt4 = [a.reshape(n, 2, rows, length) for a in mt]
    in_specs = [pl.BlockSpec((n, 1, rows, length), lambda i: (0, core, 0, 0))] * seqs + [
        pl.BlockSpec((length, chunk), lambda i: (0, i))
    ] * seqs
    args = [*mt4, *dh]
    if recv is None:
        out_shape = sds((n, rows, ff))
        out_specs = pl.BlockSpec((n, rows, chunk), lambda i: (0, 0, i))
    else:
        in_specs.append(pl.BlockSpec((n, rows, chunk), lambda i: (0, 0, i)))
        args.append(recv)
        out_shape = (sds((n // 2, rows, ff)), sds((n // 2, rows, ff)))
        out_specs = (pl.BlockSpec((n // 2, rows, chunk), lambda i: (0, 0, i)),) * 2
    return call(
        functools.partial(in_kernel, seqs, send_bit),
        out_shape,
        grid=(ff // chunk,),
        in_specs=in_specs,
        out_specs=out_specs,
        cost_estimate=cost(2 * seqs * n * rows * length * ff, 10 * 2**20),
        name="in_grad",
    )(*args)


def rest_kernel(seqs, core, send_bit, me_ref, *refs):
    at_refs, gf_refs, tk_refs, dq_refs, tt_refs, gs_refs = [refs[k * seqs : (k + 1) * seqs] for k in range(6)]
    st_ref = refs[6 * seqs]
    rest = refs[6 * seqs + 1 :]
    n, _, rows, _ = at_refs[0].shape
    width = gf_refs[0].shape[1]

    def put(res, where):
        res = res.reshape(n, rows, res.shape[-1])
        if send_bit is None:
            rest[0][:, :, where] = res.astype(BF16)
        else:
            recv_ref, send_ref, keep_ref = rest
            low = (res + recv_ref[:, :, where].astype(F32)).astype(BF16)
            split_store(low, send_ref, keep_ref, send_bit, where)

    def flat(ref):
        return ref[...].reshape(n * rows, ref.shape[-1])

    def total(terms):
        out = terms[0]
        for t in terms[1:]:
            out = out + t
        return out

    put(total([dot(flat(a), g[...]) for a, g in zip(at_refs, gf_refs)]), slice(0, width))
    put(total([dot(flat(a), g[...], 1, 1) for a, g in zip(tk_refs, dq_refs)]), slice(width, 2 * width))
    put(total([dot(flat(a), g[...], 1, 1) for a, g in zip(tt_refs, gs_refs)]), slice(2 * width, 4 * width))
    stats = jnp.stack([st_ref[(2 * i + core) ^ me_ref[0]] for i in range(n)])
    put(stats.astype(F32).reshape(n * rows, 128), slice(4 * width, 4 * width + 128))


def rest_grad(me, att, gfl, tok_t, dq_t, t_t, gs_t, stats, core, recv=None, send_bit=None):
    seqs = len(att)
    units, rows, length = att[0].shape
    width = gfl[0].shape[1]
    n = units // 2
    cols = 4 * width + 128
    m = lambda nd: (lambda i, me: (0,) * nd)
    half = lambda last: pl.BlockSpec((n, 1, rows, last), lambda i, me: (0, core, 0, 0))
    cut = lambda a: a.reshape(n, 2, rows, a.shape[-1])
    in_specs = (
        [half(length)] * seqs
        + [pl.BlockSpec((length, width), m(2))] * seqs
        + [half(length)] * seqs
        + [pl.BlockSpec((width, length), m(2))] * seqs
        + [half(KP)] * seqs
        + [pl.BlockSpec((2 * width, KP), m(2))] * seqs
        + [pl.BlockSpec((units, rows, 128), m(3))]
    )
    args = [*map(cut, att), *gfl, *map(cut, tok_t), *dq_t, *map(cut, t_t), *gs_t, stats]
    if recv is None:
        out_shape = sds((n, rows, cols))
        out_specs = pl.BlockSpec((n, rows, cols), m(3))
    else:
        in_specs.append(pl.BlockSpec((n, rows, cols), m(3)))
        args.append(recv)
        out_shape = (sds((n // 2, rows, cols)),) * 2
        out_specs = (pl.BlockSpec((n // 2, rows, cols), m(3)),) * 2
    return call(
        functools.partial(rest_kernel, seqs, core, send_bit),
        out_shape,
        grid_spec=pltpu.PrefetchScalarGridSpec(num_scalar_prefetch=1, grid=(1,), in_specs=in_specs, out_specs=out_specs),
        cost_estimate=cost(seqs * n * rows * (4 * length * width + 4 * KP * width), 12 * 2**20),
        name="rest_grad",
    )(me, *args)


def add(a, b):
    return (a.astype(F32) + b.astype(F32)).astype(BF16)


def body(n_dp, n_seq, tokens, segment_ids, mask, w_qkv, b_qkv, w_out, b_out, ln1_gain, ln1_bias, w_in, b_in, w_down, b_down, ln2_gain, ln2_bias, proj_e, cotangent):
    seqs, length, width = tokens.shape
    ff = w_in.shape[1]
    n_all = n_dp * n_seq
    fast = n_dp == 8 and n_seq == 4 and length % 128 == 0
    units = 8
    dp = lax.axis_index("dp").astype(jnp.int32)
    sq = lax.axis_index("seq").astype(jnp.int32)
    me = (dp if fast else jnp.zeros((), jnp.int32)).reshape(1)
    row = lambda v: v.reshape(1, -1)

    def swap(x, bit):
        pairs = [(i, i ^ bit) for i in range(n_all)]
        return lax.ppermute(x, ("dp", "seq"), pairs)

    def along(own):
        if not fast:
            return [lax.psum(own, "seq")]
        right = [(i, i + 1) for i in range(n_seq - 1)]
        left = [(i + 1, i) for i in range(n_seq - 1)]
        out, up, down = [own], own, own
        for _ in range(min(n_seq - 1, -(-(SEG_MAX - 1) // length))):
            up = lax.ppermute(up, "seq", right)
            down = lax.ppermute(down, "seq", left)
            out += [up, down]
        return out

    prepped = [prep(s, tokens, segment_ids, mask, proj_e) for s in range(seqs)]
    tparts = [along(p[0]) for p in prepped]
    q_t, tok_t = query(me, units, tokens, w_qkv, row(b_qkv))
    wkv_t = flip_kv(w_qkv)
    bkv = b_qkv[width:]

    tt, crow, kv, probs, att, normed, inverse = [], [], [], [], [], [], []
    mt, at, gb, dh, outs, gf, gfl, stat, gbin = [], [], [], [], [], [], [], [], []
    for s in range(seqs):
        res = attend(me, s, units, tparts[s], wkv_t, bkv.reshape(-1, 1), q_t, prepped[s][1], tokens, w_out, row(b_out))
        for store, value in zip((tt, crow, kv, probs, att, normed, inverse), res):
            store.append(value)
        res = feed(me, s, units, normed[s], inverse[s], row(ln1_gain), row(ln1_bias), w_in, row(b_in), w_down, row(b_down), row(ln2_gain), row(ln2_bias), cotangent)
        for store, value in zip((mt, at, gb, dh, outs, gf, gfl, stat, gbin), res):
            store.append(value)

    X_BIT, Y_BIT, CORE = 2 * n_seq, 4 * n_seq, n_seq

    def finish(recv, keep, bit, rows_u):
        send = add(keep[1], recv[1])
        keep = add(keep[0], recv[0])
        recv = swap(send, bit)
        cols = keep.shape[-1]
        shape = (2, 2, rows_u // 4, cols)
        z0, z1 = sq & 1, sq >> 1
        pick = lambda a, z: lax.dynamic_index_in_dim(a, z, 1, keepdims=False)
        keep, recv = keep.reshape(shape), recv.reshape(shape)
        send = add(pick(keep, 1 - z0), pick(recv, 1 - z0))
        keep = add(pick(keep, z0), pick(recv, z0))
        recv = swap(send, 1)
        pick = lambda a, z: lax.dynamic_index_in_dim(a, z, 0, keepdims=False)
        send = add(pick(keep, 1 - z1), pick(recv, 1 - z1))
        keep = add(pick(keep, z1), pick(recv, z1))
        recv = swap(send, 2)
        return keep.astype(F32) + recv.astype(F32)

    if fast:
        send1 = down_grad(at, gb, 1)
        recv1 = swap(send1, CORE)
        send2 = in_grad(mt, dh, 1)
        recv2 = swap(send2, CORE)
        sx1, kx1 = down_grad(at, gb, 0, recv1, 0)
        rx1 = swap(sx1, X_BIT)
        sx2, kx2 = in_grad(mt, dh, 0, recv2, 1)
        rx2 = swap(sx2, Y_BIT)

    back = [attend_back(s, gfl[s], w_out, kv[s], probs[s], q_t, crow[s], wkv_t, row(bkv)) for s in range(seqs)]
    gparts = [along(b[2]) for b in back]
    dq_t = [b[0] for b in back]
    gs_t = [b[1] for b in back]

    st = functools.reduce(jnp.add, stat)
    st_in = functools.reduce(jnp.add, gbin)[0]
    st_qkv = functools.reduce(jnp.add, [b[3][0] for b in back])
    tok_u = [tok_t[s] for s in range(seqs)]
    if fast:
        vectors = [st_qkv, st[5], st[3], st[4], st_in, st[2], st[0], st[1]]
        flat = jnp.concatenate([v.reshape(n_all, -1) for v in vectors], 1)
        used = flat.shape[1]
        flat = jnp.pad(flat, ((0, 0), (0, 384 - used))).reshape(n_all, 3, 128)
        rows_u = width // n_dp
        flat = jnp.pad(flat, ((0, 0), (0, width // n_all - 3), (0, 0))).reshape(units, rows_u, 128).astype(BF16)
        send3 = rest_grad(me, att, gfl, tok_u, dq_t, tt, gs_t, flat, 1)
        recv3 = swap(send3, CORE)
        sx3, kx3 = rest_grad(me, att, gfl, tok_u, dq_t, tt, gs_t, flat, 0, recv3, 0)
        rx3 = swap(sx3, X_BIT)

    parts = [token_grad(gf[s], dq_t[s], w_qkv) for s in range(seqs)]
    grad_tokens, gproj = last(gparts, parts, [p[2] for p in prepped], [p[1] for p in prepped], tokens)
    layer_out = jnp.stack(outs)

    if not fast:
        join = lambda v: v.reshape(-1, v.shape[-1])
        pair = lambda a: functools.reduce(jnp.add, [dot(join(l), r) for l, r in a])
        zeros = jnp.zeros((units, width // units, 128), BF16)
        both = [rest_grad(me, att, gfl, tok_u, dq_t, tt, gs_t, zeros, c) for c in (0, 1)]
        g3 = jnp.stack(both, 1).reshape(width, -1)
        g2 = jnp.stack([in_grad(mt, dh, c) for c in (0, 1)], 1).reshape(width, -1)
        g1 = jnp.stack([down_grad(at, gb, c) for c in (0, 1)], 1).reshape(ff, width)
        grads = (g3[:, width : 4 * width], st_qkv, g3[:, :width], st[5], st[3], st[4], g2, st_in, g1, st[2], st[0], st[1])
        grads = lax.psum_scatter(tuple(g.astype(F32) for g in grads), ("dp", "seq"), scatter_dimension=0, tiled=True)
        gproj = lax.psum(gproj, "dp").astype(F32)
        return (layer_out, grad_tokens, *grads, gproj)

    g1 = finish(rx1, kx1, Y_BIT, ff // n_dp)
    g2 = finish(rx2, kx2, X_BIT, width // n_dp)
    g3 = finish(rx3, kx3, Y_BIT, width // n_dp)
    for bit in (CORE, X_BIT, Y_BIT):
        gproj = add(gproj, swap(gproj, bit))
    small = g3[:3, 4 * width :].reshape(-1)
    sizes = [v.shape[0] // n_all for v in vectors]
    cuts, at_ = [], 0
    for size in sizes:
        cuts.append(small[at_ : at_ + size])
        at_ += size
    gb_qkv, gb_out, g_g1, g_b1, gb_in, gb_down, g_g2, g_b2 = cuts
    return (
        layer_out, grad_tokens, g3[:, width : 4 * width], gb_qkv, g3[:, :width], gb_out, g_g1, g_b1,
        g2, gb_in, g1, gb_down, g_g2, g_b2, gproj.astype(F32),
    )


def solution(mesh):
    both = ("dp", "seq")
    placed = (
        P("dp", "seq", None),
        P("dp", "seq"),
        P("dp", None, None),
        *([P()] * 12),
        P(None, "seq"),
        P("dp", "seq", None),
    )
    out = (
        P("dp", "seq", None),
        P("dp", "seq", None),
        P(both, None),
        P(both),
        P(both, None),
        P(both),
        P(both),
        P(both),
        P(both, None),
        P(both),
        P(both, None),
        P(both),
        P(both),
        P(both),
        P(None, "seq"),
    )
    run = functools.partial(body, mesh.shape["dp"], mesh.shape["seq"])
    return jax.shard_map(run, mesh=mesh, in_specs=placed, out_specs=out, check_vma=False)
```

```python
import functools

import jax
import jax.numpy as jnp
from jax import lax
from jax.experimental import pallas as pl
from jax.experimental.pallas import tpu as pltpu
from jax.sharding import PartitionSpec as P

HD = 64
KP = 256
NSEG = 4
TE = 272
EPS = 1e-05
SCALE = 0.125
HALF_ROOT = 0.7071067811865476
INV_ROOT_TAU = 0.3989422804014327
F32 = jnp.float32
BF16 = jnp.bfloat16
MIB = 2**20
VM = pl.BlockSpec(memory_space=pltpu.VMEM)
ANY = pl.BlockSpec(memory_space=pl.ANY)


def dot(left, right, cl=1, cr=0):
    return lax.dot_general(left, right, (((cl,), (cr,)), ((), ())), preferred_element_type=F32)


def in_vmem(x):
    return pltpu.with_memory_space_constraint(x, pltpu.VMEM)


def in_hbm(x):
    return pltpu.with_memory_space_constraint(x, pltpu.HBM)


def V(*shape, dtype=BF16):
    return pltpu.VMEM(shape, dtype)


def H(*shape, dtype=BF16):
    return pltpu.HBM(shape, dtype)


def call(kernel, name, args, outs, grid=(1,), in_specs=None, out_specs=None, scratch=(), limit=24, flops=0, nbytes=0, prefetch=()):
    placed = [{"v": in_vmem, "h": in_hbm}[where](x) for x, where, _ in args]
    default = {"v": VM, "h": ANY}
    specs = [default[where] if spec is None else spec for _, where, spec in args]
    single = not isinstance(outs, list)
    if single:
        outs = [outs]
    shapes = [o for o, _ in outs]
    ospecs = [spec if spec is not None else VM for o, spec in outs]
    res = pl.pallas_call(
        kernel,
        tuple(shapes),
        grid_spec=pltpu.PrefetchScalarGridSpec(
            num_scalar_prefetch=len(prefetch),
            grid=grid,
            in_specs=specs,
            out_specs=tuple(ospecs),
            scratch_shapes=list(scratch),
        ),
        compiler_params=pltpu.CompilerParams(vmem_limit_bytes=limit * MIB),
        cost_estimate=pl.CostEstimate(flops=int(flops), bytes_accessed=int(nbytes), transcendentals=0),
        name=name,
    )(*prefetch, *placed)
    return res[0] if single else res


def block(shape, index):
    return pl.BlockSpec(shape, index)


def whole(shape):
    return pl.BlockSpec(shape, lambda *_: (0,) * len(shape))


def columns(row):
    return jnp.transpose(jnp.broadcast_to(row, (8, row.shape[-1])))[:, 0:1]


def prep_kernel(s, tok_ref, seg_ref, mask_ref, proj_ref, t_ref, al_ref, wt_ref):
    width = tok_ref.shape[-1]
    length = tok_ref.shape[1]
    m = mask_ref[0]
    owner = jnp.sum(m * lax.broadcasted_iota(jnp.int32, m.shape, 0), 0, keepdims=True).astype(F32)
    allowed = columns(owner) == seg_ref[s : s + 1, :].astype(F32)
    weighted = jnp.where(allowed, proj_ref[...].astype(F32), 0.0).astype(BF16)
    al_ref[...] = jnp.where(allowed, 1.0, 0.0).astype(BF16)
    wt_ref[...] = weighted
    t_ref[0:KP, :] = dot(weighted, tok_ref[0]).astype(BF16)
    count = dot(jnp.ones((TE - KP, length), BF16), weighted, 1, 1).astype(BF16)
    t_ref[KP:TE, :] = jnp.concatenate([count, jnp.zeros((TE - KP, width - KP), BF16)], 1)


def prep(s, tokens, segment_ids, mask, proj_e):
    seqs, length, width = tokens.shape
    return call(
        functools.partial(prep_kernel, s),
        "prep",
        [
            (tokens, "h", block((1, length, width), lambda i: (s, 0, 0))),
            (segment_ids, "h", whole((seqs, length))),
            (mask, "h", block((1, NSEG, KP), lambda i: (s, 0, 0))),
            (proj_e, "h", whole((KP, length))),
        ],
        [(V(TE, width), None), (V(KP, length), None), (V(KP, length), None)],
        limit=5,
        flops=2 * KP * length * width,
        nbytes=2 * length * width,
    )


def query_kernel(me_ref, tok_ref, wq_ref, bq_ref, win_hbm, wdn_hbm, wo_hbm, q_ref, tt_ref, win_ref, wdn_ref, wo_ref, sem):
    pairs = ((wo_hbm, wo_ref), (win_hbm, win_ref), (wdn_hbm, wdn_ref))
    loads = [pltpu.make_async_copy(a, b, sem.at[k]) for k, (a, b) in enumerate(pairs)]

    @pl.when(pl.program_id(0) == 0)
    def _():
        for c in loads:
            c.start()

    units, rows = 2 * tt_ref.shape[1], tt_ref.shape[3]
    tok = tok_ref[0]
    q = (dot(tok, wq_ref[...]) + bq_ref[...]).astype(BF16).astype(F32) * SCALE
    q_ref[0] = jnp.transpose(q.astype(BF16))
    tt = jnp.transpose(tok)
    for u in range(units):
        r = u ^ me_ref[0]
        tt_ref[0, r >> 1, r & 1] = tt[u * rows : (u + 1) * rows]

    @pl.when(pl.program_id(0) == pl.num_programs(0) - 1)
    def _():
        for c in loads:
            c.wait()


def query(me, units, tokens, w_qkv, b_qkv, w_in, w_down, w_out):
    seqs, length, width = tokens.shape
    rows = width // units
    return call(
        query_kernel,
        "query",
        [
            (tokens, "h", block((1, length, width), lambda s, me: (s, 0, 0))),
            (w_qkv, "h", block((width, width), lambda s, me: (0, 0))),
            (b_qkv, "h", block((1, width), lambda s, me: (0, 0))),
            (w_in, "h", None),
            (w_down, "h", None),
            (w_out, "h", None),
        ],
        [
            (H(seqs, width, length), block((1, width, length), lambda s, me: (s, 0, 0))),
            (H(seqs, units // 2, 2, rows, length), block((1, units // 2, 2, rows, length), lambda s, me: (s, 0, 0, 0, 0))),
            (V(*w_in.shape), None),
            (V(*w_down.shape), None),
            (V(*w_out.shape), None),
        ],
        grid=(seqs,),
        prefetch=(me,),
        scratch=[pltpu.SemaphoreType.DMA((3,))],
        limit=10,
        flops=2 * seqs * width * length * width,
        nbytes=6 * seqs * length * width,
    )


def flip_kernel(w_ref, b_ref, bin_ref, o_ref, c_ref, cin_ref):
    o_ref[pl.program_id(0)] = jnp.transpose(w_ref[...])

    @pl.when(pl.program_id(0) == 0)
    def _():
        width = w_ref.shape[0]
        c_ref[...] = columns(b_ref[:, width:])
        cin_ref[...] = columns(bin_ref[...])


def flip(w_qkv, b_qkv, b_in):
    width = w_qkv.shape[0]
    ff = b_in.shape[1]
    return call(
        flip_kernel,
        "flip",
        [
            (w_qkv, "h", block((width, width), lambda i: (0, 1 + i))),
            (b_qkv, "h", whole((1, 3 * width))),
            (b_in, "h", whole((1, ff))),
        ],
        [(V(2, width, width), None), (V(2 * width, 1, dtype=F32), None), (V(ff, 1, dtype=F32), None)],
        grid=(2,),
        limit=6,
        nbytes=8 * width * width,
    )


def norm_stats(resid):
    center = resid - jnp.mean(resid, -1, keepdims=True)
    inverse = lax.rsqrt(jnp.mean(center * center, -1, keepdims=True) + EPS)
    return center * inverse, inverse


ROWS = 32
LANES = 128


def attend_kernel(nt, s, me_ref, own_ref, *refs):
    t_hbm = refs[:nt]
    wkv_ref, bkv_ref, q_hbm, al_ref, tok_ref, wo_ref, bo_ref = refs[nt : nt + 7]
    tt_ref, c_ref, kv_ref, p_hbm, att_ref, n_ref, inv_ref = refs[nt + 7 : nt + 14]
    t_scr, q_scr, p_scr, res_scr, att_scr, bias_scr, in_sem, out_sem = refs[nt + 14 :]
    width = wo_ref.shape[0]
    length = q_scr.shape[1]
    heads = width // HD
    units, rows = 2 * tt_ref.shape[0], tt_ref.shape[2]
    loads = [pltpu.make_async_copy(t_hbm[k], t_scr.at[k], in_sem.at[k]) for k in range(nt)]
    loads.append(pltpu.make_async_copy(q_hbm.at[s], q_scr, in_sem.at[nt]))
    for c in loads:
        c.start()
    bias_scr[...] = (al_ref[...].astype(F32) - 1.0) * 1e30
    for c in loads[:nt]:
        c.wait()
    total = own_ref[...].astype(F32)
    for k in range(nt):
        total = total + t_scr[k].astype(F32)
    low = total.astype(BF16)
    t_low = low[0:KP]
    c_row = low[KP : KP + 8, 0:KP]
    c_ref[...] = c_row
    wide_c = c_row[0:1].astype(F32)
    for k in range(2):
        part = slice(k * width, (k + 1) * width)
        kv_ref[part, :] = (dot(wkv_ref[k], t_low, 1, 1) + bkv_ref[part, :] * wide_c).astype(BF16)
    tt = jnp.transpose(t_low)
    me = me_ref[0]
    for u in range(units):
        r = u ^ me
        tt_ref[r >> 1, r & 1] = tt[u * rows : (u + 1) * rows]
    loads[nt].wait()

    tiles = [(h, j) for h in range(heads) for j in range(length // LANES)]
    keys = {}

    def score(h, j):
        if j == 0:
            keys[h] = jnp.transpose(kv_ref[h * HD : (h + 1) * HD, :])
        return dot(keys[h], q_scr[h * HD : (h + 1) * HD, j * LANES : (j + 1) * LANES])

    stores = [pltpu.make_async_copy(p_scr.at[h], p_hbm.at[h], out_sem.at[h]) for h in range(heads)]
    scores = score(*tiles[0])
    for i, (h, j) in enumerate(tiles):
        after = score(*tiles[i + 1]) if i + 1 < len(tiles) else None
        where = slice(j * LANES, (j + 1) * LANES)
        scores = scores + bias_scr[:, where]
        expo = jnp.exp(scores - jnp.max(scores, 0, keepdims=True))
        probs = (expo * (1.0 / jnp.sum(expo, 0, keepdims=True))).astype(BF16)
        p_scr[h, :, where] = probs
        if j == length // LANES - 1:
            att_scr[h * HD : (h + 1) * HD, :] = dot(kv_ref[width + h * HD : width + (h + 1) * HD, :], p_scr[h]).astype(BF16)
            if h:
                stores[h - 1].start()
        scores = after
    stores[heads - 1].start()
    att = att_scr[...]
    res_scr[...] = dot(att, wo_ref[...], 0, 0)
    for u in range(units):
        r = u ^ me
        att_ref[r >> 1, r & 1] = att_scr[u * rows : (u + 1) * rows, :]
    for r in range(0, length, ROWS):
        part = slice(r, r + ROWS)
        normed, inverse = norm_stats(res_scr[part, :] + tok_ref[0, part, :].astype(F32) + bo_ref[...])
        n_ref[part, :] = normed
        inv_ref[part, :] = inverse
    for c in stores:
        c.wait()


def attend(me, s, units, own, others, wkv_t, bkv_col, q_t, allow, tokens, w_out, b_out):
    seqs, length, width = tokens.shape
    rows = width // units
    heads = width // HD
    nt = len(others)
    return call(
        functools.partial(attend_kernel, nt, s),
        "attend",
        [(own, "v", None)]
        + [(t, "h", None) for t in others]
        + [
            (wkv_t, "v", None),
            (bkv_col, "v", None),
            (q_t, "h", None),
            (allow, "v", None),
            (tokens, "h", block((1, length, width), lambda i, me: (s, 0, 0))),
            (w_out, "v", None),
            (b_out, "h", whole((1, width))),
        ],
        [
            (V(units // 2, 2, rows, KP), None),
            (V(8, KP), None),
            (V(2 * width, KP), None),
            (H(heads, KP, length), ANY),
            (V(units // 2, 2, rows, length), None),
            (V(length, width, dtype=F32), None),
            (V(length, 1, dtype=F32), None),
        ],
        prefetch=(me,),
        scratch=[
            pltpu.VMEM((max(nt, 1), TE, width), BF16),
            pltpu.VMEM((width, length), BF16),
            pltpu.VMEM((heads, KP, length), BF16),
            pltpu.VMEM((length, width), F32),
            pltpu.VMEM((width, length), BF16),
            pltpu.VMEM((KP, length), F32),
            pltpu.SemaphoreType.DMA((nt + 1,)),
            pltpu.SemaphoreType.DMA((heads,)),
        ],
        limit=12,
        flops=2 * KP * width * 2 * width + 8 * KP * length * width + 2 * length * width * width,
        nbytes=10 * MIB,
    )


def norm_back(upstream, normed, inverse, gain):
    scaled = upstream * gain
    return inverse * (
        scaled
        - jnp.mean(scaled, -1, keepdims=True)
        - normed * jnp.mean(scaled * normed, -1, keepdims=True)
    )


FR = 16


def feed_kernel(
    steps, me_ref, n_ref, inv_ref, g1_ref, be1_ref, win_ref, bin_ref, wdn_ref, bdn_ref, g2_ref, be2_ref, cot_ref,
    mt_ref, at_ref, gb_ref, dh_ref, out_ref, gf_ref, gfl_ref, stat_ref,
    low_scr, acc_scr, slope_scr, h0_scr, h1_scr,
):
    step = pl.program_id(0)
    me = me_ref[0]
    units, rows = 2 * mt_ref.shape[0], mt_ref.shape[2]
    arows = at_ref.shape[2]
    length, width = n_ref.shape
    half = h0_scr.shape[0]
    per = half // arows

    @pl.when(step == 0)
    def _():
        for r in range(0, length, ROWS):
            part = slice(r, r + ROWS)
            mid = n_ref[part, :] * g1_ref[...] + be1_ref[...]
            low_scr[part, :] = mid.astype(BF16)
            acc_scr[part, :] = mid + bdn_ref[...]
        mt = jnp.transpose(low_scr[...])
        for u in range(units):
            r = u ^ me
            mt_ref[r >> 1, r & 1] = mt[u * rows : (u + 1) * rows]

    def unit(base, i):
        r = (base + i) ^ me
        return r >> 1, r & 1

    @pl.when(step < steps)
    def _():
        base = step * 2 * per

        def gelu(k, h_scr):
            for f in range(0, half, FR):
                at = k * half + f
                hidden = h_scr[f : f + FR, :] + bin_ref[pl.ds(pl.multiple_of(step * 2 * half + at, FR), FR), :]
                phi = 0.5 + 0.5 * lax.erf(hidden * HALF_ROOT)
                bell = jnp.exp(-0.5 * hidden * hidden)
                hi, lo = unit(base, at // arows)
                at_ref[hi, lo, at % arows : at % arows + FR, :] = (hidden * phi).astype(BF16)
                slope_scr[step, at : at + FR, :] = (phi + (hidden * INV_ROOT_TAU) * bell).astype(BF16)

        def cut(k):
            return pl.ds(pl.multiple_of(step * 2 * half + k * half, half), half)

        def second(k):
            activ = jnp.concatenate([at_ref[unit(base, k * per + i)] for i in range(per)], 0)
            acc_scr[...] += dot(activ, wdn_ref[cut(k), :], 0, 0)

        low = low_scr[...]
        h0_scr[...] = dot(win_ref[:, cut(0)], low, 0, 1)
        h1_scr[...] = dot(win_ref[:, cut(1)], low, 0, 1)
        gelu(0, h0_scr)
        second(0)
        gelu(1, h1_scr)
        second(1)

    @pl.when(step == steps - 1)
    def _():
        sums = [jnp.zeros((1, width), F32)] * 3
        for r in range(0, length, ROWS):
            part = slice(r, r + ROWS)
            normed, inverse = norm_stats(acc_scr[part, :])
            out_ref[part, :] = (normed * g2_ref[...] + be2_ref[...]).astype(BF16)
            cot = cot_ref[0, part, :].astype(F32)
            second = norm_back(cot, normed, inverse, g2_ref[...])
            low = second.astype(BF16)
            gb_ref[part, :] = low
            acc_scr[part, :] = second
            terms = (cot * normed, cot, low.astype(F32))
            sums = [a + jnp.sum(t, 0, keepdims=True) for a, t in zip(sums, terms)]
        for k in range(3):
            stat_ref[k : k + 1, :] = sums[k]

    @pl.when(step >= steps)
    def _():
        back = step - steps
        gb = gb_ref[...]

        def slope(k, h_scr):
            for f in range(0, half, FR):
                at = k * half + f
                dh = (h_scr[f : f + FR, :] * slope_scr[back, at : at + FR, :].astype(F32)).astype(BF16)
                row = pl.ds(pl.multiple_of(back * 2 * half + at, FR), FR)
                dh_ref[row, :] = dh

        def cut(k):
            return pl.ds(pl.multiple_of(back * 2 * half + k * half, half), half)

        def down(k):
            acc_scr[...] += dot(dh_ref[cut(k), :], win_ref[:, cut(k)], 0, 1)

        h0_scr[...] = dot(wdn_ref[cut(0), :], gb, 1, 1)
        h1_scr[...] = dot(wdn_ref[cut(1), :], gb, 1, 1)
        slope(0, h0_scr)
        down(0)
        slope(1, h1_scr)
        down(1)

    @pl.when(step == 2 * steps - 1)
    def _():
        sums = [jnp.zeros((1, width), F32)] * 3
        for r in range(0, length, ROWS):
            part = slice(r, r + ROWS)
            up = acc_scr[part, :]
            normed = n_ref[part, :]
            first = norm_back(up, normed, inv_ref[part, :], g1_ref[...])
            low = first.astype(BF16)
            gf_ref[part, :] = first
            gfl_ref[part, :] = low
            terms = (up * normed, up, low.astype(F32))
            sums = [a + jnp.sum(t, 0, keepdims=True) for a, t in zip(sums, terms)]
        for k in range(3):
            stat_ref[3 + k : 4 + k, :] = sums[k]
        stat_ref[6:8, :] = jnp.zeros((2, width), F32)


def feed(me, s, units, normed, inverse, g1, be1, w_in, bin_col, w_down, b_down, g2, be2, cot):
    length, width = normed.shape
    ff = w_in.shape[1]
    rows = width // units
    arows = ff // units
    chunk = 768
    steps = ff // chunk
    vec = whole((1, width))
    return call(
        functools.partial(feed_kernel, steps),
        "feed",
        [
            (normed, "v", None),
            (inverse, "v", None),
            (g1, "h", vec),
            (be1, "h", vec),
            (w_in, "v", None),
            (bin_col, "v", None),
            (w_down, "v", None),
            (b_down, "h", vec),
            (g2, "h", vec),
            (be2, "h", vec),
            (cot, "h", block((1, length, width), lambda i, me: (s, 0, 0))),
        ],
        [
            (V(units // 2, 2, rows, length), None),
            (V(units // 2, 2, arows, length), None),
            (V(length, width), None),
            (V(ff, length), None),
            (H(length, width), whole((length, width))),
            (H(length, width, dtype=F32), whole((length, width))),
            (V(length, width), None),
            (V(8, width, dtype=F32), None),
        ],
        grid=(2 * steps,),
        prefetch=(me,),
        scratch=[
            pltpu.VMEM((length, width), BF16),
            pltpu.VMEM((length, width), F32),
            pltpu.VMEM((steps, chunk, length), BF16),
            pltpu.VMEM((chunk // 2, length), F32),
            pltpu.VMEM((chunk // 2, length), F32),
        ],
        limit=18,
        flops=8 * length * width * ff,
        nbytes=24 * MIB,
    )


def attend_back_kernel(s, gfl_ref, wo_ref, kv_ref, p_hbm, q_hbm, c_ref, wkv_ref, bkv_ref, dq_ref, gs_ref, gt_ref, col_ref, da_scr, p_scr, q_scr, ds0_scr, ds1_scr, sem):
    width = wo_ref.shape[0]
    length = gfl_ref.shape[0]
    heads = width // HD
    loads = [pltpu.make_async_copy(q_hbm.at[s], q_scr, sem.at[heads])]
    loads += [pltpu.make_async_copy(p_hbm.at[h], p_scr.at[h], sem.at[h]) for h in range(heads)]
    for c in loads:
        c.start()
    da_scr[...] = dot(wo_ref[...], gfl_ref[...], 1, 1).astype(BF16)
    loads[0].wait()
    c_wide = c_ref[0:1, :].astype(F32)

    def cut(h):
        return slice(h * HD, (h + 1) * HD)

    def low(h):
        return slice(width + h * HD, width + (h + 1) * HD)

    tiles = [(h, j) for h in range(heads) for j in range(length // LANES)]
    vals = {}

    def first(h, j):
        if j == 0:
            loads[h + 1].wait()
            vals[h] = jnp.transpose(kv_ref[low(h), :])
        return dot(vals[h], da_scr[cut(h), j * LANES : (j + 1) * LANES])

    grad = first(*tiles[0])
    for i, (h, j) in enumerate(tiles):
        after = first(*tiles[i + 1]) if i + 1 < len(tiles) else None
        where = slice(j * LANES, (j + 1) * LANES)
        ds_scr = (ds0_scr, ds1_scr)[h % 2]
        wide = p_scr[h, :, where].astype(F32)
        prod = wide * grad
        ds_scr[:, where] = (prod - wide * jnp.sum(prod, 0, keepdims=True)).astype(BF16)
        if j == length // LANES - 1:
            gv = dot(da_scr[cut(h), :], p_scr[h], 1, 1).astype(BF16)
            gs_ref[low(h), :] = gv
            col_ref[2 * width + h * HD : 2 * width + (h + 1) * HD, :] = jnp.sum(gv.astype(F32) * c_wide, 1, keepdims=True)
            dq = (dot(kv_ref[cut(h), :], ds_scr[...]) * SCALE).astype(BF16)
            dq_ref[cut(h), :] = dq
            col_ref[cut(h), :] = jnp.sum(dq.astype(F32), 1, keepdims=True)
            gk = dot(q_scr[cut(h), :], ds_scr[...], 1, 1).astype(BF16)
            gs_ref[cut(h), :] = gk
            col_ref[low(h), :] = jnp.sum(gk.astype(F32) * c_wide, 1, keepdims=True)
        grad = after
    gt = dot(gs_ref[0:width, :], wkv_ref[0], 0, 0) + dot(gs_ref[width:, :], wkv_ref[1], 0, 0)
    gt_ref[0:KP, :] = gt.astype(BF16)
    pad = TE - KP
    b_hi = bkv_ref[...].astype(BF16)
    b_lo = (bkv_ref[...] - b_hi.astype(F32)).astype(BF16)
    gs = gs_ref[...]
    drow = dot(jnp.broadcast_to(b_hi, (pad, 2 * width)), gs) + dot(jnp.broadcast_to(b_lo, (pad, 2 * width)), gs)
    gt_ref[KP:TE, :] = jnp.concatenate([drow.astype(BF16), jnp.zeros((pad, width - KP), BF16)], 1)


def attend_back(s, gfl, w_out, kv_t, probs, q_t, c_row, wkv_t, bkv_row):
    length, width = gfl.shape
    heads = width // HD
    return call(
        functools.partial(attend_back_kernel, s),
        "attend_back",
        [
            (gfl, "v", None),
            (w_out, "v", None),
            (kv_t, "v", None),
            (probs, "h", None),
            (q_t, "h", None),
            (c_row, "v", None),
            (wkv_t, "v", None),
            (bkv_row, "h", whole((1, 2 * width))),
        ],
        [(V(width, length), None), (V(2 * width, KP), None), (V(TE, width), None), (V(3 * width, 1, dtype=F32), None)],
        scratch=[
            pltpu.VMEM((width, length), BF16),
            pltpu.VMEM((heads, KP, length), BF16),
            pltpu.VMEM((width, length), BF16),
            pltpu.VMEM((KP, length), BF16),
            pltpu.VMEM((KP, length), BF16),
            pltpu.SemaphoreType.DMA((heads + 1,)),
        ],
        limit=11,
        flops=(2 * KP * width * 2 * width + 16 * KP * length * width + 2 * length * width * width) // 1024,
        nbytes=1024,
    )


def token_kernel(gf_ref, dq_ref, wq_ref, o_ref):
    o_ref[...] = gf_ref[...] + dot(dq_ref[...], wq_ref[...], 0, 1)


def token_grad(gf, dq_t, w_qkv, weight=0):
    length, width = gf.shape
    return call(
        token_kernel,
        "token_grad",
        [(gf, "h", whole((length, width))), (dq_t, "v", None), (w_qkv, "h", block((width, width), lambda i: (0, 0)))],
        (V(length, width, dtype=F32), None),
        limit=8,
        flops=2 * length * width * width * weight,
        nbytes=MIB * weight,
    )


def last_kernel(seqs, nt, *refs):
    owns = refs[:seqs]
    t_hbm = refs[seqs : seqs + seqs * nt]
    base = seqs + seqs * nt
    part_refs = refs[base : base + seqs]
    wt_refs = refs[base + seqs : base + 2 * seqs]
    al_refs = refs[base + 2 * seqs : base + 3 * seqs]
    tok_ref, o_ref, gp_ref, low_scr, d_scr = refs[base + 3 * seqs :]
    s = pl.program_id(0)

    def one(k):
        total = owns[k][...].astype(F32)
        for r in t_hbm[k * nt : (k + 1) * nt]:
            total = total + r[...].astype(F32)
        low = total[0:KP].astype(BF16)
        d_col = columns(total[KP : KP + 1, 0:KP])
        o_ref[0] = part_refs[k][...] + dot(wt_refs[k][...], low, 0, 0)
        term = (dot(low, tok_ref[0], 1, 1) + d_col) * al_refs[k][...].astype(F32)
        d_scr[...] = term if k == 0 else d_scr[...] + term

    for k in range(seqs):
        pl.when(s == k)(functools.partial(one, k))

    @pl.when(s == seqs - 1)
    def _():
        gp_ref[...] = d_scr[...].astype(BF16)


def last(owns, others, parts, weights, allows, tokens):
    seqs, length, width = tokens.shape
    nt = len(others[0])
    return call(
        functools.partial(last_kernel, seqs, nt),
        "last",
        [(o, "v", None) for o in owns]
        + [(t, "h", whole((TE, width))) for ts in others for t in ts]
        + [(p, "v", None) for p in parts]
        + [(w, "v", None) for w in weights]
        + [(a, "v", None) for a in allows]
        + [(tokens, "h", block((1, length, width), lambda s: (s, 0, 0)))],
        [
            (H(seqs, length, width, dtype=F32), block((1, length, width), lambda s: (s, 0, 0))),
            (H(KP, length), whole((KP, length))),
        ],
        grid=(seqs,),
        scratch=[pltpu.VMEM((8, 128), BF16), pltpu.VMEM((KP, length), F32)],
        limit=14,
        flops=4 * seqs * length * width * KP,
        nbytes=8 * MIB,
    )


def split_store(low, send_ref, keep_ref, send_bit, where):
    n = low.shape[0]
    if send_bit == 0:
        for i in range(n):
            (send_ref if i & 1 else keep_ref)[i // 2, :, where] = low[i]
    else:
        half = n // 2
        keep_ref[:, :, where] = low[:half]
        send_ref[:, :, where] = low[half:]


def total(terms):
    out = terms[0]
    for t in terms[1:]:
        out = out + t
    return out


def down_kernel(seqs, core, chunk, send_bit, *refs):
    at_refs = refs[:seqs]
    gb_refs = refs[seqs : 2 * seqs]
    rest = refs[2 * seqs :]
    n, _, arows, length = at_refs[0].shape
    cols = pl.ds(pl.multiple_of(pl.program_id(0) * chunk, chunk), chunk)
    res = total([dot(a[:, core].reshape(n * arows, length), g[:, cols]) for a, g in zip(at_refs, gb_refs)])
    res = res.reshape(n, arows, chunk)
    if send_bit is None:
        rest[0][...] = res.astype(BF16)
    else:
        recv_ref, send_ref, keep_ref = rest
        low = (res + recv_ref[...].astype(F32)).astype(BF16)
        split_store(low, send_ref, keep_ref, send_bit, slice(None))


def down_grad(at, gb, core, recv=None, send_bit=None):
    seqs = len(at)
    n, _, arows, length = at[0].shape
    width = gb[0].shape[1]
    chunk = 256
    args = [(a, "v", None) for a in at] + [(g, "v", None) for g in gb]
    spec = block((n, arows, chunk), lambda i: (0, 0, i))
    if recv is None:
        outs = (H(n, arows, width), spec)
    else:
        args.append((recv, "h", spec))
        outs = [(H(n // 2, arows, width), block((n // 2, arows, chunk), lambda i: (0, 0, i)))] * 2
    return call(
        functools.partial(down_kernel, seqs, core, chunk, send_bit),
        "down_grad",
        args,
        outs,
        grid=(width // chunk,),
        limit=12,
        flops=2 * seqs * n * arows * length * width,
        nbytes=3 * MIB,
    )


def in_kernel(seqs, core, chunk, send_bit, *refs):
    mt_refs = refs[:seqs]
    dh_refs = refs[seqs : 2 * seqs]
    rest = refs[2 * seqs :]
    n, _, rows, length = mt_refs[0].shape
    part = pl.ds(pl.multiple_of(pl.program_id(0) * chunk, chunk), chunk)
    lefts = [a[:, core].reshape(n * rows, length) for a in mt_refs]
    if send_bit is None:
        lefts = [jnp.concatenate([a, jnp.ones((16, length), BF16)], 0) for a in lefts]
    res = total([dot(a, g[part, :], 1, 1) for a, g in zip(lefts, dh_refs)])
    if send_bit is None:
        out_ref, bias_ref = rest
        out_ref[...] = res[0 : n * rows].reshape(n, rows, chunk).astype(BF16)
        bias_ref[...] = res[n * rows : n * rows + 8]
    else:
        res = res.reshape(n, rows, chunk)
        recv_ref, send_ref, keep_ref = rest
        low = (res + recv_ref[...].astype(F32)).astype(BF16)
        split_store(low, send_ref, keep_ref, send_bit, slice(None))


def in_grad(mt, dh, core, recv=None, send_bit=None):
    seqs = len(mt)
    n, _, rows, length = mt[0].shape
    ff = dh[0].shape[0]
    chunk = 1536
    args = [(a, "v", None) for a in mt] + [(g, "v", None) for g in dh]
    spec = block((n, rows, chunk), lambda i: (0, 0, i))
    if recv is None:
        outs = [(H(n, rows, ff), spec), (H(8, ff, dtype=F32), block((8, chunk), lambda i: (0, i)))]
    else:
        args.append((recv, "h", spec))
        outs = [(H(n // 2, rows, ff), block((n // 2, rows, chunk), lambda i: (0, 0, i)))] * 2
    return call(
        functools.partial(in_kernel, seqs, core, chunk, send_bit),
        "in_grad",
        args,
        outs,
        grid=(ff // chunk,),
        limit=12,
        flops=2 * seqs * n * rows * length * ff,
        nbytes=3 * MIB,
    )


def pack_stats(stat_refs, bias_refs, col_refs, scr, bias_scr, group):
    rows = scr.shape[0]
    scr[...] = jnp.zeros_like(scr)
    stat = total([r[...] for r in stat_refs])
    scr[:, 0:8] = jnp.transpose(stat)
    bias_scr[...] = jnp.transpose(total([r[...] for r in bias_refs]))[:, 0:1]
    lane = 8
    for refs in (col_refs, [bias_scr]):
        per = refs[0].shape[0] // rows
        for b in range(rows // group):
            for c in range(per):
                src = slice((b * per + c) * group, (b * per + c + 1) * group)
                scr[b * group : (b + 1) * group, lane + c : lane + c + 1] = total([r[src, :] for r in refs])
        lane += per


def rest_kernel(seqs, group, me_ref, *refs):
    at_refs, gf_refs, tk_refs, dq_refs, tt_refs, gs_refs = [refs[k * seqs : (k + 1) * seqs] for k in range(6)]
    rest = refs[6 * seqs :]
    keep_ref, send_ref, st_scr, bias_scr = rest[-4:]
    n, _, rows, _ = at_refs[0].shape
    width = gf_refs[0].shape[1]

    def put(res, where):
        res = res.reshape(n, 2, rows, res.shape[-1]).astype(BF16)
        keep_ref[:, :, where] = res[:, 0]
        send_ref[:, :, where] = res[:, 1]

    def flat(ref):
        return ref[...].reshape(2 * n * rows, ref.shape[-1])

    if group:
        pack_stats(rest[:seqs], [rest[seqs]], rest[seqs + 1 : 2 * seqs + 1], st_scr, bias_scr, group)
        for u in range(2 * n):
            low = st_scr[pl.ds(pl.multiple_of((u ^ me_ref[0]) * rows, rows), rows), :].astype(BF16)
            (keep_ref, send_ref)[u % 2][u // 2, :, 4 * width : 4 * width + 128] = low
    else:
        for ref in (keep_ref, send_ref):
            ref[:, :, 4 * width : 4 * width + 128] = jnp.zeros((n, rows, 128), BF16)
    put(total([dot(flat(a), g[...]) for a, g in zip(at_refs, gf_refs)]), slice(0, width))
    put(total([dot(flat(a), g[...], 1, 1) for a, g in zip(tk_refs, dq_refs)]), slice(width, 2 * width))
    for k in range(2):
        part = slice(k * width, (k + 1) * width)
        put(total([dot(flat(a), g[part, :], 1, 1) for a, g in zip(tt_refs, gs_refs)]), slice((2 + k) * width, (3 + k) * width))


def rest_grad(me, att, gfl, tok_t, dq_t, t_t, gs_t, group, stats):
    seqs = len(att)
    n, _, rows, length = att[0].shape
    width = gfl[0].shape[1]
    cols = 4 * width + 128
    args = [(a, "v", None) for a in (*att, *gfl)]
    args += [(t, "h", block((pl.Squeezed(), n, 2, rows, length), lambda i, me, k=k: (k, 0, 0, 0, 0))) for k, t in enumerate([tok_t] * seqs)]
    args += [(a, "v", None) for a in (*dq_t, *t_t, *gs_t)]
    args += [(a, "v", None) for a in stats[0]] + [(stats[1], "h", whole(stats[1].shape))] + [(a, "v", None) for a in stats[2]]
    return call(
        functools.partial(rest_kernel, seqs, group),
        "rest_grad",
        args,
        [(H(n, rows, cols), whole((n, rows, cols)))] * 2,
        prefetch=(me,),
        scratch=[pltpu.VMEM((2 * n * rows, 128), F32), pltpu.VMEM((stats[1].shape[1], 1), F32)],
        limit=16,
        flops=seqs * 2 * n * rows * (4 * length * width + 4 * KP * width) // 1024,
        nbytes=1024,
    )


def halve_kernel(z_ref, ka_ref, ra_ref, kb_ref, rb_ref, send_ref, keep_ref):
    z = z_ref[0]
    cut = ka_ref.shape[-1]
    for k in range(2):
        for keep, recv, cols in ((ka_ref, ra_ref, slice(0, cut)), (kb_ref, rb_ref, slice(cut, None))):
            for where, out in ((1 - z, send_ref), (z, keep_ref)):
                out[k, :, cols] = (keep[k, where].astype(F32) + recv[k, where].astype(F32)).astype(BF16)


def halve_rest(z, ka, ra, kb, rb):
    group = ka.shape[0] // 4
    arrays = [x.reshape(2, 2, group, x.shape[-1]) for x in (ka, ra, kb, rb)]
    cols = ka.shape[-1] + kb.shape[-1]
    shape = (2, group, cols)
    return call(
        halve_kernel,
        "halve_rest",
        [(x, "h", whole(x.shape)) for x in arrays],
        [(H(*shape), whole(shape)), (H(*shape), whole(shape))],
        prefetch=(z,),
        limit=6,
        nbytes=2 * MIB,
    )


def finish_kernel(z_ref, keep_ref, recv_ref, qkv_ref, out_ref, small_ref):
    width = out_ref.shape[1]
    res = keep_ref[...].astype(F32) + recv_ref[...].astype(F32)
    out_ref[...] = res[:, 0:width]
    qkv_ref[...] = res[:, width : 4 * width]
    small_ref[...] = jnp.transpose(res[:, 4 * width :])[0:16]


def finish_rest(z, keep, recv):
    group, cols = keep.shape
    width = (cols - 128) // 4
    return call(
        finish_kernel,
        "finish_rest",
        [(keep, "h", whole((group, cols))), (recv, "h", whole((group, cols)))],
        [
            (H(group, 3 * width, dtype=F32), whole((group, 3 * width))),
            (H(group, width, dtype=F32), whole((group, width))),
            (H(16, group, dtype=F32), whole((16, group))),
        ],
        prefetch=(z,),
        limit=5,
        nbytes=MIB,
    )


def add(a, b):
    return (a.astype(F32) + b.astype(F32)).astype(BF16)


def body(n_dp, n_seq, tokens, segment_ids, mask, w_qkv, b_qkv, w_out, b_out, ln1_gain, ln1_bias, w_in, b_in, w_down, b_down, ln2_gain, ln2_bias, proj_e, cotangent):
    seqs, length, width = tokens.shape
    ff = w_in.shape[1]
    n_all = n_dp * n_seq
    fast = n_dp == 8 and n_seq == 4 and length >= 512
    units = 8
    dp = lax.axis_index("dp").astype(jnp.int32)
    sq = lax.axis_index("seq").astype(jnp.int32)
    me = (dp if fast else jnp.zeros((), jnp.int32)).reshape(1)
    row = lambda v: v.reshape(1, -1)

    def swap(x, bit):
        pairs = [(i, i ^ bit) for i in range(n_all)]
        return lax.ppermute(x, ("dp", "seq"), pairs)

    near = [(i, i ^ 1) for i in range(n_seq)]
    mid = [(1, 2), (2, 1)]

    def hop_one(own):
        return lax.ppermute(own, "seq", near), lax.ppermute(own, "seq", mid)

    def hop_two(first):
        return lax.ppermute(first[1], "seq", near), lax.ppermute(first[0], "seq", mid)

    def tie(x, *deps):
        return lax.optimization_barrier((x, *deps))[0]

    first = prep(0, tokens, segment_ids, mask, proj_e)
    prepped = [first] + [prep(s, tie(tokens, first[0]), segment_ids, mask, proj_e) for s in range(1, seqs)]
    owns = [p[0] for p in prepped]
    wkv_t, bkv_col, bin_col = flip(tie(w_qkv, *owns), row(b_qkv), row(b_in))
    others = [[] for _ in owns]
    if fast:
        one = tuple(tie(x, wkv_t) for x in hop_one(owns[0]))
        q_t, tok_t, w_in, w_down, w_out = query(me, units, tie(tokens, wkv_t, *one), w_qkv, row(b_qkv), w_in, w_down, w_out)
        others[0] = [*one, *(tie(x, q_t) for x in hop_two(one))]
    else:
        q_t, tok_t, w_in, w_down, w_out = query(me, units, tie(tokens, wkv_t), w_qkv, row(b_qkv), w_in, w_down, w_out)
        owns = [lax.psum(o, "seq") for o in owns]

    tt, crow, kv, probs, att, normed, inverse = [], [], [], [], [], [], []
    mt, at, gb, dh, outs, gf, gfl, stat = [], [], [], [], [], [], [], []
    for s in range(seqs):
        own = tie(owns[s], gfl[s - 1]) if s else owns[s]
        if fast and s + 1 < seqs:
            one = hop_one(tie(owns[s + 1], q_t, *others[s]))
        res = attend(me, s, units, own, others[s], wkv_t, bkv_col, q_t, prepped[s][1], tokens, w_out, row(b_out))
        for store, value in zip((tt, crow, kv, probs, att, normed, inverse), res):
            store.append(value)
        if fast and s + 1 < seqs:
            normed[s] = tie(normed[s], *one)
            others[s + 1] = [*one, *hop_two(one)]
        res = feed(me, s, units, normed[s], inverse[s], row(ln1_gain), row(ln1_bias), w_in, bin_col, w_down, row(b_down), row(ln2_gain), row(ln2_bias), cotangent)
        for store, value in zip((mt, at, gb, dh, outs, gf, gfl, stat), res):
            store.append(value)

    X_BIT, Y_BIT, CORE = 2 * n_seq, 4 * n_seq, n_seq
    z0, z1 = sq & 1, sq >> 1

    def halve(recv, keep):
        return add(keep[1], recv[1]), add(keep[0], recv[0])

    def halve_z0(recv, keep):
        group = keep.shape[0] // 4
        shape = (2, 2, group, keep.shape[-1])
        pick = lambda a, z: lax.dynamic_index_in_dim(a, z, 1, keepdims=False)
        keep, recv = keep.reshape(shape), recv.reshape(shape)
        return add(pick(keep, 1 - z0), pick(recv, 1 - z0)), add(pick(keep, z0), pick(recv, z0))

    def halve_z1(recv, keep):
        pick = lambda a, z: lax.dynamic_index_in_dim(a, z, 0, keepdims=False)
        return add(pick(keep, 1 - z1), pick(recv, 1 - z1)), add(pick(keep, z1), pick(recv, z1))

    back_in = list(gfl)
    if fast:
        send1 = down_grad(at, gb, 1)
        recv1 = swap(send1, CORE)
        send2, gbin = in_grad([tie(mt[0], send1), *mt[1:]], dh, 1)
        recv2 = swap(send2, CORE)
        sx1, kx1 = down_grad([tie(at[0], send2), *at[1:]], gb, 0, recv1, 0)
        rx1 = swap(sx1, X_BIT)
        sx2, kx2 = in_grad([tie(mt[0], sx1), *mt[1:]], dh, 0, recv2, 1)
        rx2 = swap(sx2, Y_BIT)
        back_in[0] = tie(gfl[0], sx2)

    back = []
    for s in range(seqs):
        if s:
            back_in[s] = tie(back_in[s], back[s - 1][2])
        back.append(attend_back(s, back_in[s], w_out, kv[s], probs[s], q_t, crow[s], wkv_t, row(b_qkv[width:])))
    dq_t = [b[0] for b in back]
    gs_t = [b[1] for b in back]
    gouts = [b[2] for b in back]
    if not fast:
        half2, gbin = in_grad(mt, dh, 1)
    stats = (stat, gbin, [b[3] for b in back])

    if fast:
        group = width // n_all
        gones = [hop_one(g) for g in gouts]
        sy1, ky1 = halve(rx1, kx1)
        ry1 = swap(sy1, Y_BIT)
        gtwo = hop_two(gones[0])
        sy2, ky2 = halve(rx2, kx2)
        ry2 = swap(sy2, X_BIT)
        keep3, send3 = rest_grad(me, [tie(att[0], sy1, sy2, *gones[0]), *att[1:]], gfl, tok_t, dq_t, tt, gs_t, group, stats)
        recv3 = swap(send3, CORE)
        parts = [token_grad(gf[0], tie(dq_t[0], send3), w_qkv)]
        after = (parts[0], ry1, ry2, *gtwo)
        for s in range(1, seqs):
            parts.append(token_grad(gf[s], tie(dq_t[s], *after), w_qkv, 16))
            after = (parts[-1],)
        recv3 = tie(recv3, *after)
        half, cut = units // 4, 2 * width
        pair = lambda a: a.reshape(half, 2, width // units, a.shape[-1])
        k3, r3 = pair(keep3), pair(recv3)
        sx3, kx3 = add(k3[:, 1, :, :cut], r3[:, 1, :, :cut]), add(k3[:, 0, :, :cut], r3[:, 0, :, :cut])
        sy3, ky3 = add(k3[1, :, :, cut:], r3[1, :, :, cut:]), add(k3[0, :, :, cut:], r3[0, :, :, cut:])
        rx3 = swap(sx3, X_BIT)
        ry3 = swap(sy3, Y_BIT)
        gtwos = [gtwo] + [hop_two(tuple(tie(x, sx3, sy3) for x in g)) for g in gones[1:]]
        gothers = [[*a, *b] for a, b in zip(gones, gtwos)]
    else:
        parts = [token_grad(gf[s], dq_t[s], w_qkv) for s in range(seqs)]
        gouts = [lax.psum(g, "seq") for g in gouts]
        gothers = [[] for _ in gouts]

    grad_tokens, gproj = last(gouts, gothers, parts, [p[2] for p in prepped], [p[1] for p in prepped], tokens)
    layer_out = jnp.stack(outs)

    if not fast:
        g3 = jnp.stack(rest_grad(me, att, gfl, tok_t, dq_t, tt, gs_t, 0, stats), 1).reshape(width, -1)
        g2 = jnp.stack([in_grad(mt, dh, 0)[0], half2], 1).reshape(width, -1)
        g1 = jnp.stack([down_grad(at, gb, c) for c in (0, 1)], 1).reshape(ff, width)
        st = total(stat)
        st_in, st_qkv = gbin[0], total(stats[2]).reshape(-1)
        grads = (g3[:, width : 4 * width], st_qkv, g3[:, :width], st[5], st[3], st[4], g2, st_in, g1, st[2], st[0], st[1])
        grads = lax.psum_scatter(tuple(g.astype(F32) for g in grads), ("dp", "seq"), scatter_dimension=0, tiled=True)
        gproj = lax.psum(gproj, "dp").astype(F32)
        return (layer_out, grad_tokens, *grads, gproj)

    sz1, kz1 = halve_z0(tie(ry1, sx3, sy3), ky1)
    rz1 = swap(sz1, 1)
    gproj = add(gproj, swap(gproj, CORE))
    gall = [gproj] + [swap(gproj, bit) for bit in (X_BIT, Y_BIT, X_BIT | Y_BIT)]
    sz2, kz2 = halve_z0(tie(ry2, sx3, sy3), ky2)
    rz2 = swap(sz2, 1)
    sxy, kxy = halve(rx3, kx3)
    rxy = swap(sxy, Y_BIT)
    syx, kyx = halve(ry3, ky3)
    ryx = swap(syx, X_BIT)
    sw1, kw1 = halve_z1(rz1, kz1)
    rw1 = swap(sw1, 2)
    sw2, kw2 = halve_z1(rz2, kz2)
    rw2 = swap(sw2, 2)
    sz3, kz3 = halve_rest(z0.reshape(1), kxy, rxy, kyx, ryx)
    rz3 = swap(sz3, 1)
    gproj = total([g.astype(F32) for g in gall])
    g1 = kw1.astype(F32) + rw1.astype(F32)
    g2 = kw2.astype(F32) + rw2.astype(F32)
    sw3, kw3 = halve_z1(rz3, kz3)
    rw3 = swap(sw3, 2)
    g_qkv, g_out, small = finish_rest(z1.reshape(1), kw3, rw3)
    g_g2, g_b2, gb_down, g_g1, g_b1, gb_out = [small[k] for k in range(6)]
    gb_qkv = small[8:11].reshape(-1)
    gb_in = small[11:15].reshape(-1)
    return (
        layer_out, grad_tokens, g_qkv, gb_qkv, g_out, gb_out, g_g1, g_b1,
        g2, gb_in, g1, gb_down, g_g2, g_b2, gproj,
    )


def solution(mesh):
    both = ("dp", "seq")
    placed = (
        P("dp", "seq", None),
        P("dp", "seq"),
        P("dp", None, None),
        *([P()] * 12),
        P(None, "seq"),
        P("dp", "seq", None),
    )
    out = (
        P("dp", "seq", None),
        P("dp", "seq", None),
        P(both, None),
        P(both),
        P(both, None),
        P(both),
        P(both),
        P(both),
        P(both, None),
        P(both),
        P(both, None),
        P(both),
        P(both),
        P(both),
        P(None, "seq"),
    )
    run = functools.partial(body, mesh.shape["dp"], mesh.shape["seq"])
    return jax.shard_map(run, mesh=mesh, in_specs=placed, out_specs=out, check_vma=False)
```

```python
import functools

import jax
import jax.numpy as jnp
from jax import lax
from jax.experimental import pallas as pl
from jax.experimental.pallas import tpu as pltpu
from jax.sharding import PartitionSpec as P

HD = 64
KP = 256
NSEG = 4
TE = 272
EPS = 1e-05
SCALE = 0.125
HALF_ROOT = 0.7071067811865476
INV_ROOT_TAU = 0.3989422804014327
F32 = jnp.float32
BF16 = jnp.bfloat16
MIB = 2**20
VM = pl.BlockSpec(memory_space=pltpu.VMEM)
ANY = pl.BlockSpec(memory_space=pl.ANY)


def dot(left, right, cl=1, cr=0):
    return lax.dot_general(left, right, (((cl,), (cr,)), ((), ())), preferred_element_type=F32)


def in_vmem(x):
    return pltpu.with_memory_space_constraint(x, pltpu.VMEM)


def in_hbm(x):
    return pltpu.with_memory_space_constraint(x, pltpu.HBM)


def V(*shape, dtype=BF16):
    return pltpu.VMEM(shape, dtype)


def H(*shape, dtype=BF16):
    return pltpu.HBM(shape, dtype)


def call(kernel, name, args, outs, grid=(1,), in_specs=None, out_specs=None, scratch=(), limit=24, flops=0, nbytes=0, prefetch=()):
    placed = [{"v": in_vmem, "h": in_hbm, "n": lambda x: x}[where](x) for x, where, _ in args]
    default = {"v": VM, "h": ANY, "n": ANY}
    specs = [default[where] if spec is None else spec for _, where, spec in args]
    single = not isinstance(outs, list)
    if single:
        outs = [outs]
    shapes = [o for o, _ in outs]
    ospecs = [spec if spec is not None else VM for o, spec in outs]
    res = pl.pallas_call(
        kernel,
        tuple(shapes),
        grid_spec=pltpu.PrefetchScalarGridSpec(
            num_scalar_prefetch=len(prefetch),
            grid=grid,
            in_specs=specs,
            out_specs=tuple(ospecs),
            scratch_shapes=list(scratch),
        ),
        compiler_params=pltpu.CompilerParams(vmem_limit_bytes=limit * MIB),
        cost_estimate=pl.CostEstimate(flops=int(flops), bytes_accessed=int(nbytes), transcendentals=0),
        name=name,
    )(*prefetch, *placed)
    return res[0] if single else res


def block(shape, index):
    return pl.BlockSpec(shape, index)


def whole(shape):
    return pl.BlockSpec(shape, lambda *_: (0,) * len(shape))


def columns(row):
    return jnp.transpose(jnp.broadcast_to(row, (8, row.shape[-1])))[:, 0:1]


def prep_kernel(s, tok_ref, seg_ref, mask_ref, proj_ref, t_ref, al_ref, wt_ref):
    width = tok_ref.shape[-1]
    length = tok_ref.shape[1]
    m = mask_ref[0]
    owner = jnp.sum(m * lax.broadcasted_iota(jnp.int32, m.shape, 0), 0, keepdims=True).astype(F32)
    allowed = columns(owner) == seg_ref[s : s + 1, :].astype(F32)
    weighted = jnp.where(allowed, proj_ref[...].astype(F32), 0.0).astype(BF16)
    al_ref[...] = jnp.where(allowed, 1.0, 0.0).astype(BF16)
    wt_ref[...] = weighted
    t_ref[0:KP, :] = dot(weighted, tok_ref[0]).astype(BF16)
    count = dot(jnp.ones((TE - KP, length), BF16), weighted, 1, 1).astype(BF16)
    t_ref[KP:TE, :] = jnp.concatenate([count, jnp.zeros((TE - KP, width - KP), BF16)], 1)


def prep(s, tokens, segment_ids, mask, proj_e):
    seqs, length, width = tokens.shape
    return call(
        functools.partial(prep_kernel, s),
        "prep",
        [
            (tokens, "h", block((1, length, width), lambda i: (s, 0, 0))),
            (segment_ids, "h", whole((seqs, length))),
            (mask, "h", block((1, NSEG, KP), lambda i: (s, 0, 0))),
            (proj_e, "h", whole((KP, length))),
        ],
        [(H(TE, width), whole((TE, width))), (H(KP, length), whole((KP, length))), (H(KP, length), whole((KP, length)))],
        limit=5,
        flops=2 * KP * length * width,
        nbytes=2 * length * width,
    )


def query_kernel(me_ref, tok_ref, wq_ref, bq_ref, win_hbm, wdn_hbm, wo_hbm, q_ref, tt_ref, win_ref, wdn_ref, wo_ref, sem):
    pairs = ((wo_hbm, wo_ref), (win_hbm, win_ref), (wdn_hbm, wdn_ref))
    loads = [pltpu.make_async_copy(a, b, sem.at[k]) for k, (a, b) in enumerate(pairs)]

    @pl.when(pl.program_id(0) == 0)
    def _():
        for c in loads:
            c.start()

    units, rows = 2 * tt_ref.shape[1], tt_ref.shape[3]
    tok = tok_ref[0]
    q = (dot(tok, wq_ref[...]) + bq_ref[...]).astype(BF16).astype(F32) * SCALE
    q_ref[0] = jnp.transpose(q.astype(BF16))
    tt = jnp.transpose(tok)
    for u in range(units):
        r = u ^ me_ref[0]
        tt_ref[0, r >> 1, r & 1] = tt[u * rows : (u + 1) * rows]

    @pl.when(pl.program_id(0) == pl.num_programs(0) - 1)
    def _():
        for c in loads:
            c.wait()


def query(me, units, tokens, w_qkv, b_qkv, w_in, w_down, w_out):
    seqs, length, width = tokens.shape
    rows = width // units
    return call(
        query_kernel,
        "query",
        [
            (tokens, "h", block((1, length, width), lambda s, me: (s, 0, 0))),
            (w_qkv, "h", block((width, width), lambda s, me: (0, 0))),
            (b_qkv, "h", block((1, width), lambda s, me: (0, 0))),
            (w_in, "h", None),
            (w_down, "h", None),
            (w_out, "h", None),
        ],
        [
            (H(seqs, width, length), block((1, width, length), lambda s, me: (s, 0, 0))),
            (H(seqs, units // 2, 2, rows, length), block((1, units // 2, 2, rows, length), lambda s, me: (s, 0, 0, 0, 0))),
            (V(*w_in.shape), None),
            (V(*w_down.shape), None),
            (V(*w_out.shape), None),
        ],
        grid=(seqs,),
        prefetch=(me,),
        scratch=[pltpu.SemaphoreType.DMA((3,))],
        limit=10,
        flops=2 * seqs * width * length * width,
        nbytes=6 * seqs * length * width,
    )


def flip_kernel(w_ref, b_ref, bin_ref, o_ref, c_ref, cin_ref):
    o_ref[pl.program_id(0)] = jnp.transpose(w_ref[...])

    @pl.when(pl.program_id(0) == 0)
    def _():
        width = w_ref.shape[0]
        c_ref[...] = columns(b_ref[:, width:])
        cin_ref[...] = columns(bin_ref[...])


def flip(w_qkv, b_qkv, b_in):
    width = w_qkv.shape[0]
    ff = b_in.shape[1]
    return call(
        flip_kernel,
        "flip",
        [
            (w_qkv, "h", block((width, width), lambda i: (0, 1 + i))),
            (b_qkv, "h", whole((1, 3 * width))),
            (b_in, "h", whole((1, ff))),
        ],
        [(V(2, width, width), None), (V(2 * width, 1, dtype=F32), None), (V(ff, 1, dtype=F32), None)],
        grid=(2,),
        limit=6,
        nbytes=8 * width * width,
    )


def norm_stats(resid):
    center = resid - jnp.mean(resid, -1, keepdims=True)
    inverse = lax.rsqrt(jnp.mean(center * center, -1, keepdims=True) + EPS)
    return center * inverse, inverse


ROWS = 32
LANES = 128
GROUP = 4
LN_ROWS = 128


def attend_kernel(nt, s, me_ref, *refs):
    t_hbm = refs[:nt]
    wkv_ref, bkv_ref, q_hbm, al_ref, tok_ref, wo_ref, vec_ref = refs[nt : nt + 7]
    tt_ref, c_ref, kv_ref, p_hbm, att_ref, n_ref, inv_ref = refs[nt + 7 : nt + 14]
    t_scr, q_scr, p_scr, res_scr, att_scr, bias_scr, in_sem, out_sem = refs[nt + 14 :]
    width = wo_ref.shape[0]
    length = q_scr.shape[1]
    heads = width // HD
    units, rows = 2 * tt_ref.shape[0], tt_ref.shape[2]
    loads = [pltpu.make_async_copy(t_hbm[k], t_scr.at[k], in_sem.at[k]) for k in range(nt)]
    loads.append(pltpu.make_async_copy(q_hbm.at[s], q_scr, in_sem.at[nt]))
    for c in loads:
        c.start()
    bias_scr[...] = (al_ref[...].astype(F32) - 1.0) * 1e30
    for c in loads[:nt]:
        c.wait()
    total = t_scr[0].astype(F32)
    for k in range(1, nt):
        total = total + t_scr[k].astype(F32)
    low = total.astype(BF16)
    t_low = low[0:KP]
    c_row = low[KP : KP + 8, 0:KP]
    c_ref[...] = c_row
    wide_c = c_row[0:1].astype(F32)
    for k in range(2):
        part = slice(k * width, (k + 1) * width)
        kv_ref[part, :] = (dot(wkv_ref[k], t_low, 1, 1) + bkv_ref[part, :] * wide_c).astype(BF16)
    tt = jnp.transpose(t_low)
    me = me_ref[0]
    for u in range(units):
        r = u ^ me
        tt_ref[r >> 1, r & 1] = tt[u * rows : (u + 1) * rows]
    loads[nt].wait()

    def store(g):
        part = pl.ds(g * GROUP, GROUP)
        return pltpu.make_async_copy(p_scr.at[part], p_hbm.at[part], out_sem.at[g])

    tiles = [(h, j) for h in range(GROUP) for j in range(length // LANES)]

    def heads_of(g, carry):
        keys = {}

        def cut(h, shift=0):
            return pl.ds(pl.multiple_of(shift + (g * GROUP + h) * HD, HD), HD)

        def score(h, j):
            if j == 0:
                keys[h] = jnp.transpose(kv_ref[cut(h), :])
            return dot(keys[h], q_scr[cut(h), j * LANES : (j + 1) * LANES])

        scores = score(*tiles[0])
        for i, (h, j) in enumerate(tiles):
            after = score(*tiles[i + 1]) if i + 1 < len(tiles) else None
            where = slice(j * LANES, (j + 1) * LANES)
            scores = scores + bias_scr[:, where]
            expo = jnp.exp(scores - jnp.max(scores, 0, keepdims=True))
            p_scr[g * GROUP + h, :, where] = (expo * (1.0 / jnp.sum(expo, 0, keepdims=True))).astype(BF16)
            if j == length // LANES - 1:
                att_scr[cut(h), :] = dot(kv_ref[cut(h, width), :], p_scr[g * GROUP + h]).astype(BF16)
            scores = after
        store(g).start()
        return carry

    lax.fori_loop(0, heads // GROUP, heads_of, 0)
    att = att_scr[...]
    res_scr[...] = dot(att, wo_ref[...], 0, 0)
    for u in range(units):
        r = u ^ me
        att_ref[r >> 1, r & 1] = att_scr[u * rows : (u + 1) * rows, :]

    def tile(i, carry):
        part = pl.ds(pl.multiple_of(i * LN_ROWS, LN_ROWS), LN_ROWS)
        normed, inverse = norm_stats(res_scr[part, :] + tok_ref[0, part, :].astype(F32) + vec_ref[0:1, :])
        n_ref[part, :] = normed
        inv_ref[part, :] = inverse
        return carry

    lax.fori_loop(0, length // LN_ROWS, tile, 0)
    for g in range(heads // GROUP):
        store(g).wait()


def attend(me, s, units, others, wkv_t, bkv_col, q_t, allow, tokens, w_out, vecs):
    seqs, length, width = tokens.shape
    rows = width // units
    heads = width // HD
    nt = len(others)
    return call(
        functools.partial(attend_kernel, nt, s),
        "attend",
        [(t, "n", None) for t in others]
        + [
            (wkv_t, "v", None),
            (bkv_col, "v", None),
            (q_t, "h", None),
            (allow, "h", whole((KP, length))),
            (tokens, "h", block((1, length, width), lambda i, me: (s, 0, 0))),
            (w_out, "v", None),
            (vecs, "h", whole(vecs.shape)),
        ],
        [
            (V(units // 2, 2, rows, KP), None),
            (V(8, KP), None),
            (V(2 * width, KP), None),
            (H(heads, KP, length), ANY),
            (V(units // 2, 2, rows, length), None),
            (V(length, width, dtype=F32), None),
            (V(length, 1, dtype=F32), None),
        ],
        prefetch=(me,),
        scratch=[
            pltpu.VMEM((nt, TE, width), BF16),
            pltpu.VMEM((width, length), BF16),
            pltpu.VMEM((heads, KP, length), BF16),
            pltpu.VMEM((length, width), F32),
            pltpu.VMEM((width, length), BF16),
            pltpu.VMEM((KP, length), F32),
            pltpu.SemaphoreType.DMA((nt + 1,)),
            pltpu.SemaphoreType.DMA((heads,)),
        ],
        limit=12,
        flops=2 * KP * width * 2 * width + 8 * KP * length * width + 2 * length * width * width,
        nbytes=10 * MIB,
    )


def norm_back(upstream, normed, inverse, gain):
    scaled = upstream * gain
    return inverse * (
        scaled
        - jnp.mean(scaled, -1, keepdims=True)
        - normed * jnp.mean(scaled * normed, -1, keepdims=True)
    )


FR = 16


def feed_kernel(
    steps, me_ref, n_ref, inv_ref, vec_ref, win_ref, bin_ref, wdn_ref, cot_ref,
    mt_ref, at_ref, gb_ref, dh_ref, out_ref, gf_ref, gfl_ref, stat_ref,
    low_scr, acc_scr, slope_scr, h0_scr, h1_scr,
):
    step = pl.program_id(0)
    g1_ref, be1_ref, bdn_ref, g2_ref, be2_ref = [vec_ref.at[k : k + 1, :] for k in range(1, 6)]
    me = me_ref[0]
    units, rows = 2 * mt_ref.shape[0], mt_ref.shape[2]
    arows = at_ref.shape[2]
    length, width = n_ref.shape
    half = h0_scr.shape[0]
    per = half // arows

    @pl.when(step == 0)
    def _():
        for r in range(0, length, ROWS):
            part = slice(r, r + ROWS)
            mid = n_ref[part, :] * g1_ref[...] + be1_ref[...]
            low_scr[part, :] = mid.astype(BF16)
            acc_scr[part, :] = mid + bdn_ref[...]
        mt = jnp.transpose(low_scr[...])
        for u in range(units):
            r = u ^ me
            mt_ref[r >> 1, r & 1] = mt[u * rows : (u + 1) * rows]

    def unit(base, i):
        r = (base + i) ^ me
        return r >> 1, r & 1

    @pl.when(step < steps)
    def _():
        base = step * 2 * per

        def gelu(k, h_scr):
            for f in range(0, half, FR):
                at = k * half + f
                hidden = h_scr[f : f + FR, :] + bin_ref[pl.ds(pl.multiple_of(step * 2 * half + at, FR), FR), :]
                phi = 0.5 + 0.5 * lax.erf(hidden * HALF_ROOT)
                bell = jnp.exp(-0.5 * hidden * hidden)
                hi, lo = unit(base, at // arows)
                at_ref[hi, lo, at % arows : at % arows + FR, :] = (hidden * phi).astype(BF16)
                slope_scr[step, at : at + FR, :] = (phi + (hidden * INV_ROOT_TAU) * bell).astype(BF16)

        def cut(k):
            return pl.ds(pl.multiple_of(step * 2 * half + k * half, half), half)

        def second(k):
            activ = jnp.concatenate([at_ref[unit(base, k * per + i)] for i in range(per)], 0)
            acc_scr[...] += dot(activ, wdn_ref[cut(k), :], 0, 0)

        low = low_scr[...]
        h0_scr[...] = dot(win_ref[:, cut(0)], low, 0, 1)
        h1_scr[...] = dot(win_ref[:, cut(1)], low, 0, 1)
        gelu(0, h0_scr)
        second(0)
        gelu(1, h1_scr)
        second(1)

    @pl.when(step == steps - 1)
    def _():
        def tile(i, sums):
            part = pl.ds(pl.multiple_of(i * LN_ROWS, LN_ROWS), LN_ROWS)
            normed, inverse = norm_stats(acc_scr[part, :])
            out_ref[part, :] = (normed * g2_ref[...] + be2_ref[...]).astype(BF16)
            cot = cot_ref[0, part, :].astype(F32)
            second = norm_back(cot, normed, inverse, g2_ref[...])
            low = second.astype(BF16)
            gb_ref[part, :] = low
            acc_scr[part, :] = second
            terms = (cot * normed, cot, low.astype(F32))
            return tuple(a + jnp.sum(t, 0, keepdims=True) for a, t in zip(sums, terms))

        sums = lax.fori_loop(0, length // LN_ROWS, tile, (jnp.zeros((1, width), F32),) * 3)
        for k in range(3):
            stat_ref[k : k + 1, :] = sums[k]

    @pl.when(step >= steps)
    def _():
        back = step - steps
        gb = gb_ref[...]

        def slope(k, h_scr):
            for f in range(0, half, FR):
                at = k * half + f
                dh = (h_scr[f : f + FR, :] * slope_scr[back, at : at + FR, :].astype(F32)).astype(BF16)
                row = pl.ds(pl.multiple_of(back * 2 * half + at, FR), FR)
                dh_ref[row, :] = dh

        def cut(k):
            return pl.ds(pl.multiple_of(back * 2 * half + k * half, half), half)

        def down(k):
            acc_scr[...] += dot(dh_ref[cut(k), :], win_ref[:, cut(k)], 0, 1)

        h0_scr[...] = dot(wdn_ref[cut(0), :], gb, 1, 1)
        h1_scr[...] = dot(wdn_ref[cut(1), :], gb, 1, 1)
        slope(0, h0_scr)
        down(0)
        slope(1, h1_scr)
        down(1)

    @pl.when(step == 2 * steps - 1)
    def _():
        def tile(i, sums):
            part = pl.ds(pl.multiple_of(i * LN_ROWS, LN_ROWS), LN_ROWS)
            up = acc_scr[part, :]
            normed = n_ref[part, :]
            first = norm_back(up, normed, inv_ref[part, :], g1_ref[...])
            low = first.astype(BF16)
            gf_ref[part, :] = first
            gfl_ref[part, :] = low
            terms = (up * normed, up, low.astype(F32))
            return tuple(a + jnp.sum(t, 0, keepdims=True) for a, t in zip(sums, terms))

        sums = lax.fori_loop(0, length // LN_ROWS, tile, (jnp.zeros((1, width), F32),) * 3)
        for k in range(3):
            stat_ref[3 + k : 4 + k, :] = sums[k]
        stat_ref[6:8, :] = jnp.zeros((2, width), F32)


def feed(me, s, units, normed, inverse, vecs, w_in, bin_col, w_down, cot):
    length, width = normed.shape
    ff = w_in.shape[1]
    rows = width // units
    arows = ff // units
    chunk = 768
    steps = ff // chunk
    return call(
        functools.partial(feed_kernel, steps),
        "feed",
        [
            (normed, "v", None),
            (inverse, "v", None),
            (vecs, "h", whole(vecs.shape)),
            (w_in, "v", None),
            (bin_col, "v", None),
            (w_down, "v", None),
            (cot, "h", block((1, length, width), lambda i, me: (s, 0, 0))),
        ],
        [
            (V(units // 2, 2, rows, length), None),
            (V(units // 2, 2, arows, length), None),
            (V(length, width), None),
            (V(ff, length), None),
            (H(length, width), whole((length, width))),
            (H(length, width, dtype=F32), whole((length, width))),
            (V(length, width), None),
            (V(8, width, dtype=F32), None),
        ],
        grid=(2 * steps,),
        prefetch=(me,),
        scratch=[
            pltpu.VMEM((length, width), BF16),
            pltpu.VMEM((length, width), F32),
            pltpu.VMEM((steps, chunk, length), BF16),
            pltpu.VMEM((chunk // 2, length), F32),
            pltpu.VMEM((chunk // 2, length), F32),
        ],
        limit=18,
        flops=8 * length * width * ff,
        nbytes=24 * MIB,
    )


def attend_back_kernel(s, gfl_ref, wo_ref, kv_ref, p_hbm, q_hbm, c_ref, wkv_ref, bkv_ref, dq_ref, gs_ref, gt_ref, col_ref, da_scr, p_scr, q_scr, ds0_scr, ds1_scr, sem):
    width = wo_ref.shape[0]
    length = gfl_ref.shape[0]
    heads = width // HD
    def load(g):
        part = pl.ds(g * GROUP, GROUP)
        return pltpu.make_async_copy(p_hbm.at[part], p_scr.at[part], sem.at[g])

    q_load = pltpu.make_async_copy(q_hbm.at[s], q_scr, sem.at[heads])
    q_load.start()
    for g in range(heads // GROUP):
        load(g).start()
    da_scr[...] = dot(wo_ref[...], gfl_ref[...], 1, 1).astype(BF16)
    q_load.wait()
    c_wide = c_ref[0:1, :].astype(F32)
    tiles = [(h, j) for h in range(GROUP) for j in range(length // LANES)]

    def heads_of(g, carry):
        load(g).wait()
        vals = {}

        def cut(h, shift=0):
            return pl.ds(pl.multiple_of(shift + (g * GROUP + h) * HD, HD), HD)

        def first(h, j):
            if j == 0:
                vals[h] = jnp.transpose(kv_ref[cut(h, width), :])
            return dot(vals[h], da_scr[cut(h), j * LANES : (j + 1) * LANES])

        grad = first(*tiles[0])
        for i, (h, j) in enumerate(tiles):
            after = first(*tiles[i + 1]) if i + 1 < len(tiles) else None
            where = slice(j * LANES, (j + 1) * LANES)
            ds_scr = (ds0_scr, ds1_scr)[h % 2]
            wide = p_scr[g * GROUP + h, :, where].astype(F32)
            prod = wide * grad
            ds_scr[:, where] = (prod - wide * jnp.sum(prod, 0, keepdims=True)).astype(BF16)
            if j == length // LANES - 1:
                gv = dot(da_scr[cut(h), :], p_scr[g * GROUP + h], 1, 1).astype(BF16)
                gs_ref[cut(h, width), :] = gv
                col_ref[cut(h, 2 * width), :] = jnp.sum(gv.astype(F32) * c_wide, 1, keepdims=True)
                dq = (dot(kv_ref[cut(h), :], ds_scr[...]) * SCALE).astype(BF16)
                dq_ref[cut(h), :] = dq
                col_ref[cut(h), :] = jnp.sum(dq.astype(F32), 1, keepdims=True)
                gk = dot(q_scr[cut(h), :], ds_scr[...], 1, 1).astype(BF16)
                gs_ref[cut(h), :] = gk
                col_ref[cut(h, width), :] = jnp.sum(gk.astype(F32) * c_wide, 1, keepdims=True)
            grad = after
        return carry

    lax.fori_loop(0, heads // GROUP, heads_of, 0)
    gt = dot(gs_ref[0:width, :], wkv_ref[0], 0, 0) + dot(gs_ref[width:, :], wkv_ref[1], 0, 0)
    gt_ref[0:KP, :] = gt.astype(BF16)
    pad = TE - KP
    b_hi = bkv_ref[...].astype(BF16)
    b_lo = (bkv_ref[...] - b_hi.astype(F32)).astype(BF16)
    gs = gs_ref[...]
    drow = dot(jnp.broadcast_to(b_hi, (pad, 2 * width)), gs) + dot(jnp.broadcast_to(b_lo, (pad, 2 * width)), gs)
    gt_ref[KP:TE, :] = jnp.concatenate([drow.astype(BF16), jnp.zeros((pad, width - KP), BF16)], 1)


def attend_back(s, gfl, w_out, kv_t, probs, q_t, c_row, wkv_t, bkv_row):
    length, width = gfl.shape
    heads = width // HD
    return call(
        functools.partial(attend_back_kernel, s),
        "attend_back",
        [
            (gfl, "v", None),
            (w_out, "v", None),
            (kv_t, "v", None),
            (probs, "h", None),
            (q_t, "h", None),
            (c_row, "v", None),
            (wkv_t, "v", None),
            (bkv_row, "h", whole((1, 2 * width))),
        ],
        [(V(width, length), None), (V(2 * width, KP), None), (H(TE, width), whole((TE, width))), (V(3 * width, 1, dtype=F32), None)],
        scratch=[
            pltpu.VMEM((width, length), BF16),
            pltpu.VMEM((heads, KP, length), BF16),
            pltpu.VMEM((width, length), BF16),
            pltpu.VMEM((KP, length), BF16),
            pltpu.VMEM((KP, length), BF16),
            pltpu.SemaphoreType.DMA((heads + 1,)),
        ],
        limit=11,
        flops=(2 * KP * width * 2 * width + 16 * KP * length * width + 2 * length * width * width) // 1024,
        nbytes=1024,
    )


def token_kernel(gf_refs, dq_refs, wq_ref, o_ref):
    for k, (g, d) in enumerate(zip(gf_refs, dq_refs)):
        o_ref[k] = g[...] + dot(d[...], wq_ref[...], 0, 1)


def token_grad(gf, dq_t, w_qkv):
    seqs = len(gf)
    length, width = gf[0].shape
    shape = (seqs, length, width)
    return call(
        lambda *refs: token_kernel(refs[:seqs], refs[seqs : 2 * seqs], *refs[2 * seqs :]),
        "token_grad",
        [(g, "h", whole((length, width))) for g in gf]
        + [(d, "v", None) for d in dq_t]
        + [(w_qkv, "h", block((width, width), lambda i: (0, 0)))],
        (H(*shape, dtype=F32), whole(shape)),
        limit=16,
        flops=seqs * length * width * width // 1024,
        nbytes=1024,
    )


def last_kernel(nt, *refs):
    t_refs = refs[:nt]
    part_ref, wt_ref, al_ref, tok_ref, o_ref, gp_ref, d_scr = refs[nt:]
    s = pl.program_id(0)
    total = t_refs[0][0].astype(F32)
    for r in t_refs[1:]:
        total = total + r[0].astype(F32)
    low = total[0:KP].astype(BF16)
    d_col = columns(total[KP : KP + 1, 0:KP])
    o_ref[0] = part_ref[0] + dot(wt_ref[0], low, 0, 0)
    term = (dot(low, tok_ref[0], 1, 1) + d_col) * al_ref[0].astype(F32)

    @pl.when(s == 0)
    def _():
        d_scr[...] = term

    @pl.when(s > 0)
    def _():
        d_scr[...] = d_scr[...] + term

    @pl.when(s == pl.num_programs(0) - 1)
    def _():
        gp_ref[...] = d_scr[...].astype(BF16)


def last(tparts, parts, weights, allows, tokens):
    seqs, length, width = tokens.shape
    each = lambda *shape: block((1, *shape), lambda s: (s,) + (0,) * len(shape))
    return call(
        functools.partial(last_kernel, len(tparts)),
        "last",
        [(t, "n", each(TE, width)) for t in tparts]
        + [(parts, "h", each(length, width)), (weights, "h", each(KP, length)), (allows, "h", each(KP, length)), (tokens, "h", each(length, width))],
        [(H(seqs, length, width, dtype=F32), each(length, width)), (H(KP, length), whole((KP, length)))],
        grid=(seqs,),
        scratch=[pltpu.VMEM((KP, length), F32)],
        limit=18,
        flops=4 * seqs * length * width * KP,
        nbytes=8 * MIB,
    )


def split_store(low, send_ref, keep_ref, send_bit, where):
    n = low.shape[0]
    if send_bit == 0:
        for i in range(n):
            (send_ref if i & 1 else keep_ref)[i // 2, :, where] = low[i]
    else:
        half = n // 2
        keep_ref[:, :, where] = low[:half]
        send_ref[:, :, where] = low[half:]


def total(terms):
    out = terms[0]
    for t in terms[1:]:
        out = out + t
    return out


def down_kernel(seqs, core, chunk, send_bit, *refs):
    at_refs = refs[:seqs]
    gb_refs = refs[seqs : 2 * seqs]
    rest = refs[2 * seqs :]
    n, _, arows, length = at_refs[0].shape
    cols = pl.ds(pl.multiple_of(pl.program_id(0) * chunk, chunk), chunk)
    res = total([dot(a[:, core].reshape(n * arows, length), g[:, cols]) for a, g in zip(at_refs, gb_refs)])
    res = res.reshape(n, arows, chunk)
    if send_bit is None:
        rest[0][...] = res.astype(BF16)
    else:
        recv_ref, send_ref, keep_ref = rest
        low = (res + recv_ref[...].astype(F32)).astype(BF16)
        split_store(low, send_ref, keep_ref, send_bit, slice(None))


def down_grad(at, gb, core, recv=None, send_bit=None):
    seqs = len(at)
    n, _, arows, length = at[0].shape
    width = gb[0].shape[1]
    chunk = 256
    args = [(a, "v", None) for a in at] + [(g, "v", None) for g in gb]
    spec = block((n, arows, chunk), lambda i: (0, 0, i))
    if recv is None:
        outs = (H(n, arows, width), spec)
    else:
        args.append((recv, "n", spec))
        outs = [(H(n // 2, arows, width), block((n // 2, arows, chunk), lambda i: (0, 0, i)))] * 2
    return call(
        functools.partial(down_kernel, seqs, core, chunk, send_bit),
        "down_grad",
        args,
        outs,
        grid=(width // chunk,),
        limit=12,
        flops=2 * seqs * n * arows * length * width,
        nbytes=3 * MIB,
    )


def in_kernel(seqs, core, chunk, send_bit, *refs):
    mt_refs = refs[:seqs]
    dh_refs = refs[seqs : 2 * seqs]
    rest = refs[2 * seqs :]
    n, _, rows, length = mt_refs[0].shape
    part = pl.ds(pl.multiple_of(pl.program_id(0) * chunk, chunk), chunk)
    lefts = [a[:, core].reshape(n * rows, length) for a in mt_refs]
    if send_bit is None:
        lefts = [jnp.concatenate([a, jnp.ones((16, length), BF16)], 0) for a in lefts]
    res = total([dot(a, g[part, :], 1, 1) for a, g in zip(lefts, dh_refs)])
    if send_bit is None:
        out_ref, bias_ref = rest
        out_ref[...] = res[0 : n * rows].reshape(n, rows, chunk).astype(BF16)
        bias_ref[...] = res[n * rows : n * rows + 8]
    else:
        res = res.reshape(n, rows, chunk)
        recv_ref, send_ref, keep_ref = rest
        low = (res + recv_ref[...].astype(F32)).astype(BF16)
        split_store(low, send_ref, keep_ref, send_bit, slice(None))


def in_grad(mt, dh, core, recv=None, send_bit=None):
    seqs = len(mt)
    n, _, rows, length = mt[0].shape
    ff = dh[0].shape[0]
    chunk = 1536
    args = [(a, "v", None) for a in mt] + [(g, "v", None) for g in dh]
    spec = block((n, rows, chunk), lambda i: (0, 0, i))
    if recv is None:
        outs = [(H(n, rows, ff), spec), (H(8, ff, dtype=F32), block((8, chunk), lambda i: (0, i)))]
    else:
        args.append((recv, "n", spec))
        outs = [(H(n // 2, rows, ff), block((n // 2, rows, chunk), lambda i: (0, 0, i)))] * 2
    return call(
        functools.partial(in_kernel, seqs, core, chunk, send_bit),
        "in_grad",
        args,
        outs,
        grid=(ff // chunk,),
        limit=12,
        flops=2 * seqs * n * rows * length * ff,
        nbytes=3 * MIB,
    )


def pack_stats(stat_refs, bias_refs, col_refs, scr, bias_scr, group):
    rows = scr.shape[0]
    scr[...] = jnp.zeros_like(scr)
    stat = total([r[...] for r in stat_refs])
    scr[:, 0:8] = jnp.transpose(stat)
    bias_scr[...] = jnp.transpose(total([r[...] for r in bias_refs]))[:, 0:1]
    lane = 8
    for refs in (col_refs, [bias_scr]):
        per = refs[0].shape[0] // rows
        for b in range(rows // group):
            for c in range(per):
                src = slice((b * per + c) * group, (b * per + c + 1) * group)
                scr[b * group : (b + 1) * group, lane + c : lane + c + 1] = total([r[src, :] for r in refs])
        lane += per


def rest_kernel(seqs, group, me_ref, *refs):
    at_refs, gf_refs, tk_refs, dq_refs, tt_refs, gs_refs = [refs[k * seqs : (k + 1) * seqs] for k in range(6)]
    rest = refs[6 * seqs :]
    keep_ref, send_ref, st_scr, bias_scr = rest[-4:]
    n, _, rows, _ = at_refs[0].shape
    width = gf_refs[0].shape[1]

    def put(res, where):
        res = res.reshape(n, 2, rows, res.shape[-1]).astype(BF16)
        keep_ref[:, :, where] = res[:, 0]
        send_ref[:, :, where] = res[:, 1]

    def flat(ref):
        return ref[...].reshape(2 * n * rows, ref.shape[-1])

    if group:
        pack_stats(rest[:seqs], [rest[seqs]], rest[seqs + 1 : 2 * seqs + 1], st_scr, bias_scr, group)
        for u in range(2 * n):
            low = st_scr[pl.ds(pl.multiple_of((u ^ me_ref[0]) * rows, rows), rows), :].astype(BF16)
            (keep_ref, send_ref)[u % 2][u // 2, :, 4 * width : 4 * width + 128] = low
    else:
        for ref in (keep_ref, send_ref):
            ref[:, :, 4 * width : 4 * width + 128] = jnp.zeros((n, rows, 128), BF16)
    put(total([dot(flat(a), g[...]) for a, g in zip(at_refs, gf_refs)]), slice(0, width))
    put(total([dot(flat(a), g[...], 1, 1) for a, g in zip(tk_refs, dq_refs)]), slice(width, 2 * width))
    for k in range(2):
        part = slice(k * width, (k + 1) * width)
        put(total([dot(flat(a), g[part, :], 1, 1) for a, g in zip(tt_refs, gs_refs)]), slice((2 + k) * width, (3 + k) * width))


def rest_grad(me, att, gfl, tok_t, dq_t, t_t, gs_t, group, stats):
    seqs = len(att)
    n, _, rows, length = att[0].shape
    width = gfl[0].shape[1]
    cols = 4 * width + 128
    args = [(a, "v", None) for a in (*att, *gfl)]
    args += [(t, "h", block((pl.Squeezed(), n, 2, rows, length), lambda i, me, k=k: (k, 0, 0, 0, 0))) for k, t in enumerate([tok_t] * seqs)]
    args += [(a, "v", None) for a in (*dq_t, *t_t, *gs_t)]
    args += [(a, "v", None) for a in stats[0]] + [(stats[1], "h", whole(stats[1].shape))] + [(a, "v", None) for a in stats[2]]
    return call(
        functools.partial(rest_kernel, seqs, group),
        "rest_grad",
        args,
        [(H(n, rows, cols), whole((n, rows, cols)))] * 2,
        prefetch=(me,),
        scratch=[pltpu.VMEM((2 * n * rows, 128), F32), pltpu.VMEM((stats[1].shape[1], 1), F32)],
        limit=16,
        flops=seqs * 2 * n * rows * (4 * length * width + 4 * KP * width) // 1024,
        nbytes=1024,
    )


def halve_kernel(z_ref, ka_ref, ra_ref, kb_ref, rb_ref, send_ref, keep_ref):
    z = z_ref[0]
    cut = ka_ref.shape[-1]
    for k in range(2):
        for keep, recv, cols in ((ka_ref, ra_ref, slice(0, cut)), (kb_ref, rb_ref, slice(cut, None))):
            for where, out in ((1 - z, send_ref), (z, keep_ref)):
                out[k, :, cols] = (keep[k, where].astype(F32) + recv[k, where].astype(F32)).astype(BF16)


def halve_rest(z, ka, ra, kb, rb):
    group = ka.shape[0] // 4
    arrays = [x.reshape(2, 2, group, x.shape[-1]) for x in (ka, ra, kb, rb)]
    cols = ka.shape[-1] + kb.shape[-1]
    shape = (2, group, cols)
    return call(
        halve_kernel,
        "halve_rest",
        [(x, "n", whole(x.shape)) for x in arrays],
        [(H(*shape), whole(shape)), (H(*shape), whole(shape))],
        prefetch=(z,),
        limit=6,
        nbytes=2 * MIB,
    )


def finish_kernel(z_ref, keep_ref, recv_ref, qkv_ref, out_ref, small_ref):
    width = out_ref.shape[1]
    res = keep_ref[...].astype(F32) + recv_ref[...].astype(F32)
    out_ref[...] = res[:, 0:width]
    qkv_ref[...] = res[:, width : 4 * width]
    small_ref[...] = jnp.transpose(res[:, 4 * width :])[0:16]


def finish_rest(z, keep, recv):
    group, cols = keep.shape
    width = (cols - 128) // 4
    return call(
        finish_kernel,
        "finish_rest",
        [(keep, "n", whole((group, cols))), (recv, "n", whole((group, cols)))],
        [
            (H(group, 3 * width, dtype=F32), whole((group, 3 * width))),
            (H(group, width, dtype=F32), whole((group, width))),
            (H(16, group, dtype=F32), whole((16, group))),
        ],
        prefetch=(z,),
        limit=5,
        nbytes=MIB,
    )


def add(a, b):
    return (a.astype(F32) + b.astype(F32)).astype(BF16)


def body(n_dp, n_seq, tokens, segment_ids, mask, w_qkv, b_qkv, w_out, b_out, ln1_gain, ln1_bias, w_in, b_in, w_down, b_down, ln2_gain, ln2_bias, proj_e, cotangent):
    seqs, length, width = tokens.shape
    ff = w_in.shape[1]
    n_all = n_dp * n_seq
    fast = n_dp == 8 and n_seq == 4 and length >= 512
    units = 8
    dp = lax.axis_index("dp").astype(jnp.int32)
    sq = lax.axis_index("seq").astype(jnp.int32)
    me = (dp if fast else jnp.zeros((), jnp.int32)).reshape(1)
    row = lambda v: v.reshape(1, -1)

    def swap(x, bit):
        pairs = [(i, i ^ bit) for i in range(n_all)]
        return lax.ppermute(x, ("dp", "seq"), pairs)

    near = [(i, i ^ 1) for i in range(n_seq)]
    mid = [(1, 2), (2, 1)]

    def hop_one(own):
        return lax.ppermute(own, "seq", near), lax.ppermute(own, "seq", mid)

    def hop_two(first):
        return lax.ppermute(first[1], "seq", near), lax.ppermute(first[0], "seq", mid)

    def tie(x, *deps):
        return lax.optimization_barrier((x, *deps))[0]

    vecs = jnp.stack([b_out, ln1_gain, ln1_bias, b_down, ln2_gain, ln2_bias])
    first = prep(0, tokens, segment_ids, mask, proj_e)
    prepped = [first] + [prep(s, tie(tokens, first[0]), segment_ids, mask, proj_e) for s in range(1, seqs)]
    owns = [p[0] for p in prepped]
    wkv_t, bkv_col, bin_col = flip(tie(w_qkv, vecs, *owns), row(b_qkv), row(b_in))
    if fast:
        one = tuple(tie(x, wkv_t) for x in hop_one(owns[0]))
        q_t, tok_t, w_in, w_down, w_out = query(me, units, tie(tokens, wkv_t, *one), w_qkv, row(b_qkv), w_in, w_down, w_out)
        tparts = [[owns[0], *one, *(tie(x, q_t) for x in hop_two(one))]]
    else:
        q_t, tok_t, w_in, w_down, w_out = query(me, units, tie(tokens, wkv_t), w_qkv, row(b_qkv), w_in, w_down, w_out)
        tparts = [[lax.psum(o, "seq")] for o in owns]

    tt, crow, kv, probs, att, normed, inverse = [], [], [], [], [], [], []
    mt, at, gb, dh, outs, gf, gfl, stat = [], [], [], [], [], [], [], []
    for s in range(seqs):
        if s:
            tparts[s][0] = tie(tparts[s][0], gfl[s - 1])
        if fast and s + 1 < seqs:
            own = tie(owns[s + 1], q_t, *tparts[s])
            one = hop_one(own)
        res = attend(me, s, units, tparts[s], wkv_t, bkv_col, q_t, prepped[s][1], tokens, w_out, vecs)
        for store, value in zip((tt, crow, kv, probs, att, normed, inverse), res):
            store.append(value)
        if fast and s + 1 < seqs:
            normed[s] = tie(normed[s], *one)
            tparts.append([own, *one, *hop_two(one)])
        res = feed(me, s, units, normed[s], inverse[s], vecs, w_in, bin_col, w_down, cotangent)
        for store, value in zip((mt, at, gb, dh, outs, gf, gfl, stat), res):
            store.append(value)

    X_BIT, Y_BIT, CORE = 2 * n_seq, 4 * n_seq, n_seq
    z0, z1 = sq & 1, sq >> 1

    def halve(recv, keep):
        return add(keep[1], recv[1]), add(keep[0], recv[0])

    def halve_z0(recv, keep):
        group = keep.shape[0] // 4
        shape = (2, 2, group, keep.shape[-1])
        pick = lambda a, z: lax.dynamic_index_in_dim(a, z, 1, keepdims=False)
        keep, recv = keep.reshape(shape), recv.reshape(shape)
        return add(pick(keep, 1 - z0), pick(recv, 1 - z0)), add(pick(keep, z0), pick(recv, z0))

    def halve_z1(recv, keep):
        pick = lambda a, z: lax.dynamic_index_in_dim(a, z, 0, keepdims=False)
        return add(pick(keep, 1 - z1), pick(recv, 1 - z1)), add(pick(keep, z1), pick(recv, z1))

    back_in = list(gfl)
    if fast:
        send1 = down_grad(at, gb, 1)
        recv1 = swap(send1, CORE)
        send2, gbin = in_grad([tie(mt[0], send1), *mt[1:]], dh, 1)
        recv2 = swap(send2, CORE)
        sx1, kx1 = down_grad([tie(at[0], send2), *at[1:]], gb, 0, recv1, 0)
        rx1 = swap(sx1, X_BIT)
        sx2, kx2 = in_grad([tie(mt[0], sx1), *mt[1:]], dh, 0, recv2, 1)
        rx2 = swap(sx2, Y_BIT)
        back_in[0] = tie(gfl[0], sx2)

    back = []
    for s in range(seqs):
        if s:
            back_in[s] = tie(back_in[s], back[s - 1][2])
        back.append(attend_back(s, back_in[s], w_out, kv[s], probs[s], q_t, crow[s], wkv_t, row(b_qkv[width:])))
    dq_t = [b[0] for b in back]
    gs_t = [b[1] for b in back]
    gouts = [b[2] for b in back]
    if not fast:
        half2, gbin = in_grad(mt, dh, 1)
    stats = (stat, gbin, [b[3] for b in back])

    gsum = jnp.stack(gouts)
    if fast:
        group = width // n_all
        gone = hop_one(gsum)
        parts = token_grad(gf, [tie(dq_t[0], gouts[-1]), *dq_t[1:]], w_qkv)
        sy1, ky1 = halve(tie(rx1, parts), kx1)
        ry1 = swap(sy1, Y_BIT)
        sy2, ky2 = halve(tie(rx2, parts), kx2)
        ry2 = swap(sy2, X_BIT)
        keep3, send3 = rest_grad(me, [tie(att[0], sy1, sy2, parts, gsum), *att[1:]], gfl, tok_t, dq_t, tt, gs_t, group, stats)
        recv3 = swap(send3, CORE)
        half, cut = units // 4, 2 * width
        pair = lambda a: a.reshape(half, 2, width // units, a.shape[-1])
        k3, r3 = pair(keep3), pair(recv3)
        sx3, kx3 = add(k3[:, 1, :, :cut], r3[:, 1, :, :cut]), add(k3[:, 0, :, :cut], r3[:, 0, :, :cut])
        sy3, ky3 = add(k3[1, :, :, cut:], r3[1, :, :, cut:]), add(k3[0, :, :, cut:], r3[0, :, :, cut:])
        rx3 = swap(sx3, X_BIT)
        ry3 = swap(sy3, Y_BIT)
        gone = [tie(g, sx3, sy3, ry1, ry2) for g in gone]
        gtwo = hop_two(gone)
        sxy, kxy = halve(tie(rx3, *gtwo), kx3)
        rxy = swap(sxy, Y_BIT)
        syx, kyx = halve(tie(ry3, *gtwo), ky3)
        ryx = swap(syx, X_BIT)
        sz1, kz1 = halve_z0(tie(ry1, sxy, syx), ky1)
        rz1 = swap(sz1, 1)
        sz2, kz2 = halve_z0(tie(ry2, sxy, syx), ky2)
        rz2 = swap(sz2, 1)
        gparts = [tie(gsum, sz1, sz2), *gone, *gtwo]
    else:
        parts = token_grad(gf, dq_t, w_qkv)
        gparts = [lax.psum(gsum, "seq")]

    grad_tokens, gproj = last(gparts, parts, jnp.stack([p[2] for p in prepped]), jnp.stack([p[1] for p in prepped]), tokens)
    layer_out = jnp.stack([tie(outs[0], sx3), *outs[1:]] if fast else outs)

    if not fast:
        g3 = jnp.stack(rest_grad(me, att, gfl, tok_t, dq_t, tt, gs_t, 0, stats), 1).reshape(width, -1)
        g2 = jnp.stack([in_grad(mt, dh, 0)[0], half2], 1).reshape(width, -1)
        g1 = jnp.stack([down_grad(at, gb, c) for c in (0, 1)], 1).reshape(ff, width)
        st = total(stat)
        st_in, st_qkv = gbin[0], total(stats[2]).reshape(-1)
        grads = (g3[:, width : 4 * width], st_qkv, g3[:, :width], st[5], st[3], st[4], g2, st_in, g1, st[2], st[0], st[1])
        grads = lax.psum_scatter(tuple(g.astype(F32) for g in grads), ("dp", "seq"), scatter_dimension=0, tiled=True)
        gproj = lax.psum(gproj, "dp").astype(F32)
        return (layer_out, grad_tokens, *grads, gproj)

    gproj = add(gproj, swap(gproj, CORE))
    gall = [gproj] + [swap(gproj, bit) for bit in (X_BIT, Y_BIT, X_BIT | Y_BIT)]
    sw1, kw1 = halve_z1(rz1, kz1)
    rw1 = swap(sw1, 2)
    sw2, kw2 = halve_z1(rz2, kz2)
    rw2 = swap(sw2, 2)
    sz3, kz3 = halve_rest(z0.reshape(1), kxy, rxy, kyx, ryx)
    rz3 = swap(sz3, 1)
    gproj = total([g.astype(F32) for g in gall])
    g1 = kw1.astype(F32) + rw1.astype(F32)
    g2 = kw2.astype(F32) + rw2.astype(F32)
    sw3, kw3 = halve_z1(rz3, kz3)
    rw3 = swap(sw3, 2)
    g_qkv, g_out, small = finish_rest(z1.reshape(1), kw3, rw3)
    g_g2, g_b2, gb_down, g_g1, g_b1, gb_out = [small[k] for k in range(6)]
    gb_qkv = small[8:11].reshape(-1)
    gb_in = small[11:15].reshape(-1)
    return (
        layer_out, grad_tokens, g_qkv, gb_qkv, g_out, gb_out, g_g1, g_b1,
        g2, gb_in, g1, gb_down, g_g2, g_b2, gproj,
    )


def solution(mesh):
    both = ("dp", "seq")
    placed = (
        P("dp", "seq", None),
        P("dp", "seq"),
        P("dp", None, None),
        *([P()] * 12),
        P(None, "seq"),
        P("dp", "seq", None),
    )
    out = (
        P("dp", "seq", None),
        P("dp", "seq", None),
        P(both, None),
        P(both),
        P(both, None),
        P(both),
        P(both),
        P(both),
        P(both, None),
        P(both),
        P(both, None),
        P(both),
        P(both),
        P(both),
        P(None, "seq"),
    )
    run = functools.partial(body, mesh.shape["dp"], mesh.shape["seq"])
    return jax.shard_map(run, mesh=mesh, in_specs=placed, out_specs=out, check_vma=False)
```

```python
import functools

import jax
import jax.numpy as jnp
from jax import lax
from jax.experimental import pallas as pl
from jax.experimental.pallas import tpu as pltpu
from jax.sharding import PartitionSpec as P

HD = 64
KP = 256
NSEG = 4
TE = 272
EPS = 1e-05
SCALE = 0.125
HALF_ROOT = 0.7071067811865476
INV_ROOT_TAU = 0.3989422804014327
F32 = jnp.float32
BF16 = jnp.bfloat16
MIB = 2**20
VM = pl.BlockSpec(memory_space=pltpu.VMEM)
ANY = pl.BlockSpec(memory_space=pl.ANY)


def dot(left, right, cl=1, cr=0):
    return lax.dot_general(left, right, (((cl,), (cr,)), ((), ())), preferred_element_type=F32)


def in_vmem(x):
    return pltpu.with_memory_space_constraint(x, pltpu.VMEM)


def in_hbm(x):
    return pltpu.with_memory_space_constraint(x, pltpu.HBM)


def V(*shape, dtype=BF16):
    return pltpu.VMEM(shape, dtype)


def H(*shape, dtype=BF16):
    return pltpu.HBM(shape, dtype)


def call(kernel, name, args, outs, grid=(1,), in_specs=None, out_specs=None, scratch=(), limit=24, flops=0, nbytes=0, prefetch=()):
    placed = [{"v": in_vmem, "h": in_hbm, "n": lambda x: x}[where](x) for x, where, _ in args]
    default = {"v": VM, "h": ANY, "n": ANY}
    specs = [default[where] if spec is None else spec for _, where, spec in args]
    single = not isinstance(outs, list)
    if single:
        outs = [outs]
    shapes = [o for o, _ in outs]
    ospecs = [spec if spec is not None else VM for o, spec in outs]
    res = pl.pallas_call(
        kernel,
        tuple(shapes),
        grid_spec=pltpu.PrefetchScalarGridSpec(
            num_scalar_prefetch=len(prefetch),
            grid=grid,
            in_specs=specs,
            out_specs=tuple(ospecs),
            scratch_shapes=list(scratch),
        ),
        compiler_params=pltpu.CompilerParams(vmem_limit_bytes=limit * MIB),
        cost_estimate=pl.CostEstimate(flops=int(flops), bytes_accessed=int(nbytes), transcendentals=0),
        name=name,
    )(*prefetch, *placed)
    return res[0] if single else res


def block(shape, index):
    return pl.BlockSpec(shape, index)


def whole(shape):
    return pl.BlockSpec(shape, lambda *_: (0,) * len(shape))


def columns(row):
    return jnp.transpose(jnp.broadcast_to(row, (8, row.shape[-1])))[:, 0:1]


def prep_kernel(s, tok_ref, seg_ref, mask_ref, proj_ref, t_ref, al_ref, wt_ref):
    width = tok_ref.shape[-1]
    length = tok_ref.shape[1]
    m = mask_ref[0]
    owner = jnp.sum(m * lax.broadcasted_iota(jnp.int32, m.shape, 0), 0, keepdims=True).astype(F32)
    allowed = columns(owner) == seg_ref[s : s + 1, :].astype(F32)
    weighted = jnp.where(allowed, proj_ref[...].astype(F32), 0.0).astype(BF16)
    al_ref[...] = jnp.where(allowed, 1.0, 0.0).astype(BF16)
    wt_ref[...] = weighted
    t_ref[0:KP, :] = dot(weighted, tok_ref[0]).astype(BF16)
    count = dot(jnp.ones((TE - KP, length), BF16), weighted, 1, 1).astype(BF16)
    t_ref[KP:TE, :] = jnp.concatenate([count, jnp.zeros((TE - KP, width - KP), BF16)], 1)


def prep(s, tokens, segment_ids, mask, proj_e):
    seqs, length, width = tokens.shape
    return call(
        functools.partial(prep_kernel, s),
        "prep",
        [
            (tokens, "h", block((1, length, width), lambda i: (s, 0, 0))),
            (segment_ids, "h", whole((seqs, length))),
            (mask, "h", block((1, NSEG, KP), lambda i: (s, 0, 0))),
            (proj_e, "h", whole((KP, length))),
        ],
        [(H(TE, width), whole((TE, width))), (H(KP, length), whole((KP, length))), (H(KP, length), whole((KP, length)))],
        limit=5,
        flops=2 * KP * length * width,
        nbytes=2 * length * width,
    )


def query_kernel(me_ref, tok_ref, wq_ref, bq_ref, win_hbm, wdn_hbm, wo_hbm, q_ref, tt_ref, win_ref, wdn_ref, wo_ref, sem):
    pairs = ((wo_hbm, wo_ref), (win_hbm, win_ref), (wdn_hbm, wdn_ref))
    loads = [pltpu.make_async_copy(a, b, sem.at[k]) for k, (a, b) in enumerate(pairs)]

    @pl.when(pl.program_id(0) == 0)
    def _():
        for c in loads:
            c.start()

    units, rows = 2 * tt_ref.shape[1], tt_ref.shape[3]
    tok = tok_ref[0]
    q = (dot(tok, wq_ref[...]) + bq_ref[...]).astype(BF16).astype(F32) * SCALE
    q_ref[0] = jnp.transpose(q.astype(BF16))
    tt = jnp.transpose(tok)
    for u in range(units):
        r = u ^ me_ref[0]
        tt_ref[0, r >> 1, r & 1] = tt[u * rows : (u + 1) * rows]

    @pl.when(pl.program_id(0) == pl.num_programs(0) - 1)
    def _():
        for c in loads:
            c.wait()


def query(me, units, tokens, w_qkv, b_qkv, w_in, w_down, w_out):
    seqs, length, width = tokens.shape
    rows = width // units
    return call(
        query_kernel,
        "query",
        [
            (tokens, "h", block((1, length, width), lambda s, me: (s, 0, 0))),
            (w_qkv, "h", block((width, width), lambda s, me: (0, 0))),
            (b_qkv, "h", block((1, width), lambda s, me: (0, 0))),
            (w_in, "h", None),
            (w_down, "h", None),
            (w_out, "h", None),
        ],
        [
            (H(seqs, width, length), block((1, width, length), lambda s, me: (s, 0, 0))),
            (H(seqs, units // 2, 2, rows, length), block((1, units // 2, 2, rows, length), lambda s, me: (s, 0, 0, 0, 0))),
            (V(*w_in.shape), None),
            (V(*w_down.shape), None),
            (V(*w_out.shape), None),
        ],
        grid=(seqs,),
        prefetch=(me,),
        scratch=[pltpu.SemaphoreType.DMA((3,))],
        limit=10,
        flops=2 * seqs * width * length * width,
        nbytes=6 * seqs * length * width,
    )


def flip_kernel(w_ref, b_ref, bin_ref, o_ref, c_ref, cin_ref):
    o_ref[pl.program_id(0)] = jnp.transpose(w_ref[...])

    @pl.when(pl.program_id(0) == 0)
    def _():
        width = w_ref.shape[0]
        c_ref[...] = columns(b_ref[:, width:])
        cin_ref[...] = columns(bin_ref[...])


def flip(w_qkv, b_qkv, b_in):
    width = w_qkv.shape[0]
    ff = b_in.shape[1]
    return call(
        flip_kernel,
        "flip",
        [
            (w_qkv, "h", block((width, width), lambda i: (0, 1 + i))),
            (b_qkv, "h", whole((1, 3 * width))),
            (b_in, "h", whole((1, ff))),
        ],
        [(V(2, width, width), None), (V(2 * width, 1, dtype=F32), None), (V(ff, 1, dtype=F32), None)],
        grid=(2,),
        limit=6,
        nbytes=8 * width * width,
    )


def norm_stats(resid):
    center = resid - jnp.mean(resid, -1, keepdims=True)
    inverse = lax.rsqrt(jnp.mean(center * center, -1, keepdims=True) + EPS)
    return center * inverse, inverse


ROWS = 32
LANES = 128
GROUP = 4
LN_ROWS = 128
SMALL = (1, 1, 1, 1, 1, 1, 1, 1, 3, 4)


def attend_kernel(nt, s, me_ref, *refs):
    t_hbm = refs[:nt]
    wkv_ref, bkv_ref, q_hbm, al_ref, tok_ref, wo_ref, vec_ref = refs[nt : nt + 7]
    tt_ref, c_ref, kv_ref, p_hbm, att_ref, n_ref, inv_ref = refs[nt + 7 : nt + 14]
    t_scr, q_scr, p_scr, res_scr, att_scr, bias_scr, in_sem, out_sem = refs[nt + 14 :]
    width = wo_ref.shape[0]
    length = q_scr.shape[1]
    heads = width // HD
    units, rows = 2 * tt_ref.shape[0], tt_ref.shape[2]
    loads = [pltpu.make_async_copy(t_hbm[k], t_scr.at[k], in_sem.at[k]) for k in range(nt)]
    loads.append(pltpu.make_async_copy(q_hbm.at[s], q_scr, in_sem.at[nt]))
    for c in loads:
        c.start()
    bias_scr[...] = (al_ref[...].astype(F32) - 1.0) * 1e30
    for c in loads[:nt]:
        c.wait()
    total = t_scr[0].astype(F32)
    for k in range(1, nt):
        total = total + t_scr[k].astype(F32)
    low = total.astype(BF16)
    t_low = low[0:KP]
    c_row = low[KP : KP + 8, 0:KP]
    c_ref[...] = c_row
    wide_c = c_row[0:1].astype(F32)
    for k in range(2):
        part = slice(k * width, (k + 1) * width)
        kv_ref[part, :] = (dot(wkv_ref[k], t_low, 1, 1) + bkv_ref[part, :] * wide_c).astype(BF16)
    tt = jnp.transpose(t_low)
    me = me_ref[0]
    for u in range(units):
        r = u ^ me
        tt_ref[r >> 1, r & 1] = tt[u * rows : (u + 1) * rows]
    loads[nt].wait()

    def store(g):
        part = pl.ds(g * GROUP, GROUP)
        return pltpu.make_async_copy(p_scr.at[part], p_hbm.at[part], out_sem.at[g])

    tiles = [(h, j) for h in range(GROUP) for j in range(length // LANES)]

    def heads_of(g, carry):
        keys = {}

        def cut(h, shift=0):
            return pl.ds(pl.multiple_of(shift + (g * GROUP + h) * HD, HD), HD)

        def score(h, j):
            if j == 0:
                keys[h] = jnp.transpose(kv_ref[cut(h), :])
            return dot(keys[h], q_scr[cut(h), j * LANES : (j + 1) * LANES])

        scores = score(*tiles[0])
        for i, (h, j) in enumerate(tiles):
            after = score(*tiles[i + 1]) if i + 1 < len(tiles) else None
            where = slice(j * LANES, (j + 1) * LANES)
            scores = scores + bias_scr[:, where]
            expo = jnp.exp(scores - jnp.max(scores, 0, keepdims=True))
            p_scr[g * GROUP + h, :, where] = (expo * (1.0 / jnp.sum(expo, 0, keepdims=True))).astype(BF16)
            if j == length // LANES - 1:
                att_scr[cut(h), :] = dot(kv_ref[cut(h, width), :], p_scr[g * GROUP + h]).astype(BF16)
            scores = after
        store(g).start()
        return carry

    lax.fori_loop(0, heads // GROUP, heads_of, 0)
    att = att_scr[...]
    res_scr[...] = dot(att, wo_ref[...], 0, 0)
    for u in range(units):
        r = u ^ me
        att_ref[r >> 1, r & 1] = att_scr[u * rows : (u + 1) * rows, :]

    def tile(i, carry):
        part = pl.ds(pl.multiple_of(i * LN_ROWS, LN_ROWS), LN_ROWS)
        normed, inverse = norm_stats(res_scr[part, :] + tok_ref[0, part, :].astype(F32) + vec_ref[0:1, :])
        n_ref[part, :] = normed
        inv_ref[part, :] = inverse
        return carry

    lax.fori_loop(0, length // LN_ROWS, tile, 0)
    for g in range(heads // GROUP):
        store(g).wait()


def attend(me, s, units, others, wkv_t, bkv_col, q_t, allow, tokens, w_out, vecs):
    seqs, length, width = tokens.shape
    rows = width // units
    heads = width // HD
    nt = len(others)
    return call(
        functools.partial(attend_kernel, nt, s),
        "attend",
        [(t, "n", None) for t in others]
        + [
            (wkv_t, "v", None),
            (bkv_col, "v", None),
            (q_t, "h", None),
            (allow, "h", whole((KP, length))),
            (tokens, "h", block((1, length, width), lambda i, me: (s, 0, 0))),
            (w_out, "v", None),
            (vecs, "h", whole(vecs.shape)),
        ],
        [
            (V(units // 2, 2, rows, KP), None),
            (V(8, KP), None),
            (V(2 * width, KP), None),
            (H(heads, KP, length), ANY),
            (V(units // 2, 2, rows, length), None),
            (V(length, width, dtype=F32), None),
            (V(length, 1, dtype=F32), None),
        ],
        prefetch=(me,),
        scratch=[
            pltpu.VMEM((nt, TE, width), BF16),
            pltpu.VMEM((width, length), BF16),
            pltpu.VMEM((heads, KP, length), BF16),
            pltpu.VMEM((length, width), F32),
            pltpu.VMEM((width, length), BF16),
            pltpu.VMEM((KP, length), F32),
            pltpu.SemaphoreType.DMA((nt + 1,)),
            pltpu.SemaphoreType.DMA((heads,)),
        ],
        limit=12,
        flops=2 * KP * width * 2 * width + 8 * KP * length * width + 2 * length * width * width,
        nbytes=10 * MIB,
    )


def norm_back(upstream, normed, inverse, gain):
    scaled = upstream * gain
    return inverse * (
        scaled
        - jnp.mean(scaled, -1, keepdims=True)
        - normed * jnp.mean(scaled * normed, -1, keepdims=True)
    )


FR = 16


def feed_kernel(
    steps, me_ref, n_ref, inv_ref, vec_ref, win_ref, bin_ref, wdn_ref, cot_ref,
    mt_ref, at_ref, gb_ref, dh_ref, out_ref, gf_ref, gfl_ref, stat_ref,
    low_scr, acc_scr, slope_scr, h0_scr, h1_scr,
):
    step = pl.program_id(0)
    g1_ref, be1_ref, bdn_ref, g2_ref, be2_ref = [vec_ref.at[k : k + 1, :] for k in range(1, 6)]
    me = me_ref[0]
    units, rows = 2 * mt_ref.shape[0], mt_ref.shape[2]
    arows = at_ref.shape[2]
    length, width = n_ref.shape
    half = h0_scr.shape[0]
    per = half // arows

    @pl.when(step == 0)
    def _():
        for r in range(0, length, ROWS):
            part = slice(r, r + ROWS)
            mid = n_ref[part, :] * g1_ref[...] + be1_ref[...]
            low_scr[part, :] = mid.astype(BF16)
            acc_scr[part, :] = mid + bdn_ref[...]
        mt = jnp.transpose(low_scr[...])
        for u in range(units):
            r = u ^ me
            mt_ref[r >> 1, r & 1] = mt[u * rows : (u + 1) * rows]

    def unit(base, i):
        r = (base + i) ^ me
        return r >> 1, r & 1

    @pl.when(step < steps)
    def _():
        base = step * 2 * per

        def gelu(k, h_scr):
            for f in range(0, half, FR):
                at = k * half + f
                hidden = h_scr[f : f + FR, :] + bin_ref[pl.ds(pl.multiple_of(step * 2 * half + at, FR), FR), :]
                phi = 0.5 + 0.5 * lax.erf(hidden * HALF_ROOT)
                bell = jnp.exp(-0.5 * hidden * hidden)
                hi, lo = unit(base, at // arows)
                at_ref[hi, lo, at % arows : at % arows + FR, :] = (hidden * phi).astype(BF16)
                slope_scr[step, at : at + FR, :] = (phi + (hidden * INV_ROOT_TAU) * bell).astype(BF16)

        def cut(k):
            return pl.ds(pl.multiple_of(step * 2 * half + k * half, half), half)

        def second(k):
            activ = jnp.concatenate([at_ref[unit(base, k * per + i)] for i in range(per)], 0)
            acc_scr[...] += dot(activ, wdn_ref[cut(k), :], 0, 0)

        low = low_scr[...]
        h0_scr[...] = dot(win_ref[:, cut(0)], low, 0, 1)
        h1_scr[...] = dot(win_ref[:, cut(1)], low, 0, 1)
        gelu(0, h0_scr)
        second(0)
        gelu(1, h1_scr)
        second(1)

    @pl.when(step == steps - 1)
    def _():
        def tile(i, sums):
            part = pl.ds(pl.multiple_of(i * LN_ROWS, LN_ROWS), LN_ROWS)
            normed, inverse = norm_stats(acc_scr[part, :])
            out_ref[part, :] = (normed * g2_ref[...] + be2_ref[...]).astype(BF16)
            cot = cot_ref[0, part, :].astype(F32)
            second = norm_back(cot, normed, inverse, g2_ref[...])
            low = second.astype(BF16)
            gb_ref[part, :] = low
            acc_scr[part, :] = second
            terms = (cot * normed, cot, low.astype(F32))
            return tuple(a + jnp.sum(t, 0, keepdims=True) for a, t in zip(sums, terms))

        sums = lax.fori_loop(0, length // LN_ROWS, tile, (jnp.zeros((1, width), F32),) * 3)
        for k in range(3):
            stat_ref[k : k + 1, :] = sums[k]

    @pl.when(step >= steps)
    def _():
        back = step - steps
        gb = gb_ref[...]

        def slope(k, h_scr):
            for f in range(0, half, FR):
                at = k * half + f
                dh = (h_scr[f : f + FR, :] * slope_scr[back, at : at + FR, :].astype(F32)).astype(BF16)
                row = pl.ds(pl.multiple_of(back * 2 * half + at, FR), FR)
                dh_ref[row, :] = dh

        def cut(k):
            return pl.ds(pl.multiple_of(back * 2 * half + k * half, half), half)

        def down(k):
            acc_scr[...] += dot(dh_ref[cut(k), :], win_ref[:, cut(k)], 0, 1)

        h0_scr[...] = dot(wdn_ref[cut(0), :], gb, 1, 1)
        h1_scr[...] = dot(wdn_ref[cut(1), :], gb, 1, 1)
        slope(0, h0_scr)
        down(0)
        slope(1, h1_scr)
        down(1)

    @pl.when(step == 2 * steps - 1)
    def _():
        def tile(i, sums):
            part = pl.ds(pl.multiple_of(i * LN_ROWS, LN_ROWS), LN_ROWS)
            up = acc_scr[part, :]
            normed = n_ref[part, :]
            first = norm_back(up, normed, inv_ref[part, :], g1_ref[...])
            low = first.astype(BF16)
            gf_ref[part, :] = first
            gfl_ref[part, :] = low
            terms = (up * normed, up, low.astype(F32))
            return tuple(a + jnp.sum(t, 0, keepdims=True) for a, t in zip(sums, terms))

        sums = lax.fori_loop(0, length // LN_ROWS, tile, (jnp.zeros((1, width), F32),) * 3)
        for k in range(3):
            stat_ref[3 + k : 4 + k, :] = sums[k]
        stat_ref[6:8, :] = jnp.zeros((2, width), F32)


def feed(me, s, units, normed, inverse, vecs, w_in, bin_col, w_down, cot):
    length, width = normed.shape
    ff = w_in.shape[1]
    rows = width // units
    arows = ff // units
    chunk = 768
    steps = ff // chunk
    return call(
        functools.partial(feed_kernel, steps),
        "feed",
        [
            (normed, "v", None),
            (inverse, "v", None),
            (vecs, "h", whole(vecs.shape)),
            (w_in, "v", None),
            (bin_col, "v", None),
            (w_down, "v", None),
            (cot, "h", block((1, length, width), lambda i, me: (s, 0, 0))),
        ],
        [
            (V(units // 2, 2, rows, length), None),
            (V(units // 2, 2, arows, length), None),
            (V(length, width), None),
            (V(ff, length), None),
            (H(length, width), whole((length, width))),
            (H(length, width, dtype=F32), whole((length, width))),
            (H(length, width), whole((length, width))),
            (V(8, width, dtype=F32), None),
        ],
        grid=(2 * steps,),
        prefetch=(me,),
        scratch=[
            pltpu.VMEM((length, width), BF16),
            pltpu.VMEM((length, width), F32),
            pltpu.VMEM((steps, chunk, length), BF16),
            pltpu.VMEM((chunk // 2, length), F32),
            pltpu.VMEM((chunk // 2, length), F32),
        ],
        limit=18,
        flops=8 * length * width * ff,
        nbytes=24 * MIB,
    )


def attend_back_kernel(seqs, *refs):
    gfl_hbm, kv_hbm, p_hbm, c_refs = [refs[k * seqs : (k + 1) * seqs] for k in range(4)]
    wo_ref, q_hbm, wkv_ref, bkv_ref, dq_ref, gs_ref, gt_ref, col_ref = refs[4 * seqs : 4 * seqs + 8]
    gfl_scr, kv_scr, p_scr, q_scr, c_scr, da_scr, ds0_scr, ds1_scr, sem, p_sem = refs[4 * seqs + 8 :]
    s = pl.program_id(0)
    width = wo_ref.shape[0]
    length = gfl_scr.shape[1]
    heads = width // HD
    groups = heads // GROUP

    def inputs(k):
        pairs = ((gfl_hbm[k], gfl_scr.at[k]), (q_hbm.at[k], q_scr.at[k]), (kv_hbm[k], kv_scr.at[k]))
        return [pltpu.make_async_copy(x, y, sem.at[k, i]) for i, (x, y) in enumerate(pairs)]

    def load(k, g):
        part = pl.ds(g * GROUP, GROUP)
        return pltpu.make_async_copy(p_hbm[k].at[part], p_scr.at[k, part], p_sem.at[k, g])

    @pl.when(s == 0)
    def _():
        for k in range(seqs):
            for c in inputs(k):
                c.start()
            for g in range(groups):
                load(k, g).start()

    for k in range(seqs):

        @pl.when(s == k)
        def _(k=k):
            c_scr[...] = c_refs[k][...]
            for c in inputs(k):
                c.wait()
            for g in range(groups):
                load(k, g).wait()

    da_scr[...] = dot(wo_ref[...], gfl_scr[s], 1, 1).astype(BF16)
    c_wide = c_scr[0:1, :].astype(F32)
    tiles = [(h, j) for h in range(GROUP) for j in range(length // LANES)]

    def heads_of(g, carry):
        vals = {}

        def cut(h, shift=0):
            return pl.ds(pl.multiple_of(shift + (g * GROUP + h) * HD, HD), HD)

        def first(h, j):
            if j == 0:
                vals[h] = jnp.transpose(kv_scr[s, cut(h, width), :])
            return dot(vals[h], da_scr[cut(h), j * LANES : (j + 1) * LANES])

        grad = first(*tiles[0])
        for i, (h, j) in enumerate(tiles):
            after = first(*tiles[i + 1]) if i + 1 < len(tiles) else None
            where = slice(j * LANES, (j + 1) * LANES)
            ds_scr = (ds0_scr, ds1_scr)[h % 2]
            wide = p_scr[s, g * GROUP + h, :, where].astype(F32)
            prod = wide * grad
            ds_scr[:, where] = (prod - wide * jnp.sum(prod, 0, keepdims=True)).astype(BF16)
            if j == length // LANES - 1:
                gv = dot(da_scr[cut(h), :], p_scr[s, g * GROUP + h], 1, 1).astype(BF16)
                gs_ref[s, cut(h, width), :] = gv
                col_ref[s, cut(h, 2 * width), :] = jnp.sum(gv.astype(F32) * c_wide, 1, keepdims=True)
                dq = (dot(kv_scr[s, cut(h), :], ds_scr[...]) * SCALE).astype(BF16)
                dq_ref[s, cut(h), :] = dq
                col_ref[s, cut(h), :] = jnp.sum(dq.astype(F32), 1, keepdims=True)
                gk = dot(q_scr[s, cut(h), :], ds_scr[...], 1, 1).astype(BF16)
                gs_ref[s, cut(h), :] = gk
                col_ref[s, cut(h, width), :] = jnp.sum(gk.astype(F32) * c_wide, 1, keepdims=True)
            grad = after
        return carry

    lax.fori_loop(0, groups, heads_of, 0)
    gs = gs_ref[s]
    gt = dot(gs[0:width], wkv_ref[0], 0, 0) + dot(gs[width:], wkv_ref[1], 0, 0)
    gt_ref[0, 0:KP, :] = gt.astype(BF16)
    pad = TE - KP
    b_hi = bkv_ref[...].astype(BF16)
    b_lo = (bkv_ref[...] - b_hi.astype(F32)).astype(BF16)
    drow = dot(jnp.broadcast_to(b_hi, (pad, 2 * width)), gs) + dot(jnp.broadcast_to(b_lo, (pad, 2 * width)), gs)
    gt_ref[0, KP:TE, :] = jnp.concatenate([drow.astype(BF16), jnp.zeros((pad, width - KP), BF16)], 1)


def attend_back(gfl, w_out, kv_t, probs, q_t, c_row, wkv_t, bkv_row):
    seqs = len(gfl)
    length, width = gfl[0].shape
    heads = width // HD
    return call(
        functools.partial(attend_back_kernel, seqs),
        "attend_back",
        [(x, "n", None) for x in (*gfl, *kv_t, *probs)]
        + [(c, "v", None) for c in c_row]
        + [
            (w_out, "v", None),
            (q_t, "h", None),
            (wkv_t, "v", None),
            (bkv_row, "h", whole((1, 2 * width))),
        ],
        [
            (V(seqs, width, length), None),
            (V(seqs, 2 * width, KP), None),
            (H(seqs, TE, width), block((1, TE, width), lambda s: (s, 0, 0))),
            (V(seqs, 3 * width, 1, dtype=F32), None),
        ],
        grid=(seqs,),
        scratch=[
            pltpu.VMEM((seqs, length, width), BF16),
            pltpu.VMEM((seqs, 2 * width, KP), BF16),
            pltpu.VMEM((seqs, heads, KP, length), BF16),
            pltpu.VMEM((seqs, width, length), BF16),
            pltpu.VMEM((8, KP), BF16),
            pltpu.VMEM((width, length), BF16),
            pltpu.VMEM((KP, length), BF16),
            pltpu.VMEM((KP, length), BF16),
            pltpu.SemaphoreType.DMA((seqs, 3)),
            pltpu.SemaphoreType.DMA((seqs, heads // GROUP)),
        ],
        limit=22,
        flops=(2 * KP * width * 2 * width + 16 * KP * length * width + 2 * length * width * width) // 1024,
        nbytes=1024,
    )


def token_kernel(gf_refs, dq_ref, wq_ref, o_ref):
    for k, g in enumerate(gf_refs):
        o_ref[k] = g[...] + dot(dq_ref[k], wq_ref[...], 0, 1)


def token_grad(gf, dq_t, w_qkv):
    seqs = len(gf)
    length, width = gf[0].shape
    shape = (seqs, length, width)
    return call(
        lambda *refs: token_kernel(refs[:seqs], *refs[seqs:]),
        "token_grad",
        [(g, "h", whole((length, width))) for g in gf]
        + [(dq_t, "v", None), (w_qkv, "h", block((width, width), lambda i: (0, 0)))],
        (H(*shape, dtype=F32), whole(shape)),
        limit=16,
        flops=seqs * length * width * width // 1024,
        nbytes=1024,
    )


def last_kernel(nt, *refs):
    t_refs = refs[:nt]
    part_ref, wt_ref, al_ref, tok_ref, o_ref, gp_ref, d_scr = refs[nt:]
    s = pl.program_id(0)
    total = t_refs[0][0].astype(F32)
    for r in t_refs[1:]:
        total = total + r[0].astype(F32)
    low = total[0:KP].astype(BF16)
    d_col = columns(total[KP : KP + 1, 0:KP])
    o_ref[0] = part_ref[0] + dot(wt_ref[0], low, 0, 0)
    term = (dot(low, tok_ref[0], 1, 1) + d_col) * al_ref[0].astype(F32)

    @pl.when(s == 0)
    def _():
        d_scr[...] = term

    @pl.when(s > 0)
    def _():
        d_scr[...] = d_scr[...] + term

    @pl.when(s == pl.num_programs(0) - 1)
    def _():
        gp_ref[...] = d_scr[...].astype(BF16)


def last(tparts, parts, weights, allows, tokens):
    seqs, length, width = tokens.shape
    each = lambda *shape: block((1, *shape), lambda s: (s,) + (0,) * len(shape))
    return call(
        functools.partial(last_kernel, len(tparts)),
        "last",
        [(t, "n", each(TE, width)) for t in tparts]
        + [(parts, "h", each(length, width)), (weights, "h", each(KP, length)), (allows, "h", each(KP, length)), (tokens, "h", each(length, width))],
        [(H(seqs, length, width, dtype=F32), each(length, width)), (H(KP, length), whole((KP, length)))],
        grid=(seqs,),
        scratch=[pltpu.VMEM((KP, length), F32)],
        limit=18,
        flops=4 * seqs * length * width * KP,
        nbytes=8 * MIB,
    )


def split_store(low, send_ref, keep_ref, send_bit, where):
    n = low.shape[0]
    if send_bit == 0:
        for i in range(n):
            (send_ref if i & 1 else keep_ref)[i // 2, :, where] = low[i]
    else:
        half = n // 2
        keep_ref[:, :, where] = low[:half]
        send_ref[:, :, where] = low[half:]


def total(terms):
    out = terms[0]
    for t in terms[1:]:
        out = out + t
    return out


def down_kernel(seqs, core, chunk, send_bit, *refs):
    at_refs = refs[:seqs]
    gb_refs = refs[seqs : 2 * seqs]
    rest = refs[2 * seqs :]
    n, _, arows, length = at_refs[0].shape
    cols = pl.ds(pl.multiple_of(pl.program_id(0) * chunk, chunk), chunk)
    res = total([dot(a[:, core].reshape(n * arows, length), g[:, cols]) for a, g in zip(at_refs, gb_refs)])
    res = res.reshape(n, arows, chunk)
    if send_bit is None:
        rest[0][...] = res.astype(BF16)
    else:
        recv_ref, send_ref, keep_ref = rest
        low = (res + recv_ref[...].astype(F32)).astype(BF16)
        split_store(low, send_ref, keep_ref, send_bit, slice(None))


def down_grad(at, gb, core, recv=None, send_bit=None):
    seqs = len(at)
    n, _, arows, length = at[0].shape
    width = gb[0].shape[1]
    chunk = 256
    args = [(a, "v", None) for a in at] + [(g, "v", None) for g in gb]
    spec = block((n, arows, chunk), lambda i: (0, 0, i))
    if recv is None:
        outs = (H(n, arows, width), spec)
    else:
        args.append((recv, "n", spec))
        outs = [(H(n // 2, arows, width), block((n // 2, arows, chunk), lambda i: (0, 0, i)))] * 2
    return call(
        functools.partial(down_kernel, seqs, core, chunk, send_bit),
        "down_grad",
        args,
        outs,
        grid=(width // chunk,),
        limit=12,
        flops=2 * seqs * n * arows * length * width,
        nbytes=3 * MIB,
    )


def in_kernel(seqs, core, chunk, send_bit, *refs):
    mt_refs = refs[:seqs]
    dh_refs = refs[seqs : 2 * seqs]
    rest = refs[2 * seqs :]
    n, _, rows, length = mt_refs[0].shape
    part = pl.ds(pl.multiple_of(pl.program_id(0) * chunk, chunk), chunk)
    lefts = [a[:, core].reshape(n * rows, length) for a in mt_refs]
    if send_bit is None:
        lefts = [jnp.concatenate([a, jnp.ones((16, length), BF16)], 0) for a in lefts]
    res = total([dot(a, g[part, :], 1, 1) for a, g in zip(lefts, dh_refs)])
    if send_bit is None:
        out_ref, bias_ref = rest
        out_ref[...] = res[0 : n * rows].reshape(n, rows, chunk).astype(BF16)
        bias_ref[...] = res[n * rows : n * rows + 8]
    else:
        res = res.reshape(n, rows, chunk)
        recv_ref, send_ref, keep_ref = rest
        low = (res + recv_ref[...].astype(F32)).astype(BF16)
        split_store(low, send_ref, keep_ref, send_bit, slice(None))


def in_grad(mt, dh, core, recv=None, send_bit=None):
    seqs = len(mt)
    n, _, rows, length = mt[0].shape
    ff = dh[0].shape[0]
    chunk = 1536
    args = [(a, "v", None) for a in mt] + [(g, "v", None) for g in dh]
    spec = block((n, rows, chunk), lambda i: (0, 0, i))
    if recv is None:
        outs = [(H(n, rows, ff), spec), (H(8, ff, dtype=F32), block((8, chunk), lambda i: (0, i)))]
    else:
        args.append((recv, "n", spec))
        outs = [(H(n // 2, rows, ff), block((n // 2, rows, chunk), lambda i: (0, 0, i)))] * 2
    return call(
        functools.partial(in_kernel, seqs, core, chunk, send_bit),
        "in_grad",
        args,
        outs,
        grid=(ff // chunk,),
        limit=12,
        flops=2 * seqs * n * rows * length * ff,
        nbytes=3 * MIB,
    )


def pack_stats(stat_refs, bias_refs, col_refs, scr, bias_scr, group):
    rows = scr.shape[0]
    scr[...] = jnp.zeros_like(scr)
    stat = total([r[...] for r in stat_refs])
    scr[:, 0:8] = jnp.transpose(stat)
    bias_scr[...] = jnp.transpose(total([r[...] for r in bias_refs]))[:, 0:1]
    lane = 8
    for refs in (col_refs, [bias_scr]):
        per = refs[0].shape[0] // rows
        for b in range(rows // group):
            for c in range(per):
                src = slice((b * per + c) * group, (b * per + c + 1) * group)
                scr[b * group : (b + 1) * group, lane + c : lane + c + 1] = total([r[src, :] for r in refs])
        lane += per


def rest_kernel(seqs, group, me_ref, *refs):
    at_refs, gf_refs, tk_refs, tt_refs = [refs[k * seqs : (k + 1) * seqs] for k in range(4)]
    dq_refs, gs_refs = [[refs[4 * seqs + k].at[i] for i in range(seqs)] for k in range(2)]
    rest = refs[4 * seqs + 2 :]
    keep_ref, send_ref, st_scr, bias_scr = rest[-4:]
    n, _, rows, _ = at_refs[0].shape
    width = gf_refs[0].shape[1]

    def put(res, where):
        res = res.reshape(n, 2, rows, res.shape[-1]).astype(BF16)
        keep_ref[:, :, where] = res[:, 0]
        send_ref[:, :, where] = res[:, 1]

    def flat(ref):
        return ref[...].reshape(2 * n * rows, ref.shape[-1])

    if group:
        pack_stats(rest[:seqs], [rest[seqs]], [rest[seqs + 1].at[k] for k in range(seqs)], st_scr, bias_scr, group)
        for u in range(2 * n):
            low = st_scr[pl.ds(pl.multiple_of((u ^ me_ref[0]) * rows, rows), rows), :].astype(BF16)
            (keep_ref, send_ref)[u % 2][u // 2, :, 4 * width : 4 * width + 128] = low
    else:
        for ref in (keep_ref, send_ref):
            ref[:, :, 4 * width : 4 * width + 128] = jnp.zeros((n, rows, 128), BF16)
    put(total([dot(flat(a), g[...]) for a, g in zip(at_refs, gf_refs)]), slice(0, width))
    put(total([dot(flat(a), g[...], 1, 1) for a, g in zip(tk_refs, dq_refs)]), slice(width, 2 * width))
    for k in range(2):
        part = slice(k * width, (k + 1) * width)
        put(total([dot(flat(a), g[part, :], 1, 1) for a, g in zip(tt_refs, gs_refs)]), slice((2 + k) * width, (3 + k) * width))


def rest_grad(me, att, gfl, tok_t, dq_t, t_t, gs_t, group, stats):
    seqs = len(att)
    n, _, rows, length = att[0].shape
    width = gfl[0].shape[1]
    cols = 4 * width + 128
    args = [(a, "v", None) for a in att] + [(g, "h", whole((length, width))) for g in gfl]
    args += [(t, "h", block((pl.Squeezed(), n, 2, rows, length), lambda i, me, k=k: (k, 0, 0, 0, 0))) for k, t in enumerate([tok_t] * seqs)]
    args += [(a, "v", None) for a in (*t_t, dq_t, gs_t)]
    args += [(a, "v", None) for a in stats[0]] + [(stats[1], "h", whole(stats[1].shape)), (stats[2], "v", None)]
    return call(
        functools.partial(rest_kernel, seqs, group),
        "rest_grad",
        args,
        [(H(n, rows, cols), whole((n, rows, cols)))] * 2,
        prefetch=(me,),
        scratch=[pltpu.VMEM((2 * n * rows, 128), F32), pltpu.VMEM((stats[1].shape[1], 1), F32)],
        limit=16,
        flops=seqs * 2 * n * rows * (4 * length * width + 4 * KP * width) // 1024,
        nbytes=1024,
    )


def halve_kernel(z_ref, ka_ref, ra_ref, kb_ref, rb_ref, send_ref, keep_ref):
    z = z_ref[0]
    cut = ka_ref.shape[-1]
    for k in range(2):
        for keep, recv, cols in ((ka_ref, ra_ref, slice(0, cut)), (kb_ref, rb_ref, slice(cut, None))):
            for where, out in ((1 - z, send_ref), (z, keep_ref)):
                out[k, :, cols] = (keep[k, where].astype(F32) + recv[k, where].astype(F32)).astype(BF16)


def halve_rest(z, ka, ra, kb, rb):
    group = ka.shape[0] // 4
    arrays = [x.reshape(2, 2, group, x.shape[-1]) for x in (ka, ra, kb, rb)]
    cols = ka.shape[-1] + kb.shape[-1]
    shape = (2, group, cols)
    return call(
        halve_kernel,
        "halve_rest",
        [(x, "n", whole(x.shape)) for x in arrays],
        [(H(*shape), whole(shape)), (H(*shape), whole(shape))],
        prefetch=(z,),
        limit=6,
        nbytes=2 * MIB,
    )


def finish_kernel(z_ref, keep_ref, recv_ref, qkv_ref, out_ref, *small_refs):
    width = out_ref.shape[1]
    res = keep_ref[...].astype(F32) + recv_ref[...].astype(F32)
    out_ref[...] = res[:, 0:width]
    qkv_ref[...] = res[:, width : 4 * width]
    small = jnp.transpose(res[:, 4 * width :])
    lane = 0
    for ref, per in zip(small_refs, SMALL):
        parts = [small[lane + k : lane + k + 1, :] for k in range(per)]
        ref[...] = (jnp.concatenate(parts, 1) if per > 1 else parts[0]).reshape(ref.shape)
        lane += per


def finish_rest(z, keep, recv):
    group, cols = keep.shape
    width = (cols - 128) // 4
    return call(
        finish_kernel,
        "finish_rest",
        [(keep, "n", whole((group, cols))), (recv, "n", whole((group, cols)))],
        [
            (H(group, 3 * width, dtype=F32), whole((group, 3 * width))),
            (H(group, width, dtype=F32), whole((group, width))),
            *[(H(per * group, dtype=F32), whole((per * group,))) for per in SMALL],
        ],
        prefetch=(z,),
        limit=5,
        nbytes=MIB,
    )


def add(a, b):
    return (a.astype(F32) + b.astype(F32)).astype(BF16)


def body(n_dp, n_seq, tokens, segment_ids, mask, w_qkv, b_qkv, w_out, b_out, ln1_gain, ln1_bias, w_in, b_in, w_down, b_down, ln2_gain, ln2_bias, proj_e, cotangent):
    seqs, length, width = tokens.shape
    ff = w_in.shape[1]
    n_all = n_dp * n_seq
    fast = n_dp == 8 and n_seq == 4 and length >= 512
    units = 8
    dp = lax.axis_index("dp").astype(jnp.int32)
    sq = lax.axis_index("seq").astype(jnp.int32)
    me = (dp if fast else jnp.zeros((), jnp.int32)).reshape(1)
    row = lambda v: v.reshape(1, -1)

    def swap(x, bit):
        pairs = [(i, i ^ bit) for i in range(n_all)]
        return lax.ppermute(x, ("dp", "seq"), pairs)

    near = [(i, i ^ 1) for i in range(n_seq)]
    mid = [(1, 2), (2, 1)]

    def hop_one(own):
        return lax.ppermute(own, "seq", near), lax.ppermute(own, "seq", mid)

    def hop_two(first):
        return lax.ppermute(first[1], "seq", near), lax.ppermute(first[0], "seq", mid)

    def tie(x, *deps):
        return lax.optimization_barrier((x, *deps))[0]

    vecs = jnp.stack([b_out, ln1_gain, ln1_bias, b_down, ln2_gain, ln2_bias])
    first = prep(0, tokens, segment_ids, mask, proj_e)
    prepped = [first] + [prep(s, tie(tokens, first[0]), segment_ids, mask, proj_e) for s in range(1, seqs)]
    owns = [p[0] for p in prepped]
    wkv_t, bkv_col, bin_col = flip(tie(w_qkv, vecs, *owns), row(b_qkv), row(b_in))
    if fast:
        one = tuple(tie(x, wkv_t) for x in hop_one(owns[0]))
        q_t, tok_t, w_in, w_down, w_out = query(me, units, tie(tokens, wkv_t, *one), w_qkv, row(b_qkv), w_in, w_down, w_out)
        tparts = [[owns[0], *one, *(tie(x, q_t) for x in hop_two(one))]]
    else:
        q_t, tok_t, w_in, w_down, w_out = query(me, units, tie(tokens, wkv_t), w_qkv, row(b_qkv), w_in, w_down, w_out)
        tparts = [[lax.psum(o, "seq")] for o in owns]

    tt, crow, kv, probs, att, normed, inverse = [], [], [], [], [], [], []
    mt, at, gb, dh, outs, gf, gfl, stat = [], [], [], [], [], [], [], []
    for s in range(seqs):
        if s:
            tparts[s][0] = tie(tparts[s][0], gfl[s - 1])
        if fast and s + 1 < seqs:
            own = tie(owns[s + 1], q_t)
            one = hop_one(own)
        res = attend(me, s, units, tparts[s], wkv_t, bkv_col, q_t, prepped[s][1], tokens, w_out, vecs)
        for store, value in zip((tt, crow, kv, probs, att, normed, inverse), res):
            store.append(value)
        if fast and s + 1 < seqs:
            normed[s] = tie(normed[s], *one)
            tparts.append([own, *one, *hop_two(one)])
        res = feed(me, s, units, normed[s], inverse[s], vecs, w_in, bin_col, w_down, cotangent)
        for store, value in zip((mt, at, gb, dh, outs, gf, gfl, stat), res):
            store.append(value)

    X_BIT, Y_BIT, CORE = 2 * n_seq, 4 * n_seq, n_seq
    z0, z1 = sq & 1, sq >> 1

    def halve(recv, keep):
        return add(keep[1], recv[1]), add(keep[0], recv[0])

    def halve_z0(recv, keep):
        group = keep.shape[0] // 4
        shape = (2, 2, group, keep.shape[-1])
        pick = lambda a, z: lax.dynamic_index_in_dim(a, z, 1, keepdims=False)
        keep, recv = keep.reshape(shape), recv.reshape(shape)
        return add(pick(keep, 1 - z0), pick(recv, 1 - z0)), add(pick(keep, z0), pick(recv, z0))

    def halve_z1(recv, keep):
        pick = lambda a, z: lax.dynamic_index_in_dim(a, z, 0, keepdims=False)
        return add(pick(keep, 1 - z1), pick(recv, 1 - z1)), add(pick(keep, z1), pick(recv, z1))

    back_in = list(gfl)
    if fast:
        send1 = down_grad(at, gb, 1)
        recv1 = swap(send1, CORE)
        send2, gbin = in_grad([tie(mt[0], send1), *mt[1:]], dh, 1)
        recv2 = swap(send2, CORE)
        sx1, kx1 = down_grad([tie(at[0], send2), *at[1:]], gb, 0, recv1, 0)
        rx1 = swap(sx1, X_BIT)
        sx2, kx2 = in_grad([tie(mt[0], sx1), *mt[1:]], dh, 0, recv2, 1)
        rx2 = swap(sx2, Y_BIT)
        back_in[0] = tie(gfl[0], sx2)

    dq_t, gs_t, gsum, col = attend_back(back_in, w_out, kv, probs, q_t, crow, wkv_t, row(b_qkv[width:]))
    if not fast:
        half2, gbin = in_grad(mt, dh, 1)
    stats = (stat, gbin, col)

    if fast:
        group = width // n_all
        gone = hop_one(gsum)
        parts = token_grad(gf, dq_t, w_qkv)
        sy1, ky1 = halve(tie(rx1, parts), kx1)
        ry1 = swap(sy1, Y_BIT)
        sy2, ky2 = halve(tie(rx2, parts), kx2)
        ry2 = swap(sy2, X_BIT)
        keep3, send3 = rest_grad(me, [tie(att[0], sy1, sy2, parts, gsum), *att[1:]], gfl, tok_t, dq_t, tt, gs_t, group, stats)
        recv3 = swap(tie(send3, ry1, ry2, *gone), CORE)
        half, cut = units // 4, 2 * width
        pair = lambda a: a.reshape(half, 2, width // units, a.shape[-1])
        k3, r3 = pair(keep3), pair(recv3)
        sx3, kx3 = add(k3[:, 1, :, :cut], r3[:, 1, :, :cut]), add(k3[:, 0, :, :cut], r3[:, 0, :, :cut])
        sy3, ky3 = add(k3[1, :, :, cut:], r3[1, :, :, cut:]), add(k3[0, :, :, cut:], r3[0, :, :, cut:])
        rx3 = swap(sx3, X_BIT)
        ry3 = swap(sy3, Y_BIT)
        gtwo = hop_two(gone)
        layer_out = jnp.stack([tie(outs[0], sx3), *outs[1:]])
        sxy, kxy = halve(tie(rx3, layer_out, *gtwo), kx3)
        rxy = swap(sxy, Y_BIT)
        syx, kyx = halve(tie(ry3, *gtwo), ky3)
        ryx = swap(syx, X_BIT)
        sz1, kz1 = halve_z0(tie(ry1, sxy, syx), ky1)
        rz1 = swap(sz1, 1)
        sz2, kz2 = halve_z0(tie(ry2, sxy, syx), ky2)
        rz2 = swap(sz2, 1)
        gparts = [tie(gsum, sz1, sz2), *gone, *gtwo]
    else:
        parts = token_grad(gf, dq_t, w_qkv)
        gparts = [lax.psum(gsum, "seq")]

    grad_tokens, gproj = last(gparts, parts, jnp.stack([p[2] for p in prepped]), jnp.stack([p[1] for p in prepped]), tokens)
    if not fast:
        layer_out = jnp.stack(outs)

    if not fast:
        g3 = jnp.stack(rest_grad(me, att, gfl, tok_t, dq_t, tt, gs_t, 0, stats), 1).reshape(width, -1)
        g2 = jnp.stack([in_grad(mt, dh, 0)[0], half2], 1).reshape(width, -1)
        g1 = jnp.stack([down_grad(at, gb, c) for c in (0, 1)], 1).reshape(ff, width)
        st = total(stat)
        st_in, st_qkv = gbin[0], jnp.sum(col, 0).reshape(-1)
        grads = (g3[:, width : 4 * width], st_qkv, g3[:, :width], st[5], st[3], st[4], g2, st_in, g1, st[2], st[0], st[1])
        grads = lax.psum_scatter(tuple(g.astype(F32) for g in grads), ("dp", "seq"), scatter_dimension=0, tiled=True)
        gproj = lax.psum(gproj, "dp").astype(F32)
        return (layer_out, grad_tokens, *grads, gproj)

    gproj = add(gproj, swap(gproj, CORE))
    sz3, kz3 = halve_rest(z0.reshape(1), kxy, rxy, kyx, ryx)
    rz3 = swap(sz3, 1)
    gproj = add(gproj, swap(gproj, X_BIT))
    gall = [gproj, swap(gproj, Y_BIT)]
    sw1, kw1 = halve_z1(rz1, kz1)
    rw1 = swap(sw1, 2)
    sw2, kw2 = halve_z1(rz2, kz2)
    rw2 = swap(sw2, 2)
    gproj = total([g.astype(F32) for g in gall])
    g1 = kw1.astype(F32) + rw1.astype(F32)
    g2 = kw2.astype(F32) + rw2.astype(F32)
    sw3, kw3 = halve_z1(rz3, kz3)
    rw3 = swap(sw3, 2)
    g_qkv, g_out, *small = finish_rest(z1.reshape(1), kw3, rw3)
    g_g2, g_b2, gb_down, g_g1, g_b1, gb_out, _, _, gb_qkv, gb_in = small
    return (
        layer_out, grad_tokens, g_qkv, gb_qkv, g_out, gb_out, g_g1, g_b1,
        g2, gb_in, g1, gb_down, g_g2, g_b2, gproj,
    )


def solution(mesh):
    both = ("dp", "seq")
    placed = (
        P("dp", "seq", None),
        P("dp", "seq"),
        P("dp", None, None),
        *([P()] * 12),
        P(None, "seq"),
        P("dp", "seq", None),
    )
    out = (
        P("dp", "seq", None),
        P("dp", "seq", None),
        P(both, None),
        P(both),
        P(both, None),
        P(both),
        P(both),
        P(both),
        P(both, None),
        P(both),
        P(both, None),
        P(both),
        P(both),
        P(both),
        P(None, "seq"),
    )
    run = functools.partial(body, mesh.shape["dp"], mesh.shape["seq"])
    return jax.shard_map(run, mesh=mesh, in_specs=placed, out_specs=out, check_vma=False)
```

```python
import functools

import jax
import jax.numpy as jnp
from jax import lax
from jax.experimental import pallas as pl
from jax.experimental.pallas import tpu as pltpu
from jax.sharding import PartitionSpec as P

HD = 64
KP = 256
NSEG = 4
TE = 272
EPS = 1e-05
SCALE = 0.125
HALF_ROOT = 0.7071067811865476
INV_ROOT_TAU = 0.3989422804014327
F32 = jnp.float32
BF16 = jnp.bfloat16
MIB = 2**20
VM = pl.BlockSpec(memory_space=pltpu.VMEM)
ANY = pl.BlockSpec(memory_space=pl.ANY)


def dot(left, right, cl=1, cr=0):
    return lax.dot_general(left, right, (((cl,), (cr,)), ((), ())), preferred_element_type=F32)


def in_vmem(x):
    return pltpu.with_memory_space_constraint(x, pltpu.VMEM)


def in_hbm(x):
    return pltpu.with_memory_space_constraint(x, pltpu.HBM)


def V(*shape, dtype=BF16):
    return pltpu.VMEM(shape, dtype)


def H(*shape, dtype=BF16):
    return pltpu.HBM(shape, dtype)


def call(kernel, name, args, outs, grid=(1,), in_specs=None, out_specs=None, scratch=(), limit=24, flops=0, nbytes=0, prefetch=()):
    placed = [{"v": in_vmem, "h": in_hbm, "n": lambda x: x}[where](x) for x, where, _ in args]
    default = {"v": VM, "h": ANY, "n": ANY}
    specs = [default[where] if spec is None else spec for _, where, spec in args]
    single = not isinstance(outs, list)
    if single:
        outs = [outs]
    shapes = [o for o, _ in outs]
    ospecs = [spec if spec is not None else VM for o, spec in outs]
    res = pl.pallas_call(
        kernel,
        tuple(shapes),
        grid_spec=pltpu.PrefetchScalarGridSpec(
            num_scalar_prefetch=len(prefetch),
            grid=grid,
            in_specs=specs,
            out_specs=tuple(ospecs),
            scratch_shapes=list(scratch),
        ),
        compiler_params=pltpu.CompilerParams(vmem_limit_bytes=limit * MIB),
        cost_estimate=pl.CostEstimate(flops=int(flops), bytes_accessed=int(nbytes), transcendentals=0),
        name=name,
    )(*prefetch, *placed)
    return res[0] if single else res


def block(shape, index):
    return pl.BlockSpec(shape, index)


def whole(shape):
    return pl.BlockSpec(shape, lambda *_: (0,) * len(shape))


def columns(row):
    return jnp.transpose(jnp.broadcast_to(row, (8, row.shape[-1])))[:, 0:1]


def prep_kernel(s, tok_ref, seg_ref, mask_ref, proj_ref, t_ref, al_ref, wt_ref):
    width = tok_ref.shape[-1]
    length = tok_ref.shape[1]
    m = mask_ref[0]
    owner = jnp.sum(m * lax.broadcasted_iota(jnp.int32, m.shape, 0), 0, keepdims=True).astype(F32)
    allowed = columns(owner) == seg_ref[s : s + 1, :].astype(F32)
    weighted = jnp.where(allowed, proj_ref[...].astype(F32), 0.0).astype(BF16)
    al_ref[...] = jnp.where(allowed, 1.0, 0.0).astype(BF16)
    wt_ref[...] = weighted
    t_ref[0:KP, :] = dot(weighted, tok_ref[0]).astype(BF16)
    count = dot(jnp.ones((TE - KP, length), BF16), weighted, 1, 1).astype(BF16)
    t_ref[KP:TE, :] = jnp.concatenate([count, jnp.zeros((TE - KP, width - KP), BF16)], 1)


def prep(s, tokens, segment_ids, mask, proj_e):
    seqs, length, width = tokens.shape
    return call(
        functools.partial(prep_kernel, s),
        "prep",
        [
            (tokens, "h", block((1, length, width), lambda i: (s, 0, 0))),
            (segment_ids, "h", whole((seqs, length))),
            (mask, "h", block((1, NSEG, KP), lambda i: (s, 0, 0))),
            (proj_e, "h", whole((KP, length))),
        ],
        [(H(TE, width), whole((TE, width))), (H(KP, length), whole((KP, length))), (H(KP, length), whole((KP, length)))],
        limit=5,
        flops=2 * KP * length * width,
        nbytes=2 * length * width,
    )


def query_kernel(me_ref, tok_ref, wq_ref, bq_ref, win_hbm, wdn_hbm, wo_hbm, q_ref, tt_ref, win_ref, wdn_ref, wo_ref, sem):
    pairs = ((wo_hbm, wo_ref), (win_hbm, win_ref), (wdn_hbm, wdn_ref))
    loads = [pltpu.make_async_copy(a, b, sem.at[k]) for k, (a, b) in enumerate(pairs)]

    @pl.when(pl.program_id(0) == 0)
    def _():
        for c in loads:
            c.start()

    units, rows = 2 * tt_ref.shape[1], tt_ref.shape[3]
    tok = tok_ref[0]
    q = (dot(tok, wq_ref[...]) + bq_ref[...]).astype(BF16).astype(F32) * SCALE
    q_ref[0] = jnp.transpose(q.astype(BF16))
    tt = jnp.transpose(tok)
    for u in range(units):
        r = u ^ me_ref[0]
        tt_ref[0, r >> 1, r & 1] = tt[u * rows : (u + 1) * rows]

    @pl.when(pl.program_id(0) == pl.num_programs(0) - 1)
    def _():
        for c in loads:
            c.wait()


def query(me, units, tokens, w_qkv, b_qkv, w_in, w_down, w_out):
    seqs, length, width = tokens.shape
    rows = width // units
    return call(
        query_kernel,
        "query",
        [
            (tokens, "h", block((1, length, width), lambda s, me: (s, 0, 0))),
            (w_qkv, "h", block((width, width), lambda s, me: (0, 0))),
            (b_qkv, "h", block((1, width), lambda s, me: (0, 0))),
            (w_in, "h", None),
            (w_down, "h", None),
            (w_out, "h", None),
        ],
        [
            (H(seqs, width, length), block((1, width, length), lambda s, me: (s, 0, 0))),
            (H(seqs, units // 2, 2, rows, length), block((1, units // 2, 2, rows, length), lambda s, me: (s, 0, 0, 0, 0))),
            (V(*w_in.shape), None),
            (V(*w_down.shape), None),
            (V(*w_out.shape), None),
        ],
        grid=(seqs,),
        prefetch=(me,),
        scratch=[pltpu.SemaphoreType.DMA((3,))],
        limit=10,
        flops=2 * seqs * width * length * width,
        nbytes=6 * seqs * length * width,
    )


def flip_kernel(w_ref, b_ref, bin_ref, o_ref, c_ref, cin_ref):
    o_ref[pl.program_id(0)] = jnp.transpose(w_ref[...])

    @pl.when(pl.program_id(0) == 0)
    def _():
        width = w_ref.shape[0]
        c_ref[...] = columns(b_ref[:, width:])
        cin_ref[...] = columns(bin_ref[...])


def flip(w_qkv, b_qkv, b_in):
    width = w_qkv.shape[0]
    ff = b_in.shape[1]
    return call(
        flip_kernel,
        "flip",
        [
            (w_qkv, "h", block((width, width), lambda i: (0, 1 + i))),
            (b_qkv, "h", whole((1, 3 * width))),
            (b_in, "h", whole((1, ff))),
        ],
        [(V(2, width, width), None), (V(2 * width, 1, dtype=F32), None), (V(ff, 1, dtype=F32), None)],
        grid=(2,),
        limit=6,
        nbytes=8 * width * width,
    )


def norm_stats(resid):
    center = resid - jnp.mean(resid, -1, keepdims=True)
    inverse = lax.rsqrt(jnp.mean(center * center, -1, keepdims=True) + EPS)
    return center * inverse, inverse


ROWS = 32
LANES = 128
GROUP = 4
LN_ROWS = 128
SMALL = (1, 1, 1, 1, 1, 1, 1, 1, 3, 4)


def attend_kernel(nt, s, me_ref, *refs):
    t_hbm = refs[:nt]
    wkv_ref, bkv_ref, q_hbm, al_ref, tok_ref, wo_ref, vec_ref = refs[nt : nt + 7]
    tt_ref, c_ref, kv_ref, p_hbm, att_ref, n_ref, inv_ref = refs[nt + 7 : nt + 14]
    t_scr, q_scr, p_scr, res_scr, att_scr, bias_scr, in_sem, out_sem = refs[nt + 14 :]
    width = wo_ref.shape[0]
    length = q_scr.shape[1]
    heads = width // HD
    units, rows = 2 * tt_ref.shape[0], tt_ref.shape[2]
    loads = [pltpu.make_async_copy(t_hbm[k], t_scr.at[k], in_sem.at[k]) for k in range(nt)]
    loads.append(pltpu.make_async_copy(q_hbm.at[s], q_scr, in_sem.at[nt]))
    for c in loads:
        c.start()
    bias_scr[...] = (al_ref[...].astype(F32) - 1.0) * 1e30
    for c in loads[:nt]:
        c.wait()
    total = t_scr[0].astype(F32)
    for k in range(1, nt):
        total = total + t_scr[k].astype(F32)
    low = total.astype(BF16)
    t_low = low[0:KP]
    c_row = low[KP : KP + 8, 0:KP]
    c_ref[...] = c_row
    wide_c = c_row[0:1].astype(F32)
    for k in range(2):
        part = slice(k * width, (k + 1) * width)
        kv_ref[part, :] = (dot(wkv_ref[k], t_low, 1, 1) + bkv_ref[part, :] * wide_c).astype(BF16)
    tt = jnp.transpose(t_low)
    me = me_ref[0]
    for u in range(units):
        r = u ^ me
        tt_ref[r >> 1, r & 1] = tt[u * rows : (u + 1) * rows]
    loads[nt].wait()

    def store(g):
        part = pl.ds(g * GROUP, GROUP)
        return pltpu.make_async_copy(p_scr.at[part], p_hbm.at[part], out_sem.at[g])

    tiles = [(h, j) for h in range(GROUP) for j in range(length // LANES)]

    def heads_of(g, carry):
        keys = {}

        def cut(h, shift=0):
            return pl.ds(pl.multiple_of(shift + (g * GROUP + h) * HD, HD), HD)

        def score(h, j):
            if j == 0:
                keys[h] = jnp.transpose(kv_ref[cut(h), :])
            return dot(keys[h], q_scr[cut(h), j * LANES : (j + 1) * LANES])

        scores = score(*tiles[0])
        for i, (h, j) in enumerate(tiles):
            after = score(*tiles[i + 1]) if i + 1 < len(tiles) else None
            where = slice(j * LANES, (j + 1) * LANES)
            scores = scores + bias_scr[:, where]
            expo = jnp.exp(scores - jnp.max(scores, 0, keepdims=True))
            p_scr[g * GROUP + h, :, where] = (expo * (1.0 / jnp.sum(expo, 0, keepdims=True))).astype(BF16)
            if j == length // LANES - 1:
                att_scr[cut(h), :] = dot(kv_ref[cut(h, width), :], p_scr[g * GROUP + h]).astype(BF16)
            scores = after
        store(g).start()
        return carry

    lax.fori_loop(0, heads // GROUP, heads_of, 0)
    att = att_scr[...]
    res_scr[...] = dot(att, wo_ref[...], 0, 0)
    block_rows = min(2 * LN_ROWS, length)
    for u in range(units):
        r = u ^ me
        att_ref[r >> 1, r & 1] = att_scr[u * rows : (u + 1) * rows, :]

    def tile(i, carry):
        part = pl.ds(pl.multiple_of(i * block_rows, block_rows), block_rows)
        normed, inverse = norm_stats(res_scr[part, :] + tok_ref[0, part, :].astype(F32) + vec_ref[0:1, :])
        n_ref[part, :] = normed
        inv_ref[part, :] = inverse
        return carry

    lax.fori_loop(0, length // block_rows, tile, 0)
    for g in range(heads // GROUP):
        store(g).wait()


def attend(me, s, units, others, wkv_t, bkv_col, q_t, allow, tokens, w_out, vecs):
    seqs, length, width = tokens.shape
    rows = width // units
    heads = width // HD
    nt = len(others)
    return call(
        functools.partial(attend_kernel, nt, s),
        "attend",
        [(t, "n", None) for t in others]
        + [
            (wkv_t, "v", None),
            (bkv_col, "v", None),
            (q_t, "h", None),
            (allow, "h", whole((KP, length))),
            (tokens, "h", block((1, length, width), lambda i, me: (s, 0, 0))),
            (w_out, "v", None),
            (vecs, "h", whole(vecs.shape)),
        ],
        [
            (V(units // 2, 2, rows, KP), None),
            (V(8, KP), None),
            (V(2 * width, KP), None),
            (H(heads, KP, length), ANY),
            (V(units // 2, 2, rows, length), None),
            (V(length, width, dtype=F32), None),
            (V(length, 1, dtype=F32), None),
        ],
        prefetch=(me,),
        scratch=[
            pltpu.VMEM((nt, TE, width), BF16),
            pltpu.VMEM((width, length), BF16),
            pltpu.VMEM((heads, KP, length), BF16),
            pltpu.VMEM((length, width), F32),
            pltpu.VMEM((width, length), BF16),
            pltpu.VMEM((KP, length), F32),
            pltpu.SemaphoreType.DMA((nt + 1,)),
            pltpu.SemaphoreType.DMA((heads,)),
        ],
        limit=12,
        flops=2 * KP * width * 2 * width + 8 * KP * length * width + 2 * length * width * width,
        nbytes=10 * MIB,
    )


def norm_back(upstream, normed, inverse, gain):
    scaled = upstream * gain
    return inverse * (
        scaled
        - jnp.mean(scaled, -1, keepdims=True)
        - normed * jnp.mean(scaled * normed, -1, keepdims=True)
    )


FR = 16


def feed_kernel(
    steps, me_ref, n_ref, inv_ref, vec_ref, win_ref, bin_ref, wdn_ref, cot_ref,
    mt_ref, at_ref, gb_ref, dh_ref, out_ref, gf_ref, gfl_ref, stat_ref,
    low_scr, acc_scr, slope_scr, h0_scr, h1_scr,
):
    step = pl.program_id(0)
    g1_ref, be1_ref, bdn_ref, g2_ref, be2_ref = [vec_ref.at[k : k + 1, :] for k in range(1, 6)]
    me = me_ref[0]
    units, rows = 2 * mt_ref.shape[0], mt_ref.shape[2]
    arows = at_ref.shape[2]
    length, width = n_ref.shape
    half = h0_scr.shape[0]
    per = half // arows

    @pl.when(step == 0)
    def _():
        for r in range(0, length, ROWS):
            part = slice(r, r + ROWS)
            mid = n_ref[part, :] * g1_ref[...] + be1_ref[...]
            low_scr[part, :] = mid.astype(BF16)
            acc_scr[part, :] = mid + bdn_ref[...]
        mt = jnp.transpose(low_scr[...])
        for u in range(units):
            r = u ^ me
            mt_ref[r >> 1, r & 1] = mt[u * rows : (u + 1) * rows]

    def unit(base, i):
        r = (base + i) ^ me
        return r >> 1, r & 1

    @pl.when(step < steps)
    def _():
        base = step * 2 * per

        def gelu(k, h_scr):
            for f in range(0, half, FR):
                at = k * half + f
                hidden = h_scr[f : f + FR, :] + bin_ref[pl.ds(pl.multiple_of(step * 2 * half + at, FR), FR), :]
                phi = 0.5 + 0.5 * lax.erf(hidden * HALF_ROOT)
                bell = jnp.exp(-0.5 * hidden * hidden)
                hi, lo = unit(base, at // arows)
                at_ref[hi, lo, at % arows : at % arows + FR, :] = (hidden * phi).astype(BF16)
                slope_scr[step, at : at + FR, :] = (phi + (hidden * INV_ROOT_TAU) * bell).astype(BF16)

        def cut(k):
            return pl.ds(pl.multiple_of(step * 2 * half + k * half, half), half)

        def second(k):
            activ = jnp.concatenate([at_ref[unit(base, k * per + i)] for i in range(per)], 0)
            acc_scr[...] += dot(activ, wdn_ref[cut(k), :], 0, 0)

        low = low_scr[...]
        h0_scr[...] = dot(win_ref[:, cut(0)], low, 0, 1)
        h1_scr[...] = dot(win_ref[:, cut(1)], low, 0, 1)
        gelu(0, h0_scr)
        second(0)
        gelu(1, h1_scr)
        second(1)

    @pl.when(step == steps - 1)
    def _():
        def tile(i, sums):
            part = pl.ds(pl.multiple_of(i * LN_ROWS, LN_ROWS), LN_ROWS)
            normed, inverse = norm_stats(acc_scr[part, :])
            out_ref[part, :] = (normed * g2_ref[...] + be2_ref[...]).astype(BF16)
            cot = cot_ref[0, part, :].astype(F32)
            second = norm_back(cot, normed, inverse, g2_ref[...])
            low = second.astype(BF16)
            gb_ref[part, :] = low
            acc_scr[part, :] = second
            terms = (cot * normed, cot, low.astype(F32))
            return tuple(a + jnp.sum(t, 0, keepdims=True) for a, t in zip(sums, terms))

        sums = lax.fori_loop(0, length // LN_ROWS, tile, (jnp.zeros((1, width), F32),) * 3)
        for k in range(3):
            stat_ref[k : k + 1, :] = sums[k]

    @pl.when(step >= steps)
    def _():
        back = step - steps
        gb = gb_ref[...]

        def slope(k, h_scr):
            for f in range(0, half, FR):
                at = k * half + f
                dh = (h_scr[f : f + FR, :] * slope_scr[back, at : at + FR, :].astype(F32)).astype(BF16)
                row = pl.ds(pl.multiple_of(back * 2 * half + at, FR), FR)
                dh_ref[row, :] = dh

        def cut(k):
            return pl.ds(pl.multiple_of(back * 2 * half + k * half, half), half)

        def down(k):
            acc_scr[...] += dot(dh_ref[cut(k), :], win_ref[:, cut(k)], 0, 1)

        h0_scr[...] = dot(wdn_ref[cut(0), :], gb, 1, 1)
        h1_scr[...] = dot(wdn_ref[cut(1), :], gb, 1, 1)
        slope(0, h0_scr)
        down(0)
        slope(1, h1_scr)
        down(1)

    @pl.when(step == 2 * steps - 1)
    def _():
        def tile(i, sums):
            part = pl.ds(pl.multiple_of(i * LN_ROWS, LN_ROWS), LN_ROWS)
            up = acc_scr[part, :]
            normed = n_ref[part, :]
            first = norm_back(up, normed, inv_ref[part, :], g1_ref[...])
            low = first.astype(BF16)
            gf_ref[part, :] = first
            gfl_ref[part, :] = low
            terms = (up * normed, up, low.astype(F32))
            return tuple(a + jnp.sum(t, 0, keepdims=True) for a, t in zip(sums, terms))

        sums = lax.fori_loop(0, length // LN_ROWS, tile, (jnp.zeros((1, width), F32),) * 3)
        for k in range(3):
            stat_ref[3 + k : 4 + k, :] = sums[k]
        stat_ref[6:8, :] = jnp.zeros((2, width), F32)


def feed(me, s, units, normed, inverse, vecs, w_in, bin_col, w_down, cot):
    length, width = normed.shape
    ff = w_in.shape[1]
    rows = width // units
    arows = ff // units
    chunk = 768
    steps = ff // chunk
    return call(
        functools.partial(feed_kernel, steps),
        "feed",
        [
            (normed, "v", None),
            (inverse, "v", None),
            (vecs, "h", whole(vecs.shape)),
            (w_in, "v", None),
            (bin_col, "v", None),
            (w_down, "v", None),
            (cot, "h", block((1, length, width), lambda i, me: (s, 0, 0))),
        ],
        [
            (V(units // 2, 2, rows, length), None),
            (V(units // 2, 2, arows, length), None),
            (V(length, width), None),
            (V(ff, length), None),
            (H(length, width), whole((length, width))),
            (H(length, width, dtype=F32), whole((length, width))),
            (H(length, width), whole((length, width))),
            (V(8, width, dtype=F32), None),
        ],
        grid=(2 * steps,),
        prefetch=(me,),
        scratch=[
            pltpu.VMEM((length, width), BF16),
            pltpu.VMEM((length, width), F32),
            pltpu.VMEM((steps, chunk, length), BF16),
            pltpu.VMEM((chunk // 2, length), F32),
            pltpu.VMEM((chunk // 2, length), F32),
        ],
        limit=18,
        flops=8 * length * width * ff,
        nbytes=24 * MIB,
    )


def attend_back_kernel(seqs, *refs):
    gfl_hbm, kv_hbm, p_hbm, c_refs = [refs[k * seqs : (k + 1) * seqs] for k in range(4)]
    wo_ref, q_hbm, wkv_ref, bkv_ref, dq_ref, gs_ref, gt_ref, col_ref = refs[4 * seqs : 4 * seqs + 8]
    gfl_scr, kv_scr, p_scr, q_scr, c_scr, da_scr, ds0_scr, ds1_scr, sem, p_sem = refs[4 * seqs + 8 :]
    s = pl.program_id(0)
    width = wo_ref.shape[0]
    length = gfl_scr.shape[1]
    heads = width // HD
    groups = heads // GROUP

    def inputs(k):
        pairs = ((gfl_hbm[k], gfl_scr.at[k]), (q_hbm.at[k], q_scr.at[k]), (kv_hbm[k], kv_scr.at[k]))
        return [pltpu.make_async_copy(x, y, sem.at[k, i]) for i, (x, y) in enumerate(pairs)]

    def load(k, g):
        part = pl.ds(g * GROUP, GROUP)
        return pltpu.make_async_copy(p_hbm[k].at[part], p_scr.at[k, part], p_sem.at[k, g])

    @pl.when(s == 0)
    def _():
        for k in range(seqs):
            for c in inputs(k):
                c.start()
            for g in range(groups):
                load(k, g).start()

    for k in range(seqs):

        @pl.when(s == k)
        def _(k=k):
            c_scr[...] = c_refs[k][...]
            for c in inputs(k):
                c.wait()
            for g in range(groups):
                load(k, g).wait()

    da_scr[...] = dot(wo_ref[...], gfl_scr[s], 1, 1).astype(BF16)
    c_wide = c_scr[0:1, :].astype(F32)
    tiles = [(h, j) for h in range(GROUP) for j in range(length // LANES)]

    def heads_of(g, carry):
        vals = {}

        def cut(h, shift=0):
            return pl.ds(pl.multiple_of(shift + (g * GROUP + h) * HD, HD), HD)

        def first(h, j):
            if j == 0:
                vals[h] = jnp.transpose(kv_scr[s, cut(h, width), :])
            return dot(vals[h], da_scr[cut(h), j * LANES : (j + 1) * LANES])

        grad = first(*tiles[0])
        for i, (h, j) in enumerate(tiles):
            after = first(*tiles[i + 1]) if i + 1 < len(tiles) else None
            where = slice(j * LANES, (j + 1) * LANES)
            ds_scr = (ds0_scr, ds1_scr)[h % 2]
            wide = p_scr[s, g * GROUP + h, :, where].astype(F32)
            prod = wide * grad
            ds_scr[:, where] = (prod - wide * jnp.sum(prod, 0, keepdims=True)).astype(BF16)
            if j == length // LANES - 1:
                gv = dot(da_scr[cut(h), :], p_scr[s, g * GROUP + h], 1, 1).astype(BF16)
                gs_ref[s, cut(h, width), :] = gv
                col_ref[s, cut(h, 2 * width), :] = jnp.sum(gv.astype(F32) * c_wide, 1, keepdims=True)
                dq = (dot(kv_scr[s, cut(h), :], ds_scr[...]) * SCALE).astype(BF16)
                dq_ref[s, cut(h), :] = dq
                col_ref[s, cut(h), :] = jnp.sum(dq.astype(F32), 1, keepdims=True)
                gk = dot(q_scr[s, cut(h), :], ds_scr[...], 1, 1).astype(BF16)
                gs_ref[s, cut(h), :] = gk
                col_ref[s, cut(h, width), :] = jnp.sum(gk.astype(F32) * c_wide, 1, keepdims=True)
            grad = after
        return carry

    lax.fori_loop(0, groups, heads_of, 0)
    gs = gs_ref[s]
    gt = dot(gs[0:width], wkv_ref[0], 0, 0) + dot(gs[width:], wkv_ref[1], 0, 0)
    gt_ref[0, 0:KP, :] = gt.astype(BF16)
    pad = TE - KP
    b_kv = bkv_ref[:, width:]
    b_hi = b_kv.astype(BF16)
    b_lo = (b_kv - b_hi.astype(F32)).astype(BF16)
    drow = dot(jnp.broadcast_to(b_hi, (pad, 2 * width)), gs) + dot(jnp.broadcast_to(b_lo, (pad, 2 * width)), gs)
    gt_ref[0, KP:TE, :] = jnp.concatenate([drow.astype(BF16), jnp.zeros((pad, width - KP), BF16)], 1)


def attend_back(gfl, w_out, kv_t, probs, q_t, c_row, wkv_t, bkv_row):
    seqs = len(gfl)
    length, width = gfl[0].shape
    heads = width // HD
    return call(
        functools.partial(attend_back_kernel, seqs),
        "attend_back",
        [(x, "n", None) for x in (*gfl, *kv_t, *probs)]
        + [(c, "v", None) for c in c_row]
        + [
            (w_out, "v", None),
            (q_t, "h", None),
            (wkv_t, "v", None),
            (bkv_row, "h", whole((1, 3 * width))),
        ],
        [
            (V(seqs, width, length), None),
            (V(seqs, 2 * width, KP), None),
            (H(seqs, TE, width), block((1, TE, width), lambda s: (s, 0, 0))),
            (V(seqs, 3 * width, 1, dtype=F32), None),
        ],
        grid=(seqs,),
        scratch=[
            pltpu.VMEM((seqs, length, width), BF16),
            pltpu.VMEM((seqs, 2 * width, KP), BF16),
            pltpu.VMEM((seqs, heads, KP, length), BF16),
            pltpu.VMEM((seqs, width, length), BF16),
            pltpu.VMEM((8, KP), BF16),
            pltpu.VMEM((width, length), BF16),
            pltpu.VMEM((KP, length), BF16),
            pltpu.VMEM((KP, length), BF16),
            pltpu.SemaphoreType.DMA((seqs, 3)),
            pltpu.SemaphoreType.DMA((seqs, heads // GROUP)),
        ],
        limit=22,
        flops=(2 * KP * width * 2 * width + 16 * KP * length * width + 2 * length * width * width) // 1024,
        nbytes=1024,
    )


def token_kernel(gf_refs, dq_ref, wq_ref, o_ref):
    for k, g in enumerate(gf_refs):
        o_ref[k] = g[...] + dot(dq_ref[k], wq_ref[...], 0, 1)


def token_grad(gf, dq_t, w_qkv):
    seqs = len(gf)
    length, width = gf[0].shape
    shape = (seqs, length, width)
    return call(
        lambda *refs: token_kernel(refs[:seqs], *refs[seqs:]),
        "token_grad",
        [(g, "h", whole((length, width))) for g in gf]
        + [(dq_t, "v", None), (w_qkv, "h", block((width, width), lambda i: (0, 0)))],
        (H(*shape, dtype=F32), whole(shape)),
        limit=16,
        flops=seqs * length * width * width // 1024,
        nbytes=1024,
    )


def last_kernel(nt, *refs):
    t_refs = refs[:nt]
    part_ref, wt_ref, al_ref, tok_ref, o_ref, gp_ref, d_scr = refs[nt:]
    s = pl.program_id(0)
    total = t_refs[0][0].astype(F32)
    for r in t_refs[1:]:
        total = total + r[0].astype(F32)
    low = total[0:KP].astype(BF16)
    d_col = columns(total[KP : KP + 1, 0:KP])
    o_ref[0] = part_ref[0] + dot(wt_ref[0], low, 0, 0)
    term = (dot(low, tok_ref[0], 1, 1) + d_col) * al_ref[0].astype(F32)

    @pl.when(s == 0)
    def _():
        d_scr[...] = term

    @pl.when(s > 0)
    def _():
        d_scr[...] = d_scr[...] + term

    @pl.when(s == pl.num_programs(0) - 1)
    def _():
        gp_ref[...] = d_scr[...].astype(BF16)


def last(tparts, parts, weights, allows, tokens):
    seqs, length, width = tokens.shape
    each = lambda *shape: block((1, *shape), lambda s: (s,) + (0,) * len(shape))
    return call(
        functools.partial(last_kernel, len(tparts)),
        "last",
        [(t, "n", each(TE, width)) for t in tparts]
        + [(parts, "h", each(length, width)), (weights, "h", each(KP, length)), (allows, "h", each(KP, length)), (tokens, "h", each(length, width))],
        [(H(seqs, length, width, dtype=F32), each(length, width)), (H(KP, length), whole((KP, length)))],
        grid=(seqs,),
        scratch=[pltpu.VMEM((KP, length), F32)],
        limit=18,
        flops=4 * seqs * length * width * KP,
        nbytes=8 * MIB,
    )


def split_store(low, send_ref, keep_ref, send_bit, where):
    n = low.shape[0]
    if send_bit == 0:
        for i in range(n):
            (send_ref if i & 1 else keep_ref)[i // 2, :, where] = low[i]
    else:
        half = n // 2
        keep_ref[:, :, where] = low[:half]
        send_ref[:, :, where] = low[half:]


def total(terms):
    out = terms[0]
    for t in terms[1:]:
        out = out + t
    return out


def down_kernel(seqs, core, chunk, send_bit, *refs):
    at_refs = refs[:seqs]
    gb_refs = refs[seqs : 2 * seqs]
    rest = refs[2 * seqs :]
    n, _, arows, length = at_refs[0].shape
    cols = pl.ds(pl.multiple_of(pl.program_id(0) * chunk, chunk), chunk)
    res = total([dot(a[:, core].reshape(n * arows, length), g[:, cols]) for a, g in zip(at_refs, gb_refs)])
    res = res.reshape(n, arows, chunk)
    if send_bit is None:
        rest[0][...] = res.astype(BF16)
    else:
        recv_ref, send_ref, keep_ref = rest
        low = (res + recv_ref[...].astype(F32)).astype(BF16)
        split_store(low, send_ref, keep_ref, send_bit, slice(None))


def down_grad(at, gb, core, recv=None, send_bit=None):
    seqs = len(at)
    n, _, arows, length = at[0].shape
    width = gb[0].shape[1]
    chunk = 256
    args = [(a, "v", None) for a in at] + [(g, "v", None) for g in gb]
    spec = block((n, arows, chunk), lambda i: (0, 0, i))
    if recv is None:
        outs = (H(n, arows, width), spec)
    else:
        args.append((recv, "n", spec))
        outs = [(H(n // 2, arows, width), block((n // 2, arows, chunk), lambda i: (0, 0, i)))] * 2
    return call(
        functools.partial(down_kernel, seqs, core, chunk, send_bit),
        "down_grad",
        args,
        outs,
        grid=(width // chunk,),
        limit=12,
        flops=2 * seqs * n * arows * length * width,
        nbytes=3 * MIB,
    )


def in_kernel(seqs, core, chunk, send_bit, *refs):
    mt_refs = refs[:seqs]
    dh_refs = refs[seqs : 2 * seqs]
    rest = refs[2 * seqs :]
    n, _, rows, length = mt_refs[0].shape
    part = pl.ds(pl.multiple_of(pl.program_id(0) * chunk, chunk), chunk)
    lefts = [a[:, core].reshape(n * rows, length) for a in mt_refs]
    if send_bit is None:
        lefts = [jnp.concatenate([a, jnp.ones((16, length), BF16)], 0) for a in lefts]
    res = total([dot(a, g[part, :], 1, 1) for a, g in zip(lefts, dh_refs)])
    if send_bit is None:
        out_ref, bias_ref = rest
        out_ref[...] = res[0 : n * rows].reshape(n, rows, chunk).astype(BF16)
        bias_ref[...] = res[n * rows : n * rows + 8]
    else:
        res = res.reshape(n, rows, chunk)
        recv_ref, send_ref, keep_ref = rest
        low = (res + recv_ref[...].astype(F32)).astype(BF16)
        split_store(low, send_ref, keep_ref, send_bit, slice(None))


def in_grad(mt, dh, core, recv=None, send_bit=None):
    seqs = len(mt)
    n, _, rows, length = mt[0].shape
    ff = dh[0].shape[0]
    chunk = 1536
    args = [(a, "v", None) for a in mt] + [(g, "v", None) for g in dh]
    spec = block((n, rows, chunk), lambda i: (0, 0, i))
    if recv is None:
        outs = [(H(n, rows, ff), spec), (H(8, ff, dtype=F32), block((8, chunk), lambda i: (0, i)))]
    else:
        args.append((recv, "n", spec))
        outs = [(H(n // 2, rows, ff), block((n // 2, rows, chunk), lambda i: (0, 0, i)))] * 2
    return call(
        functools.partial(in_kernel, seqs, core, chunk, send_bit),
        "in_grad",
        args,
        outs,
        grid=(ff // chunk,),
        limit=12,
        flops=2 * seqs * n * rows * length * ff,
        nbytes=3 * MIB,
    )


def pack_stats(stat_refs, bias_refs, col_refs, scr, bias_scr, group):
    rows = scr.shape[0]
    scr[...] = jnp.zeros_like(scr)
    stat = total([r[...] for r in stat_refs])
    scr[:, 0:8] = jnp.transpose(stat)
    bias_scr[...] = jnp.transpose(total([r[...] for r in bias_refs]))[:, 0:1]
    lane = 8
    for refs in (col_refs, [bias_scr]):
        per = refs[0].shape[0] // rows
        for b in range(rows // group):
            for c in range(per):
                src = slice((b * per + c) * group, (b * per + c + 1) * group)
                scr[b * group : (b + 1) * group, lane + c : lane + c + 1] = total([r[src, :] for r in refs])
        lane += per


def rest_kernel(seqs, group, me_ref, *refs):
    at_refs, gf_refs, tk_refs, tt_refs = [refs[k * seqs : (k + 1) * seqs] for k in range(4)]
    dq_refs, gs_refs = [[refs[4 * seqs + k].at[i] for i in range(seqs)] for k in range(2)]
    rest = refs[4 * seqs + 2 :]
    keep_ref, send_ref, st_scr, bias_scr = rest[-4:]
    n, _, rows, _ = at_refs[0].shape
    width = gf_refs[0].shape[1]

    def put(res, where):
        res = res.reshape(n, 2, rows, res.shape[-1]).astype(BF16)
        keep_ref[:, :, where] = res[:, 0]
        send_ref[:, :, where] = res[:, 1]

    def flat(ref):
        return ref[...].reshape(2 * n * rows, ref.shape[-1])

    if group:
        pack_stats(rest[:seqs], [rest[seqs]], [rest[seqs + 1].at[k] for k in range(seqs)], st_scr, bias_scr, group)
        for u in range(2 * n):
            low = st_scr[pl.ds(pl.multiple_of((u ^ me_ref[0]) * rows, rows), rows), :].astype(BF16)
            (keep_ref, send_ref)[u % 2][u // 2, :, 4 * width : 4 * width + 128] = low
    else:
        for ref in (keep_ref, send_ref):
            ref[:, :, 4 * width : 4 * width + 128] = jnp.zeros((n, rows, 128), BF16)
    put(total([dot(flat(a), g[...]) for a, g in zip(at_refs, gf_refs)]), slice(0, width))
    put(total([dot(flat(a), g[...], 1, 1) for a, g in zip(tk_refs, dq_refs)]), slice(width, 2 * width))
    for k in range(2):
        part = slice(k * width, (k + 1) * width)
        put(total([dot(flat(a), g[part, :], 1, 1) for a, g in zip(tt_refs, gs_refs)]), slice((2 + k) * width, (3 + k) * width))


def rest_grad(me, att, gfl, tok_t, dq_t, t_t, gs_t, group, stats):
    seqs = len(att)
    n, _, rows, length = att[0].shape
    width = gfl[0].shape[1]
    cols = 4 * width + 128
    args = [(a, "v", None) for a in att] + [(g, "h", whole((length, width))) for g in gfl]
    args += [(t, "h", block((pl.Squeezed(), n, 2, rows, length), lambda i, me, k=k: (k, 0, 0, 0, 0))) for k, t in enumerate([tok_t] * seqs)]
    args += [(a, "v", None) for a in (*t_t, dq_t, gs_t)]
    args += [(a, "v", None) for a in stats[0]] + [(stats[1], "h", whole(stats[1].shape)), (stats[2], "v", None)]
    return call(
        functools.partial(rest_kernel, seqs, group),
        "rest_grad",
        args,
        [(H(n, rows, cols), whole((n, rows, cols)))] * 2,
        prefetch=(me,),
        scratch=[pltpu.VMEM((2 * n * rows, 128), F32), pltpu.VMEM((stats[1].shape[1], 1), F32)],
        limit=16,
        flops=seqs * 2 * n * rows * (4 * length * width + 4 * KP * width) // 1024,
        nbytes=1024,
    )


def halve_kernel(z_ref, ka_ref, ra_ref, kb_ref, rb_ref, send_ref, keep_ref):
    z = z_ref[0]
    cut = ka_ref.shape[-1]
    for k in range(2):
        for keep, recv, cols in ((ka_ref, ra_ref, slice(0, cut)), (kb_ref, rb_ref, slice(cut, None))):
            for where, out in ((1 - z, send_ref), (z, keep_ref)):
                out[k, :, cols] = (keep[k, where].astype(F32) + recv[k, where].astype(F32)).astype(BF16)


def halve_rest(z, ka, ra, kb, rb):
    group = ka.shape[0] // 4
    arrays = [x.reshape(2, 2, group, x.shape[-1]) for x in (ka, ra, kb, rb)]
    cols = ka.shape[-1] + kb.shape[-1]
    shape = (2, group, cols)
    return call(
        halve_kernel,
        "halve_rest",
        [(x, "n", whole(x.shape)) for x in arrays],
        [(H(*shape), whole(shape)), (H(*shape), whole(shape))],
        prefetch=(z,),
        limit=6,
        nbytes=2 * MIB,
    )


def finish_kernel(z_ref, keep_ref, recv_ref, qkv_ref, out_ref, *small_refs):
    width = out_ref.shape[1]
    res = keep_ref[...].astype(F32) + recv_ref[...].astype(F32)
    out_ref[...] = res[:, 0:width]
    qkv_ref[...] = res[:, width : 4 * width]
    small = jnp.transpose(res[:, 4 * width :])
    lane = 0
    for ref, per in zip(small_refs, SMALL):
        parts = [small[lane + k : lane + k + 1, :] for k in range(per)]
        ref[...] = (jnp.concatenate(parts, 1) if per > 1 else parts[0]).reshape(ref.shape)
        lane += per


def finish_rest(z, keep, recv):
    group, cols = keep.shape
    width = (cols - 128) // 4
    return call(
        finish_kernel,
        "finish_rest",
        [(keep, "n", whole((group, cols))), (recv, "n", whole((group, cols)))],
        [
            (H(group, 3 * width, dtype=F32), whole((group, 3 * width))),
            (H(group, width, dtype=F32), whole((group, width))),
            *[(H(per * group, dtype=F32), whole((per * group,))) for per in SMALL],
        ],
        prefetch=(z,),
        limit=5,
        nbytes=MIB,
    )


def add(a, b):
    return (a.astype(F32) + b.astype(F32)).astype(BF16)


def body(n_dp, n_seq, tokens, segment_ids, mask, w_qkv, b_qkv, w_out, b_out, ln1_gain, ln1_bias, w_in, b_in, w_down, b_down, ln2_gain, ln2_bias, proj_e, cotangent):
    seqs, length, width = tokens.shape
    ff = w_in.shape[1]
    n_all = n_dp * n_seq
    fast = n_dp == 8 and n_seq == 4 and length >= 512
    units = 8
    dp = lax.axis_index("dp").astype(jnp.int32)
    sq = lax.axis_index("seq").astype(jnp.int32)
    me = (dp if fast else jnp.zeros((), jnp.int32)).reshape(1)
    row = lambda v: v.reshape(1, -1)

    def swap(x, bit):
        pairs = [(i, i ^ bit) for i in range(n_all)]
        return lax.ppermute(x, ("dp", "seq"), pairs)

    near = [(i, i ^ 1) for i in range(n_seq)]
    mid = [(1, 2), (2, 1)]

    def hop_one(own):
        return lax.ppermute(own, "seq", near), lax.ppermute(own, "seq", mid)

    def hop_two(first):
        return lax.ppermute(first[1], "seq", near), lax.ppermute(first[0], "seq", mid)

    def tie(x, *deps):
        return lax.optimization_barrier((x, *deps))[0]

    vecs = jnp.stack([b_out, ln1_gain, ln1_bias, b_down, ln2_gain, ln2_bias])
    first = prep(0, tokens, segment_ids, mask, proj_e)
    prepped = [first] + [prep(s, tie(tokens, first[0]), segment_ids, mask, proj_e) for s in range(1, seqs)]
    owns = [p[0] for p in prepped]
    wkv_t, bkv_col, bin_col = flip(tie(w_qkv, vecs, *owns), row(b_qkv), row(b_in))
    if fast:
        one = tuple(tie(x, wkv_t) for x in hop_one(owns[0]))
        q_t, tok_t, w_in, w_down, w_out = query(me, units, tie(tokens, wkv_t, *one), w_qkv, row(b_qkv), w_in, w_down, w_out)
        tparts = [[owns[0], *one, *(tie(x, q_t) for x in hop_two(one))]]
    else:
        q_t, tok_t, w_in, w_down, w_out = query(me, units, tie(tokens, wkv_t), w_qkv, row(b_qkv), w_in, w_down, w_out)
        tparts = [[lax.psum(o, "seq")] for o in owns]

    tt, crow, kv, probs, att, normed, inverse = [], [], [], [], [], [], []
    mt, at, gb, dh, outs, gf, gfl, stat = [], [], [], [], [], [], [], []
    for s in range(seqs):
        if s:
            tparts[s][0] = tie(tparts[s][0], gfl[s - 1])
        if fast and s + 1 < seqs:
            own = tie(owns[s + 1], q_t)
            one = hop_one(own)
        res = attend(me, s, units, tparts[s], wkv_t, bkv_col, q_t, prepped[s][1], tokens, w_out, vecs)
        for store, value in zip((tt, crow, kv, probs, att, normed, inverse), res):
            store.append(value)
        if fast and s + 1 < seqs:
            normed[s] = tie(normed[s], *one)
            tparts.append([own, *one, *hop_two(one)])
        res = feed(me, s, units, normed[s], inverse[s], vecs, w_in, bin_col, w_down, cotangent)
        for store, value in zip((mt, at, gb, dh, outs, gf, gfl, stat), res):
            store.append(value)

    X_BIT, Y_BIT, CORE = 2 * n_seq, 4 * n_seq, n_seq
    z0, z1 = sq & 1, sq >> 1

    def halve(recv, keep):
        return add(keep[1], recv[1]), add(keep[0], recv[0])

    def halve_z0(recv, keep):
        group = keep.shape[0] // 4
        shape = (2, 2, group, keep.shape[-1])
        pick = lambda a, z: lax.dynamic_index_in_dim(a, z, 1, keepdims=False)
        keep, recv = keep.reshape(shape), recv.reshape(shape)
        return add(pick(keep, 1 - z0), pick(recv, 1 - z0)), add(pick(keep, z0), pick(recv, z0))

    def halve_z1(recv, keep):
        pick = lambda a, z: lax.dynamic_index_in_dim(a, z, 0, keepdims=False)
        return add(pick(keep, 1 - z1), pick(recv, 1 - z1)), add(pick(keep, z1), pick(recv, z1))

    back_in = list(gfl)
    if fast:
        send1 = down_grad(at, gb, 1)
        recv1 = swap(send1, CORE)
        send2, gbin = in_grad([tie(mt[0], send1), *mt[1:]], dh, 1)
        recv2 = swap(send2, CORE)
        sx1, kx1 = down_grad([tie(at[0], send2), *at[1:]], gb, 0, recv1, 0)
        rx1 = swap(sx1, X_BIT)
        sx2, kx2 = in_grad([tie(mt[0], sx1), *mt[1:]], dh, 0, recv2, 1)
        rx2 = swap(sx2, Y_BIT)
        back_in[0] = tie(gfl[0], sx2)

    dq_t, gs_t, gsum, col = attend_back(back_in, w_out, kv, probs, q_t, crow, wkv_t, row(b_qkv))
    if not fast:
        half2, gbin = in_grad(mt, dh, 1)
    stats = (stat, gbin, col)

    if fast:
        group = width // n_all
        gone = hop_one(gsum)
        parts = token_grad(gf, dq_t, w_qkv)
        sy1, ky1 = halve(tie(rx1, parts), kx1)
        ry1 = swap(sy1, Y_BIT)
        sy2, ky2 = halve(tie(rx2, parts), kx2)
        ry2 = swap(sy2, X_BIT)
        keep3, send3 = rest_grad(me, [tie(att[0], sy1, sy2, parts, gsum), *att[1:]], gfl, tok_t, dq_t, tt, gs_t, group, stats)
        recv3 = swap(tie(send3, ry1, ry2, *gone), CORE)
        half, cut = units // 4, 2 * width
        pair = lambda a: a.reshape(half, 2, width // units, a.shape[-1])
        k3, r3 = pair(keep3), pair(recv3)
        sx3, kx3 = add(k3[:, 1, :, :cut], r3[:, 1, :, :cut]), add(k3[:, 0, :, :cut], r3[:, 0, :, :cut])
        sy3, ky3 = add(k3[1, :, :, cut:], r3[1, :, :, cut:]), add(k3[0, :, :, cut:], r3[0, :, :, cut:])
        rx3 = swap(sx3, X_BIT)
        ry3 = swap(sy3, Y_BIT)
        gtwo = hop_two(gone)
        layer_out = jnp.stack([tie(outs[0], sx3), *outs[1:]])
        sxy, kxy = halve(tie(rx3, layer_out, *gtwo), kx3)
        rxy = swap(sxy, Y_BIT)
        syx, kyx = halve(tie(ry3, *gtwo), ky3)
        ryx = swap(syx, X_BIT)
        sz1, kz1 = halve_z0(tie(ry1, sxy, syx), ky1)
        rz1 = swap(sz1, 1)
        sz2, kz2 = halve_z0(tie(ry2, sxy, syx), ky2)
        rz2 = swap(sz2, 1)
        gparts = [tie(gsum, sz1, sz2), *gone, *gtwo]
    else:
        parts = token_grad(gf, dq_t, w_qkv)
        gparts = [lax.psum(gsum, "seq")]

    grad_tokens, gproj = last(gparts, parts, jnp.stack([p[2] for p in prepped]), jnp.stack([p[1] for p in prepped]), tokens)
    if not fast:
        layer_out = jnp.stack(outs)

    if not fast:
        g3 = jnp.stack(rest_grad(me, att, gfl, tok_t, dq_t, tt, gs_t, 0, stats), 1).reshape(width, -1)
        g2 = jnp.stack([in_grad(mt, dh, 0)[0], half2], 1).reshape(width, -1)
        g1 = jnp.stack([down_grad(at, gb, c) for c in (0, 1)], 1).reshape(ff, width)
        st = total(stat)
        st_in, st_qkv = gbin[0], jnp.sum(col, 0).reshape(-1)
        grads = (g3[:, width : 4 * width], st_qkv, g3[:, :width], st[5], st[3], st[4], g2, st_in, g1, st[2], st[0], st[1])
        grads = lax.psum_scatter(tuple(g.astype(F32) for g in grads), ("dp", "seq"), scatter_dimension=0, tiled=True)
        gproj = lax.psum(gproj, "dp").astype(F32)
        return (layer_out, grad_tokens, *grads, gproj)

    gproj = add(gproj, swap(gproj, CORE))
    sz3, kz3 = halve_rest(z0.reshape(1), kxy, rxy, kyx, ryx)
    rz3 = swap(sz3, 1)
    gproj = add(gproj, swap(gproj, X_BIT))
    gall = [gproj, swap(gproj, Y_BIT)]
    sw1, kw1 = halve_z1(rz1, kz1)
    rw1 = swap(sw1, 2)
    sw2, kw2 = halve_z1(rz2, kz2)
    rw2 = swap(sw2, 2)
    gproj = total([g.astype(F32) for g in gall])
    g1 = kw1.astype(F32) + rw1.astype(F32)
    g2 = kw2.astype(F32) + rw2.astype(F32)
    sw3, kw3 = halve_z1(rz3, kz3)
    rw3 = swap(sw3, 2)
    g_qkv, g_out, *small = finish_rest(z1.reshape(1), kw3, rw3)
    g_g2, g_b2, gb_down, g_g1, g_b1, gb_out, _, _, gb_qkv, gb_in = small
    return (
        layer_out, grad_tokens, g_qkv, gb_qkv, g_out, gb_out, g_g1, g_b1,
        g2, gb_in, g1, gb_down, g_g2, g_b2, gproj,
    )


def solution(mesh):
    both = ("dp", "seq")
    placed = (
        P("dp", "seq", None),
        P("dp", "seq"),
        P("dp", None, None),
        *([P()] * 12),
        P(None, "seq"),
        P("dp", "seq", None),
    )
    out = (
        P("dp", "seq", None),
        P("dp", "seq", None),
        P(both, None),
        P(both),
        P(both, None),
        P(both),
        P(both),
        P(both),
        P(both, None),
        P(both),
        P(both, None),
        P(both),
        P(both),
        P(both),
        P(None, "seq"),
    )
    run = functools.partial(body, mesh.shape["dp"], mesh.shape["seq"])
    return jax.shard_map(run, mesh=mesh, in_specs=placed, out_specs=out, check_vma=False)
```
